32 devices in a mesh: seg: 2 (over y), tile: 4 (over z), depth: 4 (over x, core).
Axes of the slice: x: 2, y: 2, z: 4, core: 2. Of those that a mesh axis runs over, the one named last changes fastest.
Arguments:
- initial_states: float32 [2, 2, 76, 16, 512], P('seg', None, 'depth', 'tile'), may hold values from 0 to 2
- velocity: float32 [2, 2, 76, 16, 512], P('seg', None, 'depth', 'tile'), may hold values from -0.35 to 0.35
- growth: float32 [2, 16, 512], P('seg', 'tile'), may hold values from 0.1 to 1
- land_sea: int32 [16, 512], P('tile'), may hold values 0 or 1
- depth_index: int32 [16, 512], P('tile'), may hold values from 1 to 76
- column_ops: bfloat16 [2, 76, 76], replicated, may hold values from 0 to 1
Outputs:
- mismatch: float32 [2, 2, 76, 16, 512], P('seg', None, 'depth', 'tile')
The draws below stay inside these ranges and needn't reach their ends.
All inputs are finite; a program needn't handle non-finite values. No bound on the sum of `land_sea` on one device may be relied on, other than what follows from the above.
Results may differ from the reference program's by a relative error of at most 0.00033.
Values may be sent and summed in bfloat16 or wider, within the bound.
No kernel may reach another device: no remote copies, remote signals or barrier semaphores. Data moves between devices by JAX's collectives and lax.ppermute only.
A program may use at most 64 MiB of HBM per device.

```python
import math
import jax
import jax.numpy as jnp
from jax import lax

TRACERS = 2
LEV = 76
LON = 512
STEPS = 4
SEGS = 2
NLAT = 16


def draw_column_ops(key, part):
    spread = jax.random.uniform(key, (TRACERS, LEV, LEV), jnp.float32)
    diagonal = jnp.where(lax.iota(jnp.int32, LEV)[:, None] == lax.iota(jnp.int32, LEV)[None, :], 1.0, 0.0).astype(jnp.float32)
    values = 0.05 * diagonal + 2.85 * spread * spread / LEV
    return values.astype(jnp.bfloat16)


def draw_velocity(key, part):
    magnitude_key = jax.random.fold_in(key, 11)
    sign_key = jax.random.fold_in(key, 23)
    magnitude = jax.random.uniform(magnitude_key, (SEGS, 2, LEV, NLAT, LON), jnp.float32, 0.2, 0.35)
    flips = jax.random.bernoulli(sign_key, 0.5, (SEGS, 2, LEV, NLAT, LON))
    values = jnp.where(flips, magnitude, -magnitude)
    return values.astype(jnp.float32)


def plant(entries, key, smallest, high):
    longest = entries.shape.index(max(entries.shape))
    spots = []
    for shift in (0, 1):
        where = [jax.random.randint(jax.random.fold_in(key, axis), (), 0, length) for axis, length in enumerate(entries.shape)]
        where[longest] = (where[longest] + shift) % entries.shape[longest]
        spots.append(tuple(where))
    return entries.at[spots[0]].set(smallest).at[spots[1]].set(high)


def shard_levels(stream_key, shape, split, least, high):
    loudness, own = 1.0, jax.random.fold_in(stream_key, 6)
    for dim, parts in split:
        steps = jnp.exp(jax.random.uniform(jax.random.fold_in(own, dim), (parts,), jnp.float32, least / len(split), high / len(split)))
        loudness = loudness * jnp.repeat(steps, shape[dim] // parts).reshape([-1 if axis == dim else 1 for axis in range(len(shape))])
    return loudness


def setup_inputs(seed: int = 0) -> dict:
    keys = jax.random.split(jax.random.key(seed), 7)
    initial_states = jnp.clip(2.0 * jax.random.uniform(keys[0], (SEGS, TRACERS, LEV, NLAT, LON), jnp.float32) ** shard_levels(keys[0], (SEGS, TRACERS, LEV, NLAT, LON), ((0, 2), (2, 4), (3, 4)), -0.2, 0.2), 0.0, 2.0)
    velocity = draw_velocity(jax.random.fold_in(keys[6], 71), 0)
    growth = jnp.clip(jnp.exp(math.log(1.0) - 2.3025851 * jax.random.uniform(keys[2], (SEGS, NLAT, LON), jnp.float32) ** shard_levels(keys[2], (SEGS, NLAT, LON), ((0, 2), (1, 4)), -0.2, 0.2)), 0.1, 1.0)
    land_sea = plant((jax.random.randint(keys[3], (NLAT, LON), 0, 4) < 3).astype(jnp.int32), jax.random.fold_in(keys[3], 1), 0, 1)
    depth_index = plant(jax.random.randint(keys[4], (NLAT, LON), 1, LEV + 1), jax.random.fold_in(keys[4], 1), 1, LEV).astype(jnp.int32)
    column_ops = draw_column_ops(jax.random.fold_in(keys[6], 71), 0)
    return dict(initial_states=initial_states, velocity=velocity, growth=growth, land_sea=land_sea, depth_index=depth_index, column_ops=column_ops)


half_sat_sq = 0.25
remin_rate = 0.2


def face_flux(behind, near_side, far_side, beyond, courant):
    return courant * (7.0 * (near_side + far_side) - (behind + beyond)) / 12.0 - jnp.abs(courant) * (3.0 * (far_side - near_side) - (beyond - behind)) / 12.0


def tendency(padded, north_faces, east_faces):
    merid = face_flux(padded[..., :-3, :], padded[..., 1:-2, :], padded[..., 2:-1, :], padded[..., 3:, :], north_faces)
    centre = padded[..., 2:-2, :]
    zonal_flux = face_flux(jnp.roll(centre, 1, axis=-1), centre, jnp.roll(centre, -1, axis=-1), jnp.roll(centre, -2, axis=-1), east_faces)
    return (merid[..., :-1, :] - merid[..., 1:, :]) + (jnp.roll(zonal_flux, 1, axis=-1) - zonal_flux)


def biology(mixed, rate, light_level, wet_cells):
    phosphate = mixed[..., 0, :, :, :]
    particles = mixed[..., 1, :, :, :]
    uptake = rate * light_level * phosphate * phosphate * phosphate / (phosphate * phosphate + half_sat_sq)
    return jnp.stack([wet_cells * (phosphate - uptake + remin_rate * particles), wet_cells * (particles + uptake - remin_rate * particles)], axis=-4)


def pad_rows(values):
    return jnp.pad(values, ((0, 0), (0, 0), (2, 2), (0, 0)))


def reference(initial_states, velocity, growth, land_sea, depth_index, column_ops):
    levels = jnp.arange(LEV, dtype=jnp.int32)
    wet_cells = jnp.where((land_sea[None] == 1) & (levels[:, None, None] < depth_index[None]), 1.0, 0.0).astype(jnp.float32)
    light_level = jnp.exp(-4.0 * levels.astype(jnp.float32) / LEV)[:, None, None]
    wet_north = jnp.concatenate([wet_cells[:, 1:], jnp.zeros_like(wet_cells[:, :1])], axis=1)
    operators = column_ops.astype(jnp.float32)

    def propagate(inputs):
        start_state, flow_field, rate = inputs
        east_faces = flow_field[0] * wet_cells * jnp.roll(wet_cells, -1, axis=-1)
        north_own = flow_field[1] * wet_cells * wet_north
        north_faces = jnp.concatenate([jnp.zeros_like(north_own[:, :1]), north_own], axis=1)
        tracer_state = wet_cells * start_state
        for step_index in range(STEPS):
            first_section = wet_cells * (tracer_state + tendency(pad_rows(tracer_state), north_faces, east_faces))
            advected = wet_cells * (0.5 * tracer_state + 0.5 * (first_section + tendency(pad_rows(first_section), north_faces, east_faces)))
            rounded = lax.optimization_barrier(advected.astype(jnp.bfloat16)).astype(jnp.float32)
            mixed = wet_cells * jnp.einsum("tkm,tmrl->tkrl", operators, rounded, precision=lax.Precision.HIGHEST)
            tracer_state = biology(mixed, rate[None], light_level, wet_cells)
        return tracer_state

    ends = lax.map(propagate, (initial_states, velocity, growth))
    previous = jnp.roll(ends, 1, axis=0)
    return wet_cells * (previous - initial_states)
```

```python
import jax
import jax.numpy as jnp
from jax import lax
from jax.experimental import pallas as pl
from jax.experimental.pallas import tpu as pltpu
from jax.sharding import PartitionSpec as P

STEPS = 4


half_sat_sq = 0.25
remin_rate = 0.2


def with_halo(cells, sides, width):
    for axis, dim in sides:
        count = lax.axis_size(axis)
        ends = count - 1
        head = lax.slice_in_dim(cells, 0, width, axis=dim)
        tail = lax.slice_in_dim(cells, cells.shape[dim] - width, cells.shape[dim], axis=dim)
        cells = jnp.concatenate(
            [
                lax.ppermute(tail, axis, [(i, (i + 1) % count) for i in range(ends)]),
                cells,
                lax.ppermute(head, axis, [((i + 1) % count, i) for i in range(ends)]),
            ],
            axis=dim,
        )
    return cells


def passed_along(block, axis, distance):
    devices = range(lax.axis_size(axis))
    route = [((i - distance) % len(devices), i) for i in devices]
    return lax.ppermute(block, axis, route)


def face_flux(behind, near_side, far_side, beyond, courant):
    return (
        courant * (7.0 * (near_side + far_side) - (behind + beyond)) / 12.0
        - jnp.abs(courant) * (3.0 * (far_side - near_side) - (beyond - behind)) / 12.0
    )


def tendency(padded, north_faces, east_faces):
    merid = face_flux(
        padded[..., :-3, :],
        padded[..., 1:-2, :],
        padded[..., 2:-1, :],
        padded[..., 3:, :],
        north_faces,
    )
    centre = padded[..., 2:-2, :]
    zonal_flux = face_flux(
        jnp.roll(centre, 1, axis=-1),
        centre,
        jnp.roll(centre, -1, axis=-1),
        jnp.roll(centre, -2, axis=-1),
        east_faces,
    )
    return merid[..., :-1, :] - merid[..., 1:, :] + (jnp.roll(zonal_flux, 1, axis=-1) - zonal_flux)


def biology(mixed, rate, light_level, wet_cells):
    phosphate = mixed[..., 0, :, :, :]
    particles = mixed[..., 1, :, :, :]
    uptake = (
        rate
        * light_level
        * phosphate
        * phosphate
        * phosphate
        / (phosphate * phosphate + half_sat_sq)
    )
    return jnp.stack(
        [
            wet_cells * (phosphate - uptake + remin_rate * particles),
            wet_cells * (particles + uptake - remin_rate * particles),
        ],
        axis=-4,
    )


def stepwise_shards(initial_states, velocity, growth, land_sea, depth_index, column_ops):
    seg_dev = initial_states.shape[0]
    lev_dev = initial_states.shape[2]
    first_level = lax.axis_index("depth") * lev_dev
    levels = first_level + lax.iota(jnp.int32, lev_dev)
    wet_cells = jnp.where(
        (land_sea[None] == 1) & (levels[:, None, None] < depth_index[None]), 1.0, 0.0
    ).astype(jnp.float32)
    light_level = jnp.exp(-4.0 * levels.astype(jnp.float32) / column_ops.shape[1])[:, None, None]
    own_rows = lax.dynamic_slice_in_dim(column_ops, first_level, lev_dev, 1)
    uptake_rate = growth[:, None]
    tracer_state = wet_cells * initial_states
    flow_stack = jnp.concatenate([velocity[:, 0], velocity[:, 1], wet_cells[None]], axis=0)
    flow_edges = with_halo(flow_stack, (("tile", 2),), 3)
    wet_edges = flow_edges[2 * seg_dev]
    north_wide = (flow_edges[seg_dev : 2 * seg_dev, :, :-1] * wet_edges[:, :-1] * wet_edges[:, 1:])[
        :, None
    ]
    wet_wide = wet_edges[:, 1:-1]
    east_wide = (flow_edges[:seg_dev, :, 1:-1] * wet_wide * jnp.roll(wet_wide, -1, axis=-1))[
        :, None
    ]
    north_faces = north_wide[:, :, :, 2:-2]
    east_faces = east_wide[:, :, :, 2:-2]
    for step_index in range(STEPS):
        padded = with_halo(tracer_state, (("tile", 3),), 4)
        first_section = wet_wide * (padded[:, :, :, 2:-2] + tendency(padded, north_wide, east_wide))
        advected = wet_cells * (
            0.5 * tracer_state
            + 0.5
            * (first_section[:, :, :, 2:-2] + tendency(first_section, north_faces, east_faces))
        )
        rounded = advected.astype(jnp.bfloat16)
        mixed = jnp.einsum(
            "tkm,stmrl->stkrl",
            own_rows,
            lax.all_gather(rounded, "depth", axis=2, tiled=True),
            preferred_element_type=jnp.float32,
        )
        tracer_state = biology(wet_cells * mixed, uptake_rate, light_level, wet_cells)
    previous = passed_along(tracer_state, "seg", 1)
    before = jnp.concatenate([previous, tracer_state[: seg_dev - 1]], axis=0)
    return wet_cells * (before - initial_states)


TILES = 4
BLOCKS = 4
LEVELS = 76
OWN_LEVELS = LEVELS // BLOCKS
PITCH = 80
OWN = 32
REACH = 4 * STEPS
WINDOW = OWN + 2 * REACH
CODE = 32000.0
FASTEST = 0.35
FIELDS = 4 * OWN_LEVELS + 4
ENDS = 2 * OWN_LEVELS + 2

F32 = jnp.float32
I16 = jnp.int16
VMEM = pl.BlockSpec(memory_space=pltpu.VMEM)


def coded(values):
    return jnp.floor(values + 0.5).astype(jnp.int32).astype(I16)


def exponent(largest):
    return jnp.clip(jnp.ceil(jnp.log2(jnp.maximum(largest, 1e-36))), -119.0, 125.0)


def index(shape, dim):
    return lax.broadcasted_iota(jnp.int32, shape, dim)


def pack_kernel(state, velocity, growth, land_sea, depth_index, out):
    scales = []
    for t in range(2):
        largest = jnp.abs(state[0, t, 0])
        for k in range(1, OWN_LEVELS):
            largest = jnp.maximum(largest, jnp.abs(state[0, t, k]))
        scales.append(exponent(largest))
    per_unit = [CODE * jnp.exp2(-e) for e in scales]
    wet_levels = jnp.where(land_sea[...] == 1, depth_index[...], 0).astype(F32)

    def field(n):
        which, k = divmod(n, OWN_LEVELS)
        if which < 2:
            return state[0, which, k] * per_unit[which]
        if which < 4:
            return velocity[0, which - 2, k] * (CODE / FASTEST)
        return [growth[0] * CODE, wet_levels, scales[0], scales[1]][k]

    left = index((8, 128), 1) < 64
    for pair in range(FIELDS // 8):
        rows = []
        for group in (2 * pair, 2 * pair + 1):
            lo, hi = (
                jnp.concatenate([field(4 * group + 2 * g), field(4 * group + 2 * g + 1)], axis=0)
                for g in range(2)
            )
            quarter = []
            for m in range(4):
                a = pltpu.roll(lo, (REACH - OWN * m) % 512, 1)
                b = pltpu.roll(hi, (REACH - OWN * m + 64) % 512, 1)
                quarter.append(
                    [
                        jnp.where(left, a[:, 128 * q : 128 * q + 128], b[:, 128 * q : 128 * q + 128])
                        for q in range(4)
                    ]
                )
            rows.append(quarter)
        for q in range(4):
            for m in range(4):
                block = jnp.concatenate([rows[0][m][q], rows[1][m][q]], axis=0)
                out[4 * q + m, 16 * pair : 16 * pair + 16, :] = coded(block)


def steps_kernel(recv, ops, out0, out1, out2, out3, cells, moved, flow, coef, plane, light, ends):
    sub = index((8, 128), 0)
    lane = index((8, 128), 1)
    left = lane < 64
    row = sub + 8 * (lane // 64)

    def spread(d, pair):
        sent = [
            recv[4 * t + d, 16 * pair : 16 * pair + 16, :].astype(jnp.int32).astype(F32)
            for t in range(4)
        ]
        fields = []
        for part in range(2):
            m = [x[8 * part : 8 * part + 8] for x in sent]
            up, across = {}, {}
            for h in range(2):
                a, b = m[2 * h], m[2 * h + 1]
                up[0, h] = jnp.where(sub < 4, a, pltpu.roll(b, 4, 0))
                up[1, h] = jnp.where(sub < 4, pltpu.roll(a, 4, 0), b)
            for p in range(2):
                a, b = up[p, 0], up[p, 1]
                across[p, 0] = jnp.where(left, a, pltpu.roll(b, 64, 1))
                across[p, 1] = jnp.where(left, pltpu.roll(a, 64, 1), b)
            fields += [across[0, 0], across[1, 0], across[0, 1], across[1, 1]]
        return fields

    def take(d, carry):
        last = spread(d, FIELDS // 8 - 1)
        plane[0] = last[4] * (1.0 / CODE)
        plane[1] = last[5]
        unit = [jnp.exp2(last[6 + t]) * (1.0 / CODE) for t in range(2)]
        for pair in range(FIELDS // 8):
            fields = last if pair == FIELDS // 8 - 1 else spread(d, pair)
            for i, value in enumerate(fields):
                which, k = divmod(8 * pair + i, OWN_LEVELS)
                if which < 2:
                    cells[pl.ds(which * 8 * PITCH + OWN_LEVELS * d + k, 8, stride=PITCH), :] = (
                        value * unit[which]
                    )
                elif which < 4:
                    flow[which - 2, OWN_LEVELS * d + k] = value * (FASTEST / CODE)
        return carry

    lax.fori_loop(0, BLOCKS, take, 0)

    wet_levels = plane[1]

    def north(x, by):
        y = pltpu.roll(x, 64, 1)
        return pltpu.roll(jnp.where(sub < by, y, x), 8 - by, 0)

    def south(x, by):
        y = pltpu.roll(x, 64, 1)
        return pltpu.roll(jnp.where(sub >= 8 - by, y, x), by, 0)

    def faces(w):
        size = jnp.abs(w)
        return (
            (-w - size) * (1.0 / 12.0),
            (7.0 * w + 3.0 * size) * (1.0 / 12.0),
            (7.0 * w - 3.0 * size) * (1.0 / 12.0),
            (size - w) * (1.0 / 12.0),
        )

    def prepare(k, carry):
        wet = jnp.where(wet_levels > k.astype(F32), 1.0, 0.0)
        for t in range(2):
            at = pl.ds(t * 8 * PITCH + k, 8, stride=PITCH)
            cells[at, :] = wet * cells[at, :]
        east_w = flow[0, k] * wet * pltpu.roll(wet, 127, 1)
        north_w = jnp.where(row == 15, 0.0, flow[1, k] * wet * north(wet, 1))
        west_w = pltpu.roll(east_w, 1, 1)
        south_w = jnp.where(row == 0, 0.0, south(north_w, 1))
        a, b, d, e = faces(east_w)
        a1, b1, d1, e1 = faces(west_w)
        p, q, r, s = faces(north_w)
        p1, q1, r1, s1 = faces(south_w)
        coef[k, 0] = wet * (1.0 + (d1 - b) + (r1 - q))
        coef[k, 1] = wet * a1
        coef[k, 2] = wet * (b1 - a)
        coef[k, 3] = wet * (e1 - d)
        coef[k, 4] = -wet * e
        coef[k, 5] = jnp.where(row <= 1, 0.0, wet * p1)
        coef[k, 6] = jnp.where(row == 0, 0.0, wet * (q1 - p))
        coef[k, 7] = jnp.where(row == 15, 0.0, wet * (s1 - r))
        coef[k, 8] = jnp.where(row >= 14, 0.0, -wet * s)
        return carry

    lax.fori_loop(0, LEVELS, prepare, 0, unroll=2)

    deep = index((LEVELS, 128), 0)
    light[...] = jnp.exp(deep.astype(F32) * (-4.0 / LEVELS))

    def stage(x, c):
        y = pltpu.roll(x, 64, 1)
        total = c[0] * x
        total += c[1] * pltpu.roll(x, 2, 1) + c[2] * pltpu.roll(x, 1, 1)
        total += c[3] * pltpu.roll(x, 127, 1) + c[4] * pltpu.roll(x, 126, 1)
        total += c[5] * pltpu.roll(jnp.where(sub >= 6, y, x), 2, 0)
        total += c[6] * pltpu.roll(jnp.where(sub >= 7, y, x), 1, 0)
        total += c[7] * pltpu.roll(jnp.where(sub < 1, y, x), 7, 0)
        total += c[8] * pltpu.roll(jnp.where(sub < 2, y, x), 6, 0)
        return total

    def transport(k, carry):
        c = [coef[k, i] for i in range(9)]
        for t in range(2):
            at = pl.ds(t * 8 * PITCH + k, 8, stride=PITCH)
            x = cells[at, :]
            moved[at, :] = 0.5 * (x + stage(stage(x, c), c))
        return carry

    def step(n, carry):
        lax.fori_loop(0, LEVELS, transport, 0, unroll=4)
        for pair in range(4):
            mixed = []
            for t in range(2):
                base = (t * 8 + 2 * pair) * PITCH
                both = jnp.concatenate(
                    [moved[base : base + LEVELS, :], moved[base + PITCH : base + PITCH + LEVELS, :]],
                    axis=1,
                ).astype(jnp.bfloat16)
                mixed.append(jnp.dot(ops[t], both, preferred_element_type=F32))
            for i in range(2):
                s = 2 * pair + i
                wet = deep.astype(F32) < plane[1, s : s + 1, :]
                p = jnp.where(wet, mixed[0][:, 128 * i : 128 * i + 128], 0.0)
                q = jnp.where(wet, mixed[1][:, 128 * i : 128 * i + 128], 0.0)
                square = p * p
                uptake = (plane[0, s : s + 1, :] * light[...]) * (
                    square * p / (square + half_sat_sq)
                )
                gain = uptake - remin_rate * q
                cells[s * PITCH : s * PITCH + LEVELS, :] = p - gain
                cells[(8 + s) * PITCH : (8 + s) * PITCH + LEVELS, :] = q + gain
        return carry

    lax.fori_loop(0, STEPS, step, 0)

    own = lax.axis_index("depth")
    chunk = lane // 32

    def send(n, carry):
        to = own ^ n
        blocks = []
        for t in range(2):
            def level(k):
                return cells[pl.ds(t * 8 * PITCH + OWN_LEVELS * to + k, 8, stride=PITCH), :]

            largest = jnp.abs(level(0))
            for k in range(1, OWN_LEVELS):
                largest = jnp.maximum(largest, jnp.abs(level(k)))
            scale = exponent(largest)
            per_unit = CODE * jnp.exp2(-scale)
            blocks += [level(k) * per_unit for k in range(OWN_LEVELS)] + [scale]
        for pair in range(ENDS // 4):
            halves = []
            for i in (2 * pair, 2 * pair + 1):
                a, b = blocks[2 * i], blocks[2 * i + 1]
                halves.append(
                    jnp.where(
                        chunk == 0,
                        pltpu.roll(a, 112, 1),
                        jnp.where(
                            chunk == 1,
                            pltpu.roll(a, 80, 1),
                            jnp.where(chunk == 2, pltpu.roll(b, 48, 1), pltpu.roll(b, 16, 1)),
                        ),
                    )
                )
            ends[n, 16 * pair : 16 * pair + 16, :] = coded(jnp.concatenate(halves, axis=0))
        return carry

    lax.fori_loop(0, BLOCKS, send, 0)
    for n, out in enumerate((out0, out1, out2, out3)):
        out[...] = ends[n]


def turn_kernel(in0, in1, in2, in3, out0, out1, out2, out3, got, sent):
    block = lax.axis_index("depth")
    tile = lax.axis_index("tile")
    for n, ref in enumerate((in0, in1, in2, in3)):
        got[block ^ n] = ref[...]
    sub = index((8, 128), 0)
    chunk = index((8, 128), 1) // 32
    for pair in range(ENDS // 4):
        whole = [
            got[d, 16 * pair : 16 * pair + 16, :].astype(jnp.int32).astype(F32) for d in range(4)
        ]
        halves = {t: [] for t in range(4)}
        for part in range(2):
            m = [x[8 * part : 8 * part + 8] for x in whole]
            lined = {}
            for par in range(2):
                for h in range(2):
                    z = [pltpu.roll(m[d], (32 * (d - 2 * par - h)) % 128, 1) for d in range(4)]
                    lined[par, h] = jnp.where(
                        chunk == 0,
                        z[0],
                        jnp.where(chunk == 1, z[1], jnp.where(chunk == 2, z[2], z[3])),
                    )
            for h in range(2):
                a, b = lined[0, h], lined[1, h]
                halves[2 * h].append(jnp.where(sub < 4, a, pltpu.roll(b, 4, 0)))
                halves[2 * h + 1].append(jnp.where(sub < 4, pltpu.roll(a, 4, 0), b))
        for t in range(4):
            sent[t, 16 * pair : 16 * pair + 16, :] = (
                jnp.concatenate(halves[t], axis=0).astype(jnp.int32).astype(I16)
            )
    for n, out in enumerate((out0, out1, out2, out3)):
        out[...] = sent[(tile + n) % TILES]


def finish_kernel(in0, in1, in2, in3, state, land_sea, depth_index, out, got):
    block = lax.axis_index("depth")
    tile = lax.axis_index("tile")
    for n, ref in enumerate((in0, in1, in2, in3)):
        got[(tile + TILES - n) % TILES] = ref[...]
    wet_levels = jnp.where(land_sea[...] == 1, depth_index[...], 0)
    first = block * OWN_LEVELS
    for q in range(4):
        lanes = slice(128 * q, 128 * q + 128)
        values = []
        for pair in range(ENDS // 4):
            x = got[q, 16 * pair : 16 * pair + 16, :].astype(jnp.int32).astype(F32)
            values += [x[0:4], x[4:8], x[8:12], x[12:16]]
        for t in range(2):
            base = t * (OWN_LEVELS + 1)
            unit = jnp.exp2(values[base + OWN_LEVELS]) * (1.0 / CODE)
            for k in range(OWN_LEVELS):
                wet = wet_levels[:, lanes] > first + k
                out[0, t, k, :, lanes] = jnp.where(
                    wet, values[base + k] * unit - state[0, t, k, :, lanes], 0.0
                )


def window_shards(initial_states, velocity, growth, land_sea, depth_index, column_ops):
    group = ("tile", "depth")
    devices = TILES * BLOCKS
    chunk = (2 * FIELDS, 128)
    packed = pl.pallas_call(
        pack_kernel,
        out_shape=jax.ShapeDtypeStruct((devices,) + chunk, I16),
        in_specs=[VMEM] * 5,
        out_specs=VMEM,
    )(initial_states, velocity, growth, land_sea, depth_index)
    received = lax.all_to_all(packed, group, 0, 0, tiled=True)
    message = jax.ShapeDtypeStruct((4 * ENDS, 128), I16)
    out = pl.pallas_call(
        steps_kernel,
        out_shape=[message] * 4,
        in_specs=[VMEM] * 2,
        out_specs=[VMEM] * 4,
        scratch_shapes=[
            pltpu.VMEM((2 * 8 * PITCH, 128), F32),
            pltpu.VMEM((2 * 8 * PITCH, 128), F32),
            pltpu.VMEM((2, LEVELS, 8, 128), F32),
            pltpu.VMEM((LEVELS, 9, 8, 128), F32),
            pltpu.VMEM((2, 8, 128), F32),
            pltpu.VMEM((LEVELS, 128), F32),
            pltpu.VMEM((4, 4 * ENDS, 128), I16),
        ],
    )(received, column_ops)
    got = [out[0]] + [
        lax.ppermute(out[n], "depth", [(i, i ^ n) for i in range(BLOCKS)]) for n in range(1, 4)
    ]
    turned = pl.pallas_call(
        turn_kernel,
        out_shape=[message] * 4,
        in_specs=[VMEM] * 4,
        out_specs=[VMEM] * 4,
        scratch_shapes=[pltpu.VMEM((4, 4 * ENDS, 128), I16)] * 2,
    )(*got)
    segs = lax.axis_size("seg")
    last = [
        lax.ppermute(
            turned[n],
            ("seg", "tile"),
            [
                (s * TILES + t, ((s + 1) % segs) * TILES + (t + n) % TILES)
                for s in range(segs)
                for t in range(TILES)
            ],
        )
        for n in range(4)
    ]
    return pl.pallas_call(
        finish_kernel,
        out_shape=jax.ShapeDtypeStruct(initial_states.shape, F32),
        in_specs=[VMEM] * 7,
        out_specs=VMEM,
        scratch_shapes=[pltpu.VMEM((4, 4 * ENDS, 128), I16)],
    )(*last, initial_states, land_sea, depth_index)


def shards(initial_states, velocity, growth, land_sea, depth_index, column_ops):
    fits = (
        lax.axis_size("tile") == TILES
        and lax.axis_size("depth") == BLOCKS
        and initial_states.shape == (1, 2, OWN_LEVELS, 4, TILES * BLOCKS * OWN)
    )
    plan = window_shards if fits else stepwise_shards
    return plan(initial_states, velocity, growth, land_sea, depth_index, column_ops)


def solution(mesh):
    return jax.shard_map(
        shards,
        mesh=mesh,
        in_specs=(
            P("seg", None, "depth", "tile", None),
            P("seg", None, "depth", "tile", None),
            P("seg", "tile", None),
            P("tile", None),
            P("tile", None),
            P(),
        ),
        out_specs=P("seg", None, "depth", "tile", None),
        check_vma=False,
    )
```

```python
import jax
import jax.numpy as jnp
from jax import lax
from jax.experimental import pallas as pl
from jax.experimental.pallas import tpu as pltpu
from jax.sharding import PartitionSpec as P

STEPS = 4


half_sat_sq = 0.25
remin_rate = 0.2


def with_halo(cells, sides, width):
    for axis, dim in sides:
        count = lax.axis_size(axis)
        ends = count - 1
        head = lax.slice_in_dim(cells, 0, width, axis=dim)
        tail = lax.slice_in_dim(cells, cells.shape[dim] - width, cells.shape[dim], axis=dim)
        cells = jnp.concatenate(
            [
                lax.ppermute(tail, axis, [(i, (i + 1) % count) for i in range(ends)]),
                cells,
                lax.ppermute(head, axis, [((i + 1) % count, i) for i in range(ends)]),
            ],
            axis=dim,
        )
    return cells


def passed_along(block, axis, distance):
    devices = range(lax.axis_size(axis))
    route = [((i - distance) % len(devices), i) for i in devices]
    return lax.ppermute(block, axis, route)


def face_flux(behind, near_side, far_side, beyond, courant):
    return (
        courant * (7.0 * (near_side + far_side) - (behind + beyond)) / 12.0
        - jnp.abs(courant) * (3.0 * (far_side - near_side) - (beyond - behind)) / 12.0
    )


def tendency(padded, north_faces, east_faces):
    merid = face_flux(
        padded[..., :-3, :],
        padded[..., 1:-2, :],
        padded[..., 2:-1, :],
        padded[..., 3:, :],
        north_faces,
    )
    centre = padded[..., 2:-2, :]
    zonal_flux = face_flux(
        jnp.roll(centre, 1, axis=-1),
        centre,
        jnp.roll(centre, -1, axis=-1),
        jnp.roll(centre, -2, axis=-1),
        east_faces,
    )
    return merid[..., :-1, :] - merid[..., 1:, :] + (jnp.roll(zonal_flux, 1, axis=-1) - zonal_flux)


def biology(mixed, rate, light_level, wet_cells):
    phosphate = mixed[..., 0, :, :, :]
    particles = mixed[..., 1, :, :, :]
    uptake = (
        rate
        * light_level
        * phosphate
        * phosphate
        * phosphate
        / (phosphate * phosphate + half_sat_sq)
    )
    return jnp.stack(
        [
            wet_cells * (phosphate - uptake + remin_rate * particles),
            wet_cells * (particles + uptake - remin_rate * particles),
        ],
        axis=-4,
    )


def stepwise_shards(initial_states, velocity, growth, land_sea, depth_index, column_ops):
    seg_dev = initial_states.shape[0]
    lev_dev = initial_states.shape[2]
    first_level = lax.axis_index("depth") * lev_dev
    levels = first_level + lax.iota(jnp.int32, lev_dev)
    wet_cells = jnp.where(
        (land_sea[None] == 1) & (levels[:, None, None] < depth_index[None]), 1.0, 0.0
    ).astype(jnp.float32)
    light_level = jnp.exp(-4.0 * levels.astype(jnp.float32) / column_ops.shape[1])[:, None, None]
    own_rows = lax.dynamic_slice_in_dim(column_ops, first_level, lev_dev, 1)
    uptake_rate = growth[:, None]
    tracer_state = wet_cells * initial_states
    flow_stack = jnp.concatenate([velocity[:, 0], velocity[:, 1], wet_cells[None]], axis=0)
    flow_edges = with_halo(flow_stack, (("tile", 2),), 3)
    wet_edges = flow_edges[2 * seg_dev]
    north_wide = (flow_edges[seg_dev : 2 * seg_dev, :, :-1] * wet_edges[:, :-1] * wet_edges[:, 1:])[
        :, None
    ]
    wet_wide = wet_edges[:, 1:-1]
    east_wide = (flow_edges[:seg_dev, :, 1:-1] * wet_wide * jnp.roll(wet_wide, -1, axis=-1))[
        :, None
    ]
    north_faces = north_wide[:, :, :, 2:-2]
    east_faces = east_wide[:, :, :, 2:-2]
    for step_index in range(STEPS):
        padded = with_halo(tracer_state, (("tile", 3),), 4)
        first_section = wet_wide * (padded[:, :, :, 2:-2] + tendency(padded, north_wide, east_wide))
        advected = wet_cells * (
            0.5 * tracer_state
            + 0.5
            * (first_section[:, :, :, 2:-2] + tendency(first_section, north_faces, east_faces))
        )
        rounded = advected.astype(jnp.bfloat16)
        mixed = jnp.einsum(
            "tkm,stmrl->stkrl",
            own_rows,
            lax.all_gather(rounded, "depth", axis=2, tiled=True),
            preferred_element_type=jnp.float32,
        )
        tracer_state = biology(wet_cells * mixed, uptake_rate, light_level, wet_cells)
    previous = passed_along(tracer_state, "seg", 1)
    before = jnp.concatenate([previous, tracer_state[: seg_dev - 1]], axis=0)
    return wet_cells * (before - initial_states)


TILES = 4
BLOCKS = 4
LEVELS = 76
OWN_LEVELS = LEVELS // BLOCKS
PITCH = 80
OWN = 32
REACH = 4 * STEPS
WINDOW = OWN + 2 * REACH
CODE = 32000.0
FASTEST = 0.35
FIELDS = 4 * OWN_LEVELS + 4
ENDS = 2 * OWN_LEVELS + 2

F32 = jnp.float32
I16 = jnp.int16
VMEM = pl.BlockSpec(memory_space=pltpu.VMEM)


def coded(values):
    return jnp.floor(values + 0.5).astype(jnp.int32).astype(I16)


def exponent(largest):
    return jnp.clip(jnp.ceil(jnp.log2(jnp.maximum(largest, 1e-36))), -119.0, 125.0)


def index(shape, dim):
    return lax.broadcasted_iota(jnp.int32, shape, dim)


def pack_kernel(state, velocity, growth, land_sea, depth_index, out):
    scales = []
    for t in range(2):
        largest = jnp.abs(state[0, t, 0])
        for k in range(1, OWN_LEVELS):
            largest = jnp.maximum(largest, jnp.abs(state[0, t, k]))
        scales.append(exponent(largest))
    per_unit = [CODE * jnp.exp2(-e) for e in scales]
    wet_levels = jnp.where(land_sea[...] == 1, depth_index[...], 0).astype(F32)

    def field(n):
        which, k = divmod(n, OWN_LEVELS)
        if which < 2:
            return state[0, which, k] * per_unit[which]
        if which < 4:
            return velocity[0, which - 2, k] * (CODE / FASTEST)
        return [growth[0] * CODE, wet_levels, scales[0], scales[1]][k]

    left = index((8, 128), 1) < 64
    for pair in range(FIELDS // 8):
        rows = []
        for group in (2 * pair, 2 * pair + 1):
            lo, hi = (
                jnp.concatenate([field(4 * group + 2 * g), field(4 * group + 2 * g + 1)], axis=0)
                for g in range(2)
            )
            quarter = []
            for m in range(4):
                a = pltpu.roll(lo, (REACH - OWN * m) % 512, 1)
                b = pltpu.roll(hi, (REACH - OWN * m + 64) % 512, 1)
                quarter.append(
                    [
                        jnp.where(left, a[:, 128 * q : 128 * q + 128], b[:, 128 * q : 128 * q + 128])
                        for q in range(4)
                    ]
                )
            rows.append(quarter)
        for q in range(4):
            for m in range(4):
                block = jnp.concatenate([rows[0][m][q], rows[1][m][q]], axis=0)
                out[4 * q + m, 16 * pair : 16 * pair + 16, :] = coded(block)


def steps_kernel(recv, ops, out0, out1, out2, out3, cells, moved, flow, coef, plane, light, ends):
    sub = index((8, 128), 0)
    lane = index((8, 128), 1)
    left = lane < 64

    def spread(d, pair):
        sent = [
            recv[4 * t + d, 16 * pair : 16 * pair + 16, :].astype(jnp.int32).astype(F32)
            for t in range(4)
        ]
        fields = []
        for part in range(2):
            m = [x[8 * part : 8 * part + 8] for x in sent]
            up, across = {}, {}
            for h in range(2):
                a, b = m[2 * h], m[2 * h + 1]
                up[0, h] = jnp.where(sub < 4, a, pltpu.roll(b, 4, 0))
                up[1, h] = jnp.where(sub < 4, pltpu.roll(a, 4, 0), b)
            for p in range(2):
                a, b = up[p, 0], up[p, 1]
                across[p, 0] = jnp.where(left, a, pltpu.roll(b, 64, 1))
                across[p, 1] = jnp.where(left, pltpu.roll(a, 64, 1), b)
            fields += [across[0, 0], across[1, 0], across[0, 1], across[1, 1]]
        return fields

    def take(d, carry):
        last = spread(d, FIELDS // 8 - 1)
        plane[0] = last[4] * (1.0 / CODE)
        plane[1] = last[5]
        unit = [jnp.exp2(last[6 + t]) * (1.0 / CODE) for t in range(2)]
        for pair in range(FIELDS // 8):
            fields = last if pair == FIELDS // 8 - 1 else spread(d, pair)
            for i, value in enumerate(fields):
                which, k = divmod(8 * pair + i, OWN_LEVELS)
                if which < 2:
                    cells[pl.ds(which * 8 * PITCH + OWN_LEVELS * d + k, 8, stride=PITCH), :] = (
                        value * unit[which]
                    )
                elif which < 4:
                    at = pl.ds((which - 2) * 8 * PITCH + OWN_LEVELS * d + k, 8, stride=PITCH)
                    flow[at, :] = value * (FASTEST / CODE)
        return carry

    lax.fori_loop(0, BLOCKS, take, 0)

    for field in (cells, flow):
        for s in range(16):
            field[s * PITCH + LEVELS : (s + 1) * PITCH, :] = jnp.zeros((PITCH - LEVELS, 128), F32)

    def block(base, g):
        return pl.ds(pl.multiple_of(base * PITCH + 8 * g, 8), 8)

    def faces(w):
        size = jnp.abs(w)
        return (
            (-w - size) * (1.0 / 12.0),
            (7.0 * w + 3.0 * size) * (1.0 / 12.0),
            (7.0 * w - 3.0 * size) * (1.0 / 12.0),
            (size - w) * (1.0 / 12.0),
        )

    def prepare(g, carry):
        level = (sub + 8 * g).astype(F32)
        wet = [jnp.where(plane[1, s : s + 1, :] > level, 1.0, 0.0) for s in range(8)]
        for t in range(2):
            for s in range(8):
                at = block(8 * t + s, g)
                cells[at, :] = wet[s] * cells[at, :]
        beyond = jnp.where(left, pltpu.roll(wet[0], 64, 1), 0.0)
        north_w = [
            flow[block(8 + s, g), :] * wet[s] * (wet[s + 1] if s < 7 else beyond) for s in range(8)
        ]
        first = jnp.where(left, 0.0, pltpu.roll(north_w[7], 64, 1))
        merid = [faces(w) for w in [first] + north_w]
        for s in range(8):
            east_w = flow[block(s, g), :] * wet[s] * pltpu.roll(wet[s], 127, 1)
            a, b, d, e = faces(east_w)
            a1, b1, d1, e1 = faces(pltpu.roll(east_w, 1, 1))
            p1, q1, r1, s1 = merid[s]
            p, q, r, s0 = merid[s + 1]
            south = [wet[s] * p1, wet[s] * (q1 - p)]
            north = [wet[s] * (s1 - r), -wet[s] * s0]
            if s < 2:
                south[0] = jnp.where(left, 0.0, south[0])
            if s < 1:
                south[1] = jnp.where(left, 0.0, south[1])
            if s > 6:
                north[0] = jnp.where(left, north[0], 0.0)
            if s > 5:
                north[1] = jnp.where(left, north[1], 0.0)
            coef[g, s, 0] = wet[s] * (1.0 + (d1 - b) + (r1 - q))
            coef[g, s, 1] = wet[s] * a1
            coef[g, s, 2] = wet[s] * (b1 - a)
            coef[g, s, 3] = wet[s] * (e1 - d)
            coef[g, s, 4] = -wet[s] * e
            coef[g, s, 5], coef[g, s, 6] = south
            coef[g, s, 7], coef[g, s, 8] = north
        return carry

    lax.fori_loop(0, PITCH // 8, prepare, 0)

    deep = index((LEVELS, 128), 0)
    light[...] = jnp.exp(deep.astype(F32) * (-4.0 / LEVELS))

    def stage(x, g):
        turned = [pltpu.roll(x[s], 64, 1) for s in (6, 7, 0, 1)]
        column = turned[:2] + x + turned[2:]
        results = []
        for s in range(8):
            c = [coef[g, s, i] for i in range(9)]
            near, far = column[s + 1 : s + 4], (column[s], column[s + 4])
            centre = near[1]
            results.append(
                (c[0] * centre + c[6] * near[0] + c[7] * near[2])
                + (c[5] * far[0] + c[8] * far[1])
                + (c[2] * pltpu.roll(centre, 1, 1) + c[3] * pltpu.roll(centre, 127, 1))
                + (c[1] * pltpu.roll(centre, 2, 1) + c[4] * pltpu.roll(centre, 126, 1))
            )
        return results

    def transport(g, carry):
        for t in range(2):
            x = [cells[block(8 * t + s, g), :] for s in range(8)]
            y = stage(stage(x, g), g)
            for s in range(8):
                moved[block(8 * t + s, g), :] = 0.5 * (x[s] + y[s])
        return carry

    def step(n, carry):
        lax.fori_loop(0, PITCH // 8, transport, 0)
        for pair in range(4):
            mixed = []
            for t in range(2):
                base = (t * 8 + 2 * pair) * PITCH
                both = jnp.concatenate(
                    [moved[base : base + LEVELS, :], moved[base + PITCH : base + PITCH + LEVELS, :]],
                    axis=1,
                ).astype(jnp.bfloat16)
                mixed.append(jnp.dot(ops[t], both, preferred_element_type=F32))
            for i in range(2):
                s = 2 * pair + i
                wet = deep.astype(F32) < plane[1, s : s + 1, :]
                p = jnp.where(wet, mixed[0][:, 128 * i : 128 * i + 128], 0.0)
                q = jnp.where(wet, mixed[1][:, 128 * i : 128 * i + 128], 0.0)
                square = p * p
                uptake = (plane[0, s : s + 1, :] * light[...]) * (
                    square * p / (square + half_sat_sq)
                )
                gain = uptake - remin_rate * q
                cells[s * PITCH : s * PITCH + LEVELS, :] = p - gain
                cells[(8 + s) * PITCH : (8 + s) * PITCH + LEVELS, :] = q + gain
        return carry

    lax.fori_loop(0, STEPS, step, 0)

    own = lax.axis_index("depth")
    chunk = lane // 32

    def send(n, carry):
        to = own ^ n
        blocks = []
        for t in range(2):
            def level(k):
                return cells[pl.ds(t * 8 * PITCH + OWN_LEVELS * to + k, 8, stride=PITCH), :]

            largest = jnp.abs(level(0))
            for k in range(1, OWN_LEVELS):
                largest = jnp.maximum(largest, jnp.abs(level(k)))
            scale = exponent(largest)
            per_unit = CODE * jnp.exp2(-scale)
            blocks += [level(k) * per_unit for k in range(OWN_LEVELS)] + [scale]
        for pair in range(ENDS // 4):
            halves = []
            for i in (2 * pair, 2 * pair + 1):
                a, b = blocks[2 * i], blocks[2 * i + 1]
                halves.append(
                    jnp.where(
                        chunk == 0,
                        pltpu.roll(a, 112, 1),
                        jnp.where(
                            chunk == 1,
                            pltpu.roll(a, 80, 1),
                            jnp.where(chunk == 2, pltpu.roll(b, 48, 1), pltpu.roll(b, 16, 1)),
                        ),
                    )
                )
            ends[n, 16 * pair : 16 * pair + 16, :] = coded(jnp.concatenate(halves, axis=0))
        return carry

    lax.fori_loop(0, BLOCKS, send, 0)
    for n, out in enumerate((out0, out1, out2, out3)):
        out[...] = ends[n]


def turn_kernel(in0, in1, in2, in3, out0, out1, out2, out3, got, sent):
    block = lax.axis_index("depth")
    tile = lax.axis_index("tile")
    for n, ref in enumerate((in0, in1, in2, in3)):
        got[block ^ n] = ref[...]
    sub = index((8, 128), 0)
    chunk = index((8, 128), 1) // 32
    for pair in range(ENDS // 4):
        whole = [
            got[d, 16 * pair : 16 * pair + 16, :].astype(jnp.int32).astype(F32) for d in range(4)
        ]
        halves = {t: [] for t in range(4)}
        for part in range(2):
            m = [x[8 * part : 8 * part + 8] for x in whole]
            lined = {}
            for par in range(2):
                for h in range(2):
                    z = [pltpu.roll(m[d], (32 * (d - 2 * par - h)) % 128, 1) for d in range(4)]
                    lined[par, h] = jnp.where(
                        chunk == 0,
                        z[0],
                        jnp.where(chunk == 1, z[1], jnp.where(chunk == 2, z[2], z[3])),
                    )
            for h in range(2):
                a, b = lined[0, h], lined[1, h]
                halves[2 * h].append(jnp.where(sub < 4, a, pltpu.roll(b, 4, 0)))
                halves[2 * h + 1].append(jnp.where(sub < 4, pltpu.roll(a, 4, 0), b))
        for t in range(4):
            sent[t, 16 * pair : 16 * pair + 16, :] = (
                jnp.concatenate(halves[t], axis=0).astype(jnp.int32).astype(I16)
            )
    for n, out in enumerate((out0, out1, out2, out3)):
        out[...] = sent[(tile + n) % TILES]


def finish_kernel(in0, in1, in2, in3, state, land_sea, depth_index, out, got):
    block = lax.axis_index("depth")
    tile = lax.axis_index("tile")
    for n, ref in enumerate((in0, in1, in2, in3)):
        got[(tile + TILES - n) % TILES] = ref[...]
    wet_levels = jnp.where(land_sea[...] == 1, depth_index[...], 0)
    first = block * OWN_LEVELS
    for q in range(4):
        lanes = slice(128 * q, 128 * q + 128)
        values = []
        for pair in range(ENDS // 4):
            x = got[q, 16 * pair : 16 * pair + 16, :].astype(jnp.int32).astype(F32)
            values += [x[0:4], x[4:8], x[8:12], x[12:16]]
        for t in range(2):
            base = t * (OWN_LEVELS + 1)
            unit = jnp.exp2(values[base + OWN_LEVELS]) * (1.0 / CODE)
            for k in range(OWN_LEVELS):
                wet = wet_levels[:, lanes] > first + k
                out[0, t, k, :, lanes] = jnp.where(
                    wet, values[base + k] * unit - state[0, t, k, :, lanes], 0.0
                )


def near(*arrays):
    return [pltpu.with_memory_space_constraint(x, pltpu.VMEM) for x in arrays]


def call(kernel, outs, scratch, *args, reserve=8, place=near):
    return pl.pallas_call(
        kernel,
        out_shape=outs,
        in_specs=[VMEM] * len(args),
        out_specs=jax.tree.map(lambda _: VMEM, outs),
        scratch_shapes=scratch,
        compiler_params=pltpu.CompilerParams(vmem_limit_bytes=reserve << 20),
    )(*place(*args))


def window_shards(initial_states, velocity, growth, land_sea, depth_index, column_ops):
    message = pltpu.VMEM((4 * ENDS, 128), I16)
    slots = pltpu.VMEM((4, 4 * ENDS, 128), I16)
    cells = pltpu.VMEM((2 * 8 * PITCH, 128), F32)
    packed = call(
        pack_kernel,
        pltpu.VMEM((TILES * BLOCKS, 2 * FIELDS, 128), I16),
        [],
        initial_states,
        velocity,
        growth,
        land_sea,
        depth_index,
        place=lambda *args: args,
    )
    received = lax.all_to_all(packed, ("tile", "depth"), 0, 0, tiled=True)
    out = call(
        steps_kernel,
        [message] * 4,
        [
            cells,
            cells,
            cells,
            pltpu.VMEM((PITCH // 8, 8, 9, 8, 128), F32),
            pltpu.VMEM((2, 8, 128), F32),
            pltpu.VMEM((LEVELS, 128), F32),
            slots,
        ],
        received,
        column_ops,
        reserve=16,
    )
    got = [out[0]] + [
        lax.ppermute(out[n], "depth", [(i, i ^ n) for i in range(BLOCKS)]) for n in range(1, 4)
    ]
    turned = call(turn_kernel, [message] * 4, [slots] * 2, *got)
    segs = lax.axis_size("seg")
    last = [
        lax.ppermute(
            turned[n],
            ("seg", "tile"),
            [
                (s * TILES + t, ((s + 1) % segs) * TILES + (t + n) % TILES)
                for s in range(segs)
                for t in range(TILES)
            ],
        )
        for n in range(4)
    ]
    return call(
        finish_kernel,
        jax.ShapeDtypeStruct(initial_states.shape, F32),
        [slots],
        *last,
        initial_states,
        land_sea,
        depth_index,
    )


def shards(initial_states, velocity, growth, land_sea, depth_index, column_ops):
    fits = (
        lax.axis_size("tile") == TILES
        and lax.axis_size("depth") == BLOCKS
        and initial_states.shape == (1, 2, OWN_LEVELS, 4, TILES * BLOCKS * OWN)
    )
    plan = window_shards if fits else stepwise_shards
    return plan(initial_states, velocity, growth, land_sea, depth_index, column_ops)


def solution(mesh):
    return jax.shard_map(
        shards,
        mesh=mesh,
        in_specs=(
            P("seg", None, "depth", "tile", None),
            P("seg", None, "depth", "tile", None),
            P("seg", "tile", None),
            P("tile", None),
            P("tile", None),
            P(),
        ),
        out_specs=P("seg", None, "depth", "tile", None),
        check_vma=False,
    )
```

```python
import jax
import jax.numpy as jnp
from jax import lax
from jax.experimental import pallas as pl
from jax.experimental.pallas import tpu as pltpu
from jax.sharding import PartitionSpec as P

STEPS = 4


half_sat_sq = 0.25
remin_rate = 0.2


def with_halo(cells, sides, width):
    for axis, dim in sides:
        count = lax.axis_size(axis)
        ends = count - 1
        head = lax.slice_in_dim(cells, 0, width, axis=dim)
        tail = lax.slice_in_dim(cells, cells.shape[dim] - width, cells.shape[dim], axis=dim)
        cells = jnp.concatenate(
            [
                lax.ppermute(tail, axis, [(i, (i + 1) % count) for i in range(ends)]),
                cells,
                lax.ppermute(head, axis, [((i + 1) % count, i) for i in range(ends)]),
            ],
            axis=dim,
        )
    return cells


def passed_along(block, axis, distance):
    devices = range(lax.axis_size(axis))
    route = [((i - distance) % len(devices), i) for i in devices]
    return lax.ppermute(block, axis, route)


def face_flux(behind, near_side, far_side, beyond, courant):
    return (
        courant * (7.0 * (near_side + far_side) - (behind + beyond)) / 12.0
        - jnp.abs(courant) * (3.0 * (far_side - near_side) - (beyond - behind)) / 12.0
    )


def tendency(padded, north_faces, east_faces):
    merid = face_flux(
        padded[..., :-3, :],
        padded[..., 1:-2, :],
        padded[..., 2:-1, :],
        padded[..., 3:, :],
        north_faces,
    )
    centre = padded[..., 2:-2, :]
    zonal_flux = face_flux(
        jnp.roll(centre, 1, axis=-1),
        centre,
        jnp.roll(centre, -1, axis=-1),
        jnp.roll(centre, -2, axis=-1),
        east_faces,
    )
    return merid[..., :-1, :] - merid[..., 1:, :] + (jnp.roll(zonal_flux, 1, axis=-1) - zonal_flux)


def biology(mixed, rate, light_level, wet_cells):
    phosphate = mixed[..., 0, :, :, :]
    particles = mixed[..., 1, :, :, :]
    uptake = (
        rate
        * light_level
        * phosphate
        * phosphate
        * phosphate
        / (phosphate * phosphate + half_sat_sq)
    )
    return jnp.stack(
        [
            wet_cells * (phosphate - uptake + remin_rate * particles),
            wet_cells * (particles + uptake - remin_rate * particles),
        ],
        axis=-4,
    )


def stepwise_shards(initial_states, velocity, growth, land_sea, depth_index, column_ops):
    seg_dev = initial_states.shape[0]
    lev_dev = initial_states.shape[2]
    first_level = lax.axis_index("depth") * lev_dev
    levels = first_level + lax.iota(jnp.int32, lev_dev)
    wet_cells = jnp.where(
        (land_sea[None] == 1) & (levels[:, None, None] < depth_index[None]), 1.0, 0.0
    ).astype(jnp.float32)
    light_level = jnp.exp(-4.0 * levels.astype(jnp.float32) / column_ops.shape[1])[:, None, None]
    own_rows = lax.dynamic_slice_in_dim(column_ops, first_level, lev_dev, 1)
    uptake_rate = growth[:, None]
    tracer_state = wet_cells * initial_states
    flow_stack = jnp.concatenate([velocity[:, 0], velocity[:, 1], wet_cells[None]], axis=0)
    flow_edges = with_halo(flow_stack, (("tile", 2),), 3)
    wet_edges = flow_edges[2 * seg_dev]
    north_wide = (flow_edges[seg_dev : 2 * seg_dev, :, :-1] * wet_edges[:, :-1] * wet_edges[:, 1:])[
        :, None
    ]
    wet_wide = wet_edges[:, 1:-1]
    east_wide = (flow_edges[:seg_dev, :, 1:-1] * wet_wide * jnp.roll(wet_wide, -1, axis=-1))[
        :, None
    ]
    north_faces = north_wide[:, :, :, 2:-2]
    east_faces = east_wide[:, :, :, 2:-2]
    for step_index in range(STEPS):
        padded = with_halo(tracer_state, (("tile", 3),), 4)
        first_section = wet_wide * (padded[:, :, :, 2:-2] + tendency(padded, north_wide, east_wide))
        advected = wet_cells * (
            0.5 * tracer_state
            + 0.5
            * (first_section[:, :, :, 2:-2] + tendency(first_section, north_faces, east_faces))
        )
        rounded = advected.astype(jnp.bfloat16)
        mixed = jnp.einsum(
            "tkm,stmrl->stkrl",
            own_rows,
            lax.all_gather(rounded, "depth", axis=2, tiled=True),
            preferred_element_type=jnp.float32,
        )
        tracer_state = biology(wet_cells * mixed, uptake_rate, light_level, wet_cells)
    previous = passed_along(tracer_state, "seg", 1)
    before = jnp.concatenate([previous, tracer_state[: seg_dev - 1]], axis=0)
    return wet_cells * (before - initial_states)


TILES = 4
BLOCKS = 4
LEVELS = 76
OWN_LEVELS = LEVELS // BLOCKS
PITCH = 80
OWN = 32
REACH = 4 * STEPS
WINDOW = OWN + 2 * REACH
CODE = 32000.0
FASTEST = 0.35
FIELDS = 4 * OWN_LEVELS + 4
ENDS = 2 * OWN_LEVELS + 2

F32 = jnp.float32
I16 = jnp.int16
VMEM = pl.BlockSpec(memory_space=pltpu.VMEM)


def coded(values):
    return jnp.floor(values + 0.5).astype(jnp.int32).astype(I16)


def exponent(largest):
    return jnp.clip(jnp.ceil(jnp.log2(jnp.maximum(largest, 1e-36))), -119.0, 125.0)


def index(shape, dim):
    return lax.broadcasted_iota(jnp.int32, shape, dim)


def pack_kernel(state, velocity, growth, land_sea, depth_index, out):
    scales = []
    for t in range(2):
        largest = jnp.abs(state[0, t, 0])
        for k in range(1, OWN_LEVELS):
            largest = jnp.maximum(largest, jnp.abs(state[0, t, k]))
        scales.append(exponent(largest))
    per_unit = [CODE * jnp.exp2(-e) for e in scales]
    wet_levels = jnp.where(land_sea[...] == 1, depth_index[...], 0).astype(F32)

    def field(n):
        which, k = divmod(n, OWN_LEVELS)
        if which < 2:
            return state[0, which, k] * per_unit[which]
        if which < 4:
            return velocity[0, which - 2, k] * (CODE / FASTEST)
        return [growth[0] * CODE, wet_levels, scales[0], scales[1]][k]

    left = index((8, 128), 1) < 64
    for pair in range(FIELDS // 8):
        rows = []
        for group in (2 * pair, 2 * pair + 1):
            lo, hi = (
                jnp.concatenate([field(4 * group + 2 * g), field(4 * group + 2 * g + 1)], axis=0)
                for g in range(2)
            )
            quarter = []
            for m in range(4):
                a = pltpu.roll(lo, (REACH - OWN * m) % 512, 1)
                b = pltpu.roll(hi, (REACH - OWN * m + 64) % 512, 1)
                quarter.append(
                    [
                        jnp.where(left, a[:, 128 * q : 128 * q + 128], b[:, 128 * q : 128 * q + 128])
                        for q in range(4)
                    ]
                )
            rows.append(quarter)
        for q in range(4):
            for m in range(4):
                block = jnp.concatenate([rows[0][m][q], rows[1][m][q]], axis=0)
                out[4 * q + m, 16 * pair : 16 * pair + 16, :] = coded(block)


def steps_kernel(
    recv, ops, out0, out1, out2, out3, cells, firsts, moved, flow, coef, plane, light, ends
):
    sub = index((8, 128), 0)
    lane = index((8, 128), 1)
    left = lane < 64

    def spread(d, pair):
        sent = [
            recv[4 * t + d, 16 * pair : 16 * pair + 16, :].astype(jnp.int32).astype(F32)
            for t in range(4)
        ]
        fields = []
        for part in range(2):
            m = [x[8 * part : 8 * part + 8] for x in sent]
            up, across = {}, {}
            for h in range(2):
                a, b = m[2 * h], m[2 * h + 1]
                up[0, h] = jnp.where(sub < 4, a, pltpu.roll(b, 4, 0))
                up[1, h] = jnp.where(sub < 4, pltpu.roll(a, 4, 0), b)
            for p in range(2):
                a, b = up[p, 0], up[p, 1]
                across[p, 0] = jnp.where(left, a, pltpu.roll(b, 64, 1))
                across[p, 1] = jnp.where(left, pltpu.roll(a, 64, 1), b)
            fields += [across[0, 0], across[1, 0], across[0, 1], across[1, 1]]
        return fields

    def take(d, carry):
        last = spread(d, FIELDS // 8 - 1)
        plane[0] = last[4] * (1.0 / CODE)
        plane[1] = last[5]
        unit = [jnp.exp2(last[6 + t]) * (1.0 / CODE) for t in range(2)]
        for pair in range(FIELDS // 8):
            fields = last if pair == FIELDS // 8 - 1 else spread(d, pair)
            for i, value in enumerate(fields):
                which, k = divmod(8 * pair + i, OWN_LEVELS)
                if which < 2:
                    cells[pl.ds(which * 8 * PITCH + OWN_LEVELS * d + k, 8, stride=PITCH), :] = (
                        value * unit[which]
                    )
                elif which < 4:
                    at = pl.ds((which - 2) * 8 * PITCH + OWN_LEVELS * d + k, 8, stride=PITCH)
                    flow[at, :] = value * (FASTEST / CODE)
        return carry

    lax.fori_loop(0, BLOCKS, take, 0)

    for field in (cells, flow):
        for s in range(16):
            field[s * PITCH + LEVELS : (s + 1) * PITCH, :] = jnp.zeros((PITCH - LEVELS, 128), F32)

    def block(base, g):
        return pl.ds(pl.multiple_of(base * PITCH + 8 * g, 8), 8)

    def faces(w):
        size = jnp.abs(w)
        return (
            (-w - size) * (1.0 / 12.0),
            (7.0 * w + 3.0 * size) * (1.0 / 12.0),
            (7.0 * w - 3.0 * size) * (1.0 / 12.0),
            (size - w) * (1.0 / 12.0),
        )

    def prepare(g, carry):
        level = (sub + 8 * g).astype(F32)
        wet = [jnp.where(plane[1, s : s + 1, :] > level, 1.0, 0.0) for s in range(8)]
        for t in range(2):
            for s in range(8):
                at = block(8 * t + s, g)
                cells[at, :] = wet[s] * cells[at, :]
        beyond = jnp.where(left, pltpu.roll(wet[0], 64, 1), 0.0)
        north_w = [
            flow[block(8 + s, g), :] * wet[s] * (wet[s + 1] if s < 7 else beyond) for s in range(8)
        ]
        first = jnp.where(left, 0.0, pltpu.roll(north_w[7], 64, 1))
        merid = [faces(w) for w in [first] + north_w]
        for s in range(8):
            east_w = flow[block(s, g), :] * wet[s] * pltpu.roll(wet[s], 127, 1)
            a, b, d, e = faces(east_w)
            a1, b1, d1, e1 = faces(pltpu.roll(east_w, 1, 1))
            p1, q1, r1, s1 = merid[s]
            p, q, r, s0 = merid[s + 1]
            south = [wet[s] * p1, wet[s] * (q1 - p)]
            north = [wet[s] * (s1 - r), -wet[s] * s0]
            if s < 2:
                south[0] = jnp.where(left, 0.0, south[0])
            if s < 1:
                south[1] = jnp.where(left, 0.0, south[1])
            if s > 6:
                north[0] = jnp.where(left, north[0], 0.0)
            if s > 5:
                north[1] = jnp.where(left, north[1], 0.0)
            coef[g, s, 0] = wet[s] * (1.0 + (d1 - b) + (r1 - q))
            coef[g, s, 1] = wet[s] * a1
            coef[g, s, 2] = wet[s] * (b1 - a)
            coef[g, s, 3] = wet[s] * (e1 - d)
            coef[g, s, 4] = -wet[s] * e
            coef[g, s, 5], coef[g, s, 6] = south
            coef[g, s, 7], coef[g, s, 8] = north
        return carry

    lax.fori_loop(0, PITCH // 8, prepare, 0, unroll=5)

    deep = index((LEVELS, 128), 0)
    light[...] = jnp.exp(deep.astype(F32) * (-4.0 / LEVELS))

    def combine(c, near, far):
        centre = near[1]
        return (
            (c[0] * centre + c[6] * near[0] + c[7] * near[2])
            + (c[5] * far[0] + c[8] * far[1])
            + (c[2] * pltpu.roll(centre, 1, 1) + c[3] * pltpu.roll(centre, 127, 1))
            + (c[1] * pltpu.roll(centre, 2, 1) + c[4] * pltpu.roll(centre, 126, 1))
        )

    def stage(source, g, emit):
        def at(t, s):
            return source[block(8 * t + s, g), :]

        columns = []
        for t in range(2):
            inner = [at(t, s) for s in range(8)]
            turned = [pltpu.roll(inner[s], 64, 1) for s in (6, 7, 0, 1)]
            columns.append(turned[:2] + inner + turned[2:])
        for s in range(8):
            c = [coef[g, s, i] for i in range(9)]
            for t in range(2):
                k = columns[t]
                emit(t, s, combine(c, k[s + 1 : s + 4], (k[s], k[s + 4])))

    def first_stage(g, carry):
        def emit(t, s, value):
            firsts[block(8 * t + s, g), :] = value

        stage(cells, g, emit)
        return carry

    def second_stage(g, carry):
        def emit(t, s, value):
            at = block(8 * t + s, g)
            moved[at, :] = 0.5 * (cells[at, :] + value)

        stage(firsts, g, emit)
        return carry

    def step(n, carry):
        lax.fori_loop(0, PITCH // 8, first_stage, 0, unroll=True)
        lax.fori_loop(0, PITCH // 8, second_stage, 0, unroll=True)
        for pair in range(4):
            mixed = []
            for t in range(2):
                base = (t * 8 + 2 * pair) * PITCH
                both = jnp.concatenate(
                    [moved[base : base + LEVELS, :], moved[base + PITCH : base + PITCH + LEVELS, :]],
                    axis=1,
                ).astype(jnp.bfloat16)
                mixed.append(jnp.dot(ops[t], both, preferred_element_type=F32))
            for i in range(2):
                s = 2 * pair + i
                wet = deep.astype(F32) < plane[1, s : s + 1, :]
                p = jnp.where(wet, mixed[0][:, 128 * i : 128 * i + 128], 0.0)
                q = jnp.where(wet, mixed[1][:, 128 * i : 128 * i + 128], 0.0)
                square = p * p
                uptake = (plane[0, s : s + 1, :] * light[...]) * (
                    square * p / (square + half_sat_sq)
                )
                gain = uptake - remin_rate * q
                cells[s * PITCH : s * PITCH + LEVELS, :] = p - gain
                cells[(8 + s) * PITCH : (8 + s) * PITCH + LEVELS, :] = q + gain
        return carry

    lax.fori_loop(0, STEPS, step, 0)

    own = lax.axis_index("depth")
    chunk = lane // 32

    def send(n, carry):
        to = own ^ n
        blocks = []
        for t in range(2):
            def level(k):
                return cells[pl.ds(t * 8 * PITCH + OWN_LEVELS * to + k, 8, stride=PITCH), :]

            largest = jnp.abs(level(0))
            for k in range(1, OWN_LEVELS):
                largest = jnp.maximum(largest, jnp.abs(level(k)))
            scale = exponent(largest)
            per_unit = CODE * jnp.exp2(-scale)
            blocks += [level(k) * per_unit for k in range(OWN_LEVELS)] + [scale]
        for pair in range(ENDS // 4):
            halves = []
            for i in (2 * pair, 2 * pair + 1):
                a, b = blocks[2 * i], blocks[2 * i + 1]
                halves.append(
                    jnp.where(
                        chunk == 0,
                        pltpu.roll(a, 112, 1),
                        jnp.where(
                            chunk == 1,
                            pltpu.roll(a, 80, 1),
                            jnp.where(chunk == 2, pltpu.roll(b, 48, 1), pltpu.roll(b, 16, 1)),
                        ),
                    )
                )
            ends[n, 16 * pair : 16 * pair + 16, :] = coded(jnp.concatenate(halves, axis=0))
        return carry

    lax.fori_loop(0, BLOCKS, send, 0)
    for n, out in enumerate((out0, out1, out2, out3)):
        out[...] = ends[n]


def turn_kernel(in0, in1, in2, in3, out0, out1, out2, out3, got, sent):
    block = lax.axis_index("depth")
    tile = lax.axis_index("tile")
    for n, ref in enumerate((in0, in1, in2, in3)):
        got[block ^ n] = ref[...]
    sub = index((8, 128), 0)
    chunk = index((8, 128), 1) // 32
    for pair in range(ENDS // 4):
        whole = [
            got[d, 16 * pair : 16 * pair + 16, :].astype(jnp.int32).astype(F32) for d in range(4)
        ]
        halves = {t: [] for t in range(4)}
        for part in range(2):
            m = [x[8 * part : 8 * part + 8] for x in whole]
            lined = {}
            for par in range(2):
                for h in range(2):
                    z = [pltpu.roll(m[d], (32 * (d - 2 * par - h)) % 128, 1) for d in range(4)]
                    lined[par, h] = jnp.where(
                        chunk == 0,
                        z[0],
                        jnp.where(chunk == 1, z[1], jnp.where(chunk == 2, z[2], z[3])),
                    )
            for h in range(2):
                a, b = lined[0, h], lined[1, h]
                halves[2 * h].append(jnp.where(sub < 4, a, pltpu.roll(b, 4, 0)))
                halves[2 * h + 1].append(jnp.where(sub < 4, pltpu.roll(a, 4, 0), b))
        for t in range(4):
            sent[t, 16 * pair : 16 * pair + 16, :] = (
                jnp.concatenate(halves[t], axis=0).astype(jnp.int32).astype(I16)
            )
    for n, out in enumerate((out0, out1, out2, out3)):
        out[...] = sent[(tile + n) % TILES]


def finish_kernel(in0, in1, in2, in3, state, land_sea, depth_index, out, got):
    block = lax.axis_index("depth")
    tile = lax.axis_index("tile")
    for n, ref in enumerate((in0, in1, in2, in3)):
        got[(tile + TILES - n) % TILES] = ref[...]
    wet_levels = jnp.where(land_sea[...] == 1, depth_index[...], 0)
    first = block * OWN_LEVELS
    for q in range(4):
        lanes = slice(128 * q, 128 * q + 128)
        values = []
        for pair in range(ENDS // 4):
            x = got[q, 16 * pair : 16 * pair + 16, :].astype(jnp.int32).astype(F32)
            values += [x[0:4], x[4:8], x[8:12], x[12:16]]
        for t in range(2):
            base = t * (OWN_LEVELS + 1)
            unit = jnp.exp2(values[base + OWN_LEVELS]) * (1.0 / CODE)
            for k in range(OWN_LEVELS):
                wet = wet_levels[:, lanes] > first + k
                out[0, t, k, :, lanes] = jnp.where(
                    wet, values[base + k] * unit - state[0, t, k, :, lanes], 0.0
                )


def near(*arrays):
    return [pltpu.with_memory_space_constraint(x, pltpu.VMEM) for x in arrays]


def call(kernel, outs, scratch, *args, reserve=8, place=near):
    return pl.pallas_call(
        kernel,
        out_shape=outs,
        in_specs=[VMEM] * len(args),
        out_specs=jax.tree.map(lambda _: VMEM, outs),
        scratch_shapes=scratch,
        compiler_params=pltpu.CompilerParams(vmem_limit_bytes=reserve << 20),
    )(*place(*args))


def window_shards(initial_states, velocity, growth, land_sea, depth_index, column_ops):
    message = pltpu.VMEM((4 * ENDS, 128), I16)
    slots = pltpu.VMEM((4, 4 * ENDS, 128), I16)
    cells = pltpu.VMEM((2 * 8 * PITCH, 128), F32)
    packed = call(
        pack_kernel,
        pltpu.VMEM((TILES * BLOCKS, 2 * FIELDS, 128), I16),
        [],
        initial_states,
        velocity,
        growth,
        land_sea,
        depth_index,
        reserve=60,
        place=lambda *args: args,
    )
    received = lax.all_to_all(packed, ("tile", "depth"), 0, 0, tiled=True)
    out = call(
        steps_kernel,
        [message] * 4,
        [
            cells,
            cells,
            cells,
            cells,
            pltpu.VMEM((PITCH // 8, 8, 9, 8, 128), F32),
            pltpu.VMEM((2, 8, 128), F32),
            pltpu.VMEM((LEVELS, 128), F32),
            slots,
        ],
        received,
        column_ops,
        reserve=16,
    )
    got = [out[0]] + [
        lax.ppermute(out[n], "depth", [(i, i ^ n) for i in range(BLOCKS)]) for n in range(1, 4)
    ]
    turned = call(turn_kernel, [message] * 4, [slots] * 2, *got)
    segs = lax.axis_size("seg")
    last = [
        lax.ppermute(
            turned[n],
            ("seg", "tile"),
            [
                (s * TILES + t, ((s + 1) % segs) * TILES + (t + n) % TILES)
                for s in range(segs)
                for t in range(TILES)
            ],
        )
        for n in range(4)
    ]
    return call(
        finish_kernel,
        jax.ShapeDtypeStruct(initial_states.shape, F32),
        [slots],
        *last,
        initial_states,
        land_sea,
        depth_index,
    )


def shards(initial_states, velocity, growth, land_sea, depth_index, column_ops):
    fits = (
        lax.axis_size("tile") == TILES
        and lax.axis_size("depth") == BLOCKS
        and initial_states.shape == (1, 2, OWN_LEVELS, 4, TILES * BLOCKS * OWN)
    )
    plan = window_shards if fits else stepwise_shards
    return plan(initial_states, velocity, growth, land_sea, depth_index, column_ops)


def solution(mesh):
    return jax.shard_map(
        shards,
        mesh=mesh,
        in_specs=(
            P("seg", None, "depth", "tile", None),
            P("seg", None, "depth", "tile", None),
            P("seg", "tile", None),
            P("tile", None),
            P("tile", None),
            P(),
        ),
        out_specs=P("seg", None, "depth", "tile", None),
        check_vma=False,
    )
```

```python
import jax
import jax.numpy as jnp
from jax import lax
from jax.experimental import pallas as pl
from jax.experimental.pallas import tpu as pltpu
from jax.sharding import PartitionSpec as P

STEPS = 4


half_sat_sq = 0.25
remin_rate = 0.2


def with_halo(cells, sides, width):
    for axis, dim in sides:
        count = lax.axis_size(axis)
        ends = count - 1
        head = lax.slice_in_dim(cells, 0, width, axis=dim)
        tail = lax.slice_in_dim(cells, cells.shape[dim] - width, cells.shape[dim], axis=dim)
        cells = jnp.concatenate(
            [
                lax.ppermute(tail, axis, [(i, (i + 1) % count) for i in range(ends)]),
                cells,
                lax.ppermute(head, axis, [((i + 1) % count, i) for i in range(ends)]),
            ],
            axis=dim,
        )
    return cells


def passed_along(block, axis, distance):
    devices = range(lax.axis_size(axis))
    route = [((i - distance) % len(devices), i) for i in devices]
    return lax.ppermute(block, axis, route)


def face_flux(behind, near_side, far_side, beyond, courant):
    return (
        courant * (7.0 * (near_side + far_side) - (behind + beyond)) / 12.0
        - jnp.abs(courant) * (3.0 * (far_side - near_side) - (beyond - behind)) / 12.0
    )


def tendency(padded, north_faces, east_faces):
    merid = face_flux(
        padded[..., :-3, :],
        padded[..., 1:-2, :],
        padded[..., 2:-1, :],
        padded[..., 3:, :],
        north_faces,
    )
    centre = padded[..., 2:-2, :]
    zonal_flux = face_flux(
        jnp.roll(centre, 1, axis=-1),
        centre,
        jnp.roll(centre, -1, axis=-1),
        jnp.roll(centre, -2, axis=-1),
        east_faces,
    )
    return merid[..., :-1, :] - merid[..., 1:, :] + (jnp.roll(zonal_flux, 1, axis=-1) - zonal_flux)


def biology(mixed, rate, light_level, wet_cells):
    phosphate = mixed[..., 0, :, :, :]
    particles = mixed[..., 1, :, :, :]
    uptake = (
        rate
        * light_level
        * phosphate
        * phosphate
        * phosphate
        / (phosphate * phosphate + half_sat_sq)
    )
    return jnp.stack(
        [
            wet_cells * (phosphate - uptake + remin_rate * particles),
            wet_cells * (particles + uptake - remin_rate * particles),
        ],
        axis=-4,
    )


def stepwise_shards(initial_states, velocity, growth, land_sea, depth_index, column_ops):
    seg_dev = initial_states.shape[0]
    lev_dev = initial_states.shape[2]
    first_level = lax.axis_index("depth") * lev_dev
    levels = first_level + lax.iota(jnp.int32, lev_dev)
    wet_cells = jnp.where(
        (land_sea[None] == 1) & (levels[:, None, None] < depth_index[None]), 1.0, 0.0
    ).astype(jnp.float32)
    light_level = jnp.exp(-4.0 * levels.astype(jnp.float32) / column_ops.shape[1])[:, None, None]
    own_rows = lax.dynamic_slice_in_dim(column_ops, first_level, lev_dev, 1)
    uptake_rate = growth[:, None]
    tracer_state = wet_cells * initial_states
    flow_stack = jnp.concatenate([velocity[:, 0], velocity[:, 1], wet_cells[None]], axis=0)
    flow_edges = with_halo(flow_stack, (("tile", 2),), 3)
    wet_edges = flow_edges[2 * seg_dev]
    north_wide = (flow_edges[seg_dev : 2 * seg_dev, :, :-1] * wet_edges[:, :-1] * wet_edges[:, 1:])[
        :, None
    ]
    wet_wide = wet_edges[:, 1:-1]
    east_wide = (flow_edges[:seg_dev, :, 1:-1] * wet_wide * jnp.roll(wet_wide, -1, axis=-1))[
        :, None
    ]
    north_faces = north_wide[:, :, :, 2:-2]
    east_faces = east_wide[:, :, :, 2:-2]
    for step_index in range(STEPS):
        padded = with_halo(tracer_state, (("tile", 3),), 4)
        first_section = wet_wide * (padded[:, :, :, 2:-2] + tendency(padded, north_wide, east_wide))
        advected = wet_cells * (
            0.5 * tracer_state
            + 0.5
            * (first_section[:, :, :, 2:-2] + tendency(first_section, north_faces, east_faces))
        )
        rounded = advected.astype(jnp.bfloat16)
        mixed = jnp.einsum(
            "tkm,stmrl->stkrl",
            own_rows,
            lax.all_gather(rounded, "depth", axis=2, tiled=True),
            preferred_element_type=jnp.float32,
        )
        tracer_state = biology(wet_cells * mixed, uptake_rate, light_level, wet_cells)
    previous = passed_along(tracer_state, "seg", 1)
    before = jnp.concatenate([previous, tracer_state[: seg_dev - 1]], axis=0)
    return wet_cells * (before - initial_states)


TILES = 4
BLOCKS = 4
LEVELS = 76
OWN_LEVELS = LEVELS // BLOCKS
PITCH = 80
OWN = 32
REACH = 4 * STEPS
WINDOW = OWN + 2 * REACH
CODE = 32000.0
FASTEST = 0.35
FIELDS = 4 * OWN_LEVELS + 4
ENDS = 2 * OWN_LEVELS + 2
PIECE = 2 * FIELDS
MAIN = 4 * FIELDS
NEAR, FAR = (0, 1, 3), (2,)

F32 = jnp.float32
I16 = jnp.int16
VMEM = pl.BlockSpec(memory_space=pltpu.VMEM)


def coded(values):
    return jnp.floor(values + 0.5).astype(jnp.int32).astype(I16)


def exponent(largest):
    return jnp.clip(jnp.ceil(jnp.log2(jnp.maximum(largest, 1e-36))), -119.0, 125.0)


def index(shape, dim):
    return lax.broadcasted_iota(jnp.int32, shape, dim)


def pack_kernel(state, velocity, growth, land_sea, depth_index, *refs):
    outs, turned = refs[:-1], refs[-1]
    scales = []
    for t in range(2):
        largest = jnp.abs(state[0, t, 0])
        for k in range(1, OWN_LEVELS):
            largest = jnp.maximum(largest, jnp.abs(state[0, t, k]))
        scales.append(exponent(largest))
    per_unit = [CODE * jnp.exp2(-e) for e in scales]
    wet_levels = jnp.where(land_sea[...] == 1, depth_index[...], 0).astype(F32)

    def field(n):
        which, k = divmod(n, OWN_LEVELS)
        if which < 2:
            return state[0, which, k] * per_unit[which]
        if which < 4:
            return velocity[0, which - 2, k] * (CODE / FASTEST)
        return [growth[0] * CODE, wet_levels, scales[0], scales[1]][k]

    for pair in range(FIELDS // 2):
        rows = jnp.concatenate([field(2 * pair), field(2 * pair + 1)], axis=0)
        turned[8 * pair : 8 * pair + 8, :] = pltpu.roll(rows, REACH, 1)
    tile = lax.axis_index("tile")
    chunk = index((8, 128), 1) // 32

    def part(row, count, q):
        lanes = pl.ds(pl.multiple_of(128 * (q % TILES), 128), 128)
        return turned[row : row + count, lanes]

    for n, out in enumerate(outs):
        q = tile + n
        for row in range(0, MAIN, 16):
            out[row : row + 16, :] = coded(part(row, 16, q))
        for pair in range(FIELDS // 16):
            halves = []
            for group in (2 * pair, 2 * pair + 1):
                late = group + FIELDS // 8
                tails = [part(8 * i, 8, q + 1) for i in (2 * late, 2 * group, 2 * late + 1, 2 * group + 1)]
                tails = [tails[0]] + [pltpu.roll(tails[i], 32 * i, 1) for i in (1, 2, 3)]
                halves.append(by_chunk(chunk, tails))
            row = MAIN + 16 * pair
            out[row : row + 16, :] = coded(jnp.concatenate(halves, axis=0))


def by_chunk(chunk, values):
    return jnp.where(
        chunk == 0,
        values[0],
        jnp.where(chunk == 1, values[1], jnp.where(chunk == 2, values[2], values[3])),
    )


def wide(values):
    return values.astype(jnp.int32).astype(F32)


def narrow(values):
    return values.astype(jnp.int32).astype(I16)


def split_kernel(*refs):
    count = len(refs) - BLOCKS - 1
    sources, outs, sent = refs[:count], refs[count:-1], refs[-1]
    block = lax.axis_index("depth")
    left = index((8, 128), 1) < 64
    chunk = index((8, 128), 1) // 32
    odd = chunk % 2 == 1
    for i, ref in enumerate(sources):
        for pair in range(FIELDS // 8):
            pieces = [[] for _ in range(BLOCKS)]
            both = wide(ref[32 * pair : 32 * pair + 16, :]), wide(ref[32 * pair + 16 : 32 * pair + 32, :])
            late = pair // (FIELDS // 16)
            row = MAIN + 16 * (pair % (FIELDS // 16))
            tails = wide(ref[row : row + 16, :])
            for part in range(2):
                lo, hi = both[part][0:8], both[part][8:16]
                tail = tails[8 * part : 8 * part + 8]
                if late:
                    tail = pltpu.roll(tail, 32, 1)
                pieces[0].append(jnp.where(left, lo, pltpu.roll(hi, 64, 1)))
                pieces[1].append(jnp.where(left, pltpu.roll(lo, 96, 1), pltpu.roll(hi, 32, 1)))
                pieces[2].append(jnp.where(left, pltpu.roll(lo, 64, 1), hi))
                last = jnp.where(left, pltpu.roll(lo, 32, 1), pltpu.roll(hi, 96, 1))
                pieces[3].append(jnp.where(odd, tail, last))
            row = PIECE * i + 16 * pair
            for d in range(BLOCKS):
                sent[d, row : row + 16, :] = narrow(jnp.concatenate(pieces[d], axis=0))
    for n, out in enumerate(outs):
        out[...] = sent[block ^ n]


def steps_kernel(*refs):
    arrived, (ops, out0, out1, out2, out3, recv), scratch = refs[:8], refs[8:14], refs[14:]
    cells, firsts, moved, flow, coef, plane, light, ends = scratch
    own = lax.axis_index("depth")
    tile = lax.axis_index("tile")
    for n in range(BLOCKS):
        for ref, distances in ((arrived[n], NEAR), (arrived[BLOCKS + n], FAR)):
            for i, distance in enumerate(distances):
                source = (tile + TILES - distance) % TILES
                recv[4 * source + (own ^ n)] = ref[PIECE * i : PIECE * i + PIECE, :]
    sub = index((8, 128), 0)
    lane = index((8, 128), 1)
    left = lane < 64

    def spread(d, pair):
        sent = [
            recv[4 * t + d, 16 * pair : 16 * pair + 16, :].astype(jnp.int32).astype(F32)
            for t in range(4)
        ]
        fields = []
        for part in range(2):
            m = [x[8 * part : 8 * part + 8] for x in sent]
            up, across = {}, {}
            for h in range(2):
                a, b = m[2 * h], m[2 * h + 1]
                up[0, h] = jnp.where(sub < 4, a, pltpu.roll(b, 4, 0))
                up[1, h] = jnp.where(sub < 4, pltpu.roll(a, 4, 0), b)
            for p in range(2):
                a, b = up[p, 0], up[p, 1]
                across[p, 0] = jnp.where(left, a, pltpu.roll(b, 64, 1))
                across[p, 1] = jnp.where(left, pltpu.roll(a, 64, 1), b)
            fields += [across[0, 0], across[1, 0], across[0, 1], across[1, 1]]
        return fields

    def take(d, carry):
        last = spread(d, FIELDS // 8 - 1)
        plane[0] = last[4] * (1.0 / CODE)
        plane[1] = last[5]
        unit = [jnp.exp2(last[6 + t]) * (1.0 / CODE) for t in range(2)]
        for pair in range(FIELDS // 8):
            fields = last if pair == FIELDS // 8 - 1 else spread(d, pair)
            for i, value in enumerate(fields):
                which, k = divmod(8 * pair + i, OWN_LEVELS)
                if which < 2:
                    cells[pl.ds(which * 8 * PITCH + OWN_LEVELS * d + k, 8, stride=PITCH), :] = (
                        value * unit[which]
                    )
                elif which < 4:
                    at = pl.ds((which - 2) * 8 * PITCH + OWN_LEVELS * d + k, 8, stride=PITCH)
                    flow[at, :] = value * (FASTEST / CODE)
        return carry

    lax.fori_loop(0, BLOCKS, take, 0)

    for field in (cells, flow):
        for s in range(16):
            field[s * PITCH + LEVELS : (s + 1) * PITCH, :] = jnp.zeros((PITCH - LEVELS, 128), F32)

    def block(base, g):
        return pl.ds(pl.multiple_of(base * PITCH + 8 * g, 8), 8)

    def faces(w):
        size = jnp.abs(w)
        return (
            (-w - size) * (1.0 / 12.0),
            (7.0 * w + 3.0 * size) * (1.0 / 12.0),
            (7.0 * w - 3.0 * size) * (1.0 / 12.0),
            (size - w) * (1.0 / 12.0),
        )

    def prepare(g, carry):
        level = (sub + 8 * g).astype(F32)
        wet = [jnp.where(plane[1, s : s + 1, :] > level, 1.0, 0.0) for s in range(8)]
        for t in range(2):
            for s in range(8):
                at = block(8 * t + s, g)
                cells[at, :] = wet[s] * cells[at, :]
        beyond = jnp.where(left, pltpu.roll(wet[0], 64, 1), 0.0)
        north_w = [
            flow[block(8 + s, g), :] * wet[s] * (wet[s + 1] if s < 7 else beyond) for s in range(8)
        ]
        first = jnp.where(left, 0.0, pltpu.roll(north_w[7], 64, 1))
        merid = [faces(w) for w in [first] + north_w]
        for s in range(8):
            east_w = flow[block(s, g), :] * wet[s] * pltpu.roll(wet[s], 127, 1)
            a, b, d, e = faces(east_w)
            a1, b1, d1, e1 = faces(pltpu.roll(east_w, 1, 1))
            p1, q1, r1, s1 = merid[s]
            p, q, r, s0 = merid[s + 1]
            south = [wet[s] * p1, wet[s] * (q1 - p)]
            north = [wet[s] * (s1 - r), -wet[s] * s0]
            if s < 2:
                south[0] = jnp.where(left, 0.0, south[0])
            if s < 1:
                south[1] = jnp.where(left, 0.0, south[1])
            if s > 6:
                north[0] = jnp.where(left, north[0], 0.0)
            if s > 5:
                north[1] = jnp.where(left, north[1], 0.0)
            coef[g, s, 0] = wet[s] * (1.0 + (d1 - b) + (r1 - q))
            coef[g, s, 1] = wet[s] * a1
            coef[g, s, 2] = wet[s] * (b1 - a)
            coef[g, s, 3] = wet[s] * (e1 - d)
            coef[g, s, 4] = -wet[s] * e
            coef[g, s, 5], coef[g, s, 6] = south
            coef[g, s, 7], coef[g, s, 8] = north
        return carry

    lax.fori_loop(0, PITCH // 8, prepare, 0, unroll=5)

    deep = index((LEVELS, 128), 0)
    light[...] = jnp.exp(deep.astype(F32) * (-4.0 / LEVELS))

    def combine(c, near, far):
        centre = near[1]
        return (
            (c[0] * centre + c[6] * near[0] + c[7] * near[2])
            + (c[5] * far[0] + c[8] * far[1])
            + (c[2] * pltpu.roll(centre, 1, 1) + c[3] * pltpu.roll(centre, 127, 1))
            + (c[1] * pltpu.roll(centre, 2, 1) + c[4] * pltpu.roll(centre, 126, 1))
        )

    def stage(source, g, emit):
        def at(t, s):
            return source[block(8 * t + s, g), :]

        columns = []
        for t in range(2):
            inner = [at(t, s) for s in range(8)]
            turned = [pltpu.roll(inner[s], 64, 1) for s in (6, 7, 0, 1)]
            columns.append(turned[:2] + inner + turned[2:])
        for s in range(8):
            c = [coef[g, s, i] for i in range(9)]
            for t in range(2):
                k = columns[t]
                emit(t, s, combine(c, k[s + 1 : s + 4], (k[s], k[s + 4])))

    def first_stage(g, carry):
        def emit(t, s, value):
            firsts[block(8 * t + s, g), :] = value

        stage(cells, g, emit)
        return carry

    def second_stage(g, carry):
        def emit(t, s, value):
            at = block(8 * t + s, g)
            moved[at, :] = 0.5 * (cells[at, :] + value)

        stage(firsts, g, emit)
        return carry

    def step(n, carry):
        lax.fori_loop(0, PITCH // 8, first_stage, 0, unroll=True)
        lax.fori_loop(0, PITCH // 8, second_stage, 0, unroll=True)
        for pair in range(4):
            mixed = []
            for t in range(2):
                base = (t * 8 + 2 * pair) * PITCH
                both = jnp.concatenate(
                    [moved[base : base + LEVELS, :], moved[base + PITCH : base + PITCH + LEVELS, :]],
                    axis=1,
                ).astype(jnp.bfloat16)
                mixed.append(jnp.dot(ops[t], both, preferred_element_type=F32))
            for i in range(2):
                s = 2 * pair + i
                wet = deep.astype(F32) < plane[1, s : s + 1, :]
                p = jnp.where(wet, mixed[0][:, 128 * i : 128 * i + 128], 0.0)
                q = jnp.where(wet, mixed[1][:, 128 * i : 128 * i + 128], 0.0)
                square = p * p
                uptake = (plane[0, s : s + 1, :] * light[...]) * (
                    square * p / (square + half_sat_sq)
                )
                gain = uptake - remin_rate * q
                cells[s * PITCH : s * PITCH + LEVELS, :] = p - gain
                cells[(8 + s) * PITCH : (8 + s) * PITCH + LEVELS, :] = q + gain
        return carry

    lax.fori_loop(0, STEPS, step, 0)

    chunk = lane // 32

    def send(n, carry):
        to = own ^ n
        blocks = []
        for t in range(2):
            def level(k):
                return cells[pl.ds(t * 8 * PITCH + OWN_LEVELS * to + k, 8, stride=PITCH), :]

            largest = jnp.abs(level(0))
            for k in range(1, OWN_LEVELS):
                largest = jnp.maximum(largest, jnp.abs(level(k)))
            scale = exponent(largest)
            per_unit = CODE * jnp.exp2(-scale)
            blocks += [level(k) * per_unit for k in range(OWN_LEVELS)] + [scale]
        for pair in range(ENDS // 4):
            halves = []
            for i in (2 * pair, 2 * pair + 1):
                a, b = blocks[2 * i], blocks[2 * i + 1]
                halves.append(
                    jnp.where(
                        chunk == 0,
                        pltpu.roll(a, 112, 1),
                        jnp.where(
                            chunk == 1,
                            pltpu.roll(a, 80, 1),
                            jnp.where(chunk == 2, pltpu.roll(b, 48, 1), pltpu.roll(b, 16, 1)),
                        ),
                    )
                )
            ends[n, 16 * pair : 16 * pair + 16, :] = coded(jnp.concatenate(halves, axis=0))
        return carry

    lax.fori_loop(0, BLOCKS, send, 0)
    for n, out in enumerate((out0, out1, out2, out3)):
        out[...] = ends[n]


def turn_kernel(in0, in1, in2, in3, out0, out1, out2, out3, got, sent):
    block = lax.axis_index("depth")
    tile = lax.axis_index("tile")
    for n, ref in enumerate((in0, in1, in2, in3)):
        got[block ^ n] = ref[...]
    sub = index((8, 128), 0)
    chunk = index((8, 128), 1) // 32
    for pair in range(ENDS // 4):
        whole = [
            got[d, 16 * pair : 16 * pair + 16, :].astype(jnp.int32).astype(F32) for d in range(4)
        ]
        halves = {t: [] for t in range(4)}
        for part in range(2):
            m = [x[8 * part : 8 * part + 8] for x in whole]
            lined = {}
            for par in range(2):
                for h in range(2):
                    z = [pltpu.roll(m[d], (32 * (d - 2 * par - h)) % 128, 1) for d in range(4)]
                    lined[par, h] = jnp.where(
                        chunk == 0,
                        z[0],
                        jnp.where(chunk == 1, z[1], jnp.where(chunk == 2, z[2], z[3])),
                    )
            for h in range(2):
                a, b = lined[0, h], lined[1, h]
                halves[2 * h].append(jnp.where(sub < 4, a, pltpu.roll(b, 4, 0)))
                halves[2 * h + 1].append(jnp.where(sub < 4, pltpu.roll(a, 4, 0), b))
        for t in range(4):
            sent[t, 16 * pair : 16 * pair + 16, :] = (
                jnp.concatenate(halves[t], axis=0).astype(jnp.int32).astype(I16)
            )
    for n, out in enumerate((out0, out1, out2, out3)):
        out[...] = sent[(tile + n) % TILES]


def finish_kernel(in0, in1, in2, in3, state, land_sea, depth_index, out, got):
    block = lax.axis_index("depth")
    tile = lax.axis_index("tile")
    for n, ref in enumerate((in0, in1, in2, in3)):
        got[(tile + TILES - n) % TILES] = ref[...]
    wet_levels = jnp.where(land_sea[...] == 1, depth_index[...], 0)
    first = block * OWN_LEVELS
    for q in range(4):
        lanes = slice(128 * q, 128 * q + 128)
        values = []
        for pair in range(ENDS // 4):
            x = got[q, 16 * pair : 16 * pair + 16, :].astype(jnp.int32).astype(F32)
            values += [x[0:4], x[4:8], x[8:12], x[12:16]]
        for t in range(2):
            base = t * (OWN_LEVELS + 1)
            unit = jnp.exp2(values[base + OWN_LEVELS]) * (1.0 / CODE)
            for k in range(OWN_LEVELS):
                wet = wet_levels[:, lanes] > first + k
                out[0, t, k, :, lanes] = jnp.where(
                    wet, values[base + k] * unit - state[0, t, k, :, lanes], 0.0
                )


def near(*arrays):
    return [pltpu.with_memory_space_constraint(x, pltpu.VMEM) for x in arrays]


def call(kernel, outs, scratch, *args, reserve=8, place=near):
    return pl.pallas_call(
        kernel,
        out_shape=outs,
        in_specs=[VMEM] * len(args),
        out_specs=jax.tree.map(lambda _: VMEM, outs),
        scratch_shapes=scratch,
        compiler_params=pltpu.CompilerParams(vmem_limit_bytes=reserve << 20),
    )(*place(*args))


def across_depth(messages):
    return [messages[0]] + [
        lax.ppermute(messages[n], "depth", [(i, i ^ n) for i in range(BLOCKS)])
        for n in range(1, BLOCKS)
    ]


def window_shards(initial_states, velocity, growth, land_sea, depth_index, column_ops):
    message = pltpu.VMEM((4 * ENDS, 128), I16)
    slots = pltpu.VMEM((4, 4 * ENDS, 128), I16)
    cells = pltpu.VMEM((2 * 8 * PITCH, 128), F32)
    packed = call(
        pack_kernel,
        [pltpu.VMEM((MAIN + FIELDS, 128), I16)] * TILES,
        [pltpu.VMEM((MAIN, 512), F32)],
        initial_states,
        velocity,
        growth,
        land_sea,
        depth_index,
        reserve=60,
        place=lambda *args: args,
    )
    tiles = {0: packed[0]}
    for distance in (1, 3, 2):
        route = [(i, (i + distance) % TILES) for i in range(TILES)]
        tiles[distance] = lax.ppermute(packed[distance], "tile", route)
    received = []
    for distances in (NEAR, FAR):
        rows = PIECE * len(distances)
        received += across_depth(
            call(
                split_kernel,
                [pltpu.VMEM((rows, 128), I16)] * BLOCKS,
                [pltpu.VMEM((BLOCKS, rows, 128), I16)],
                *[tiles[distance] for distance in distances],
            )
        )
    out = call(
        steps_kernel,
        [message] * 4,
        [
            pltpu.VMEM((TILES * BLOCKS, PIECE, 128), I16),
            cells,
            cells,
            cells,
            cells,
            pltpu.VMEM((PITCH // 8, 8, 9, 8, 128), F32),
            pltpu.VMEM((2, 8, 128), F32),
            pltpu.VMEM((LEVELS, 128), F32),
            slots,
        ],
        *received,
        column_ops,
        reserve=16,
    )
    turned = call(turn_kernel, [message] * 4, [slots] * 2, *across_depth(out))
    segs = lax.axis_size("seg")
    last = [
        lax.ppermute(
            turned[n],
            ("seg", "tile"),
            [
                (s * TILES + t, ((s + 1) % segs) * TILES + (t + n) % TILES)
                for s in range(segs)
                for t in range(TILES)
            ],
        )
        for n in range(4)
    ]
    return call(
        finish_kernel,
        jax.ShapeDtypeStruct(initial_states.shape, F32),
        [slots],
        *last,
        initial_states,
        land_sea,
        depth_index,
    )


def shards(initial_states, velocity, growth, land_sea, depth_index, column_ops):
    fits = (
        lax.axis_size("tile") == TILES
        and lax.axis_size("depth") == BLOCKS
        and initial_states.shape == (1, 2, OWN_LEVELS, 4, TILES * BLOCKS * OWN)
    )
    plan = window_shards if fits else stepwise_shards
    return plan(initial_states, velocity, growth, land_sea, depth_index, column_ops)


def solution(mesh):
    return jax.shard_map(
        shards,
        mesh=mesh,
        in_specs=(
            P("seg", None, "depth", "tile", None),
            P("seg", None, "depth", "tile", None),
            P("seg", "tile", None),
            P("tile", None),
            P("tile", None),
            P(),
        ),
        out_specs=P("seg", None, "depth", "tile", None),
        check_vma=False,
    )
```

```python
import jax
import jax.numpy as jnp
from jax import lax
from jax.experimental import pallas as pl
from jax.experimental.pallas import tpu as pltpu
from jax.sharding import PartitionSpec as P

STEPS = 4


half_sat_sq = 0.25
remin_rate = 0.2


def with_halo(cells, sides, width):
    for axis, dim in sides:
        count = lax.axis_size(axis)
        ends = count - 1
        head = lax.slice_in_dim(cells, 0, width, axis=dim)
        tail = lax.slice_in_dim(cells, cells.shape[dim] - width, cells.shape[dim], axis=dim)
        cells = jnp.concatenate(
            [
                lax.ppermute(tail, axis, [(i, (i + 1) % count) for i in range(ends)]),
                cells,
                lax.ppermute(head, axis, [((i + 1) % count, i) for i in range(ends)]),
            ],
            axis=dim,
        )
    return cells


def passed_along(block, axis, distance):
    devices = range(lax.axis_size(axis))
    route = [((i - distance) % len(devices), i) for i in devices]
    return lax.ppermute(block, axis, route)


def face_flux(behind, near_side, far_side, beyond, courant):
    return (
        courant * (7.0 * (near_side + far_side) - (behind + beyond)) / 12.0
        - jnp.abs(courant) * (3.0 * (far_side - near_side) - (beyond - behind)) / 12.0
    )


def tendency(padded, north_faces, east_faces):
    merid = face_flux(
        padded[..., :-3, :],
        padded[..., 1:-2, :],
        padded[..., 2:-1, :],
        padded[..., 3:, :],
        north_faces,
    )
    centre = padded[..., 2:-2, :]
    zonal_flux = face_flux(
        jnp.roll(centre, 1, axis=-1),
        centre,
        jnp.roll(centre, -1, axis=-1),
        jnp.roll(centre, -2, axis=-1),
        east_faces,
    )
    return merid[..., :-1, :] - merid[..., 1:, :] + (jnp.roll(zonal_flux, 1, axis=-1) - zonal_flux)


def biology(mixed, rate, light_level, wet_cells):
    phosphate = mixed[..., 0, :, :, :]
    particles = mixed[..., 1, :, :, :]
    uptake = (
        rate
        * light_level
        * phosphate
        * phosphate
        * phosphate
        / (phosphate * phosphate + half_sat_sq)
    )
    return jnp.stack(
        [
            wet_cells * (phosphate - uptake + remin_rate * particles),
            wet_cells * (particles + uptake - remin_rate * particles),
        ],
        axis=-4,
    )


def stepwise_shards(initial_states, velocity, growth, land_sea, depth_index, column_ops):
    seg_dev = initial_states.shape[0]
    lev_dev = initial_states.shape[2]
    first_level = lax.axis_index("depth") * lev_dev
    levels = first_level + lax.iota(jnp.int32, lev_dev)
    wet_cells = jnp.where(
        (land_sea[None] == 1) & (levels[:, None, None] < depth_index[None]), 1.0, 0.0
    ).astype(jnp.float32)
    light_level = jnp.exp(-4.0 * levels.astype(jnp.float32) / column_ops.shape[1])[:, None, None]
    own_rows = lax.dynamic_slice_in_dim(column_ops, first_level, lev_dev, 1)
    uptake_rate = growth[:, None]
    tracer_state = wet_cells * initial_states
    flow_stack = jnp.concatenate([velocity[:, 0], velocity[:, 1], wet_cells[None]], axis=0)
    flow_edges = with_halo(flow_stack, (("tile", 2),), 3)
    wet_edges = flow_edges[2 * seg_dev]
    north_wide = (flow_edges[seg_dev : 2 * seg_dev, :, :-1] * wet_edges[:, :-1] * wet_edges[:, 1:])[
        :, None
    ]
    wet_wide = wet_edges[:, 1:-1]
    east_wide = (flow_edges[:seg_dev, :, 1:-1] * wet_wide * jnp.roll(wet_wide, -1, axis=-1))[
        :, None
    ]
    north_faces = north_wide[:, :, :, 2:-2]
    east_faces = east_wide[:, :, :, 2:-2]
    for step_index in range(STEPS):
        padded = with_halo(tracer_state, (("tile", 3),), 4)
        first_section = wet_wide * (padded[:, :, :, 2:-2] + tendency(padded, north_wide, east_wide))
        advected = wet_cells * (
            0.5 * tracer_state
            + 0.5
            * (first_section[:, :, :, 2:-2] + tendency(first_section, north_faces, east_faces))
        )
        rounded = advected.astype(jnp.bfloat16)
        mixed = jnp.einsum(
            "tkm,stmrl->stkrl",
            own_rows,
            lax.all_gather(rounded, "depth", axis=2, tiled=True),
            preferred_element_type=jnp.float32,
        )
        tracer_state = biology(wet_cells * mixed, uptake_rate, light_level, wet_cells)
    previous = passed_along(tracer_state, "seg", 1)
    before = jnp.concatenate([previous, tracer_state[: seg_dev - 1]], axis=0)
    return wet_cells * (before - initial_states)


TILES = 4
BLOCKS = 4
LEVELS = 76
OWN_LEVELS = LEVELS // BLOCKS
PITCH = 80
OWN = 32
REACH = 4 * STEPS
WINDOW = OWN + 2 * REACH
CODE = 32000.0
FASTEST = 0.35
FIELDS = 4 * OWN_LEVELS + 4
ENDS = 2 * OWN_LEVELS + 2
PIECE = 2 * FIELDS
MAIN = 4 * FIELDS
BOTH = PIECE + FIELDS
CORES = 2

F32 = jnp.float32
I16 = jnp.int16
VMEM = pl.BlockSpec(memory_space=pltpu.VMEM)


def coded(values):
    return jnp.floor(values + 0.5).astype(jnp.int32).astype(I16)


def exponent(largest):
    return jnp.clip(jnp.ceil(jnp.log2(jnp.maximum(largest, 1e-36))), -119.0, 125.0)


def index(shape, dim):
    return lax.broadcasted_iota(jnp.int32, shape, dim)


def pack_kernel(state, velocity, growth, land_sea, depth_index, *refs):
    (out, *outs), (turned, sent) = refs[:-2], refs[-2:]
    scales = []
    for t in range(2):
        largest = jnp.abs(state[0, t, 0])
        for k in range(1, OWN_LEVELS):
            largest = jnp.maximum(largest, jnp.abs(state[0, t, k]))
        scales.append(exponent(largest))
    per_unit = [CODE * jnp.exp2(-e) for e in scales]
    wet_levels = jnp.where(land_sea[...] == 1, depth_index[...], 0).astype(F32)

    def field(n):
        which, k = divmod(n, OWN_LEVELS)
        if which < 2:
            return state[0, which, k] * per_unit[which]
        if which < 4:
            return velocity[0, which - 2, k] * (CODE / FASTEST)
        return [growth[0] * CODE, wet_levels, scales[0], scales[1]][k]

    for pair in range(FIELDS // 2):
        rows = jnp.concatenate([field(2 * pair), field(2 * pair + 1)], axis=0)
        turned[8 * pair : 8 * pair + 8, :] = pltpu.roll(rows, REACH, 1)
    half = lax.axis_index("depth") // CORES

    def part_of(side):
        def part(lanes, row, count):
            at = pl.ds(pl.multiple_of(128 * ((2 * side + lanes) % 4), 128), 128)
            return turned[row : row + count, at]

        return part

    other = part_of(1 - half)
    for lanes in range(2):
        for row in range(0, MAIN, 16):
            out[MAIN * lanes + row : MAIN * lanes + row + 16, :] = coded(other(lanes, row, 16))
    for pair in range(FIELDS // 16):
        row = 2 * MAIN + 16 * pair
        out[row : row + 16, :] = coded(tails(other, TILES - 1, pair))
    windows(part_of(half), coded, None, sent, outs)


def tails(part, t, pair):
    chunk = index((8, 128), 1) // 32
    lanes, first = (t + 1) // 2, 2 * ((t + 1) % 2)
    blocks = []
    for group in (2 * pair, 2 * pair + 1):
        late = group + FIELDS // 8
        rows = (2 * late, 2 * group, 2 * late + 1, 2 * group + 1)
        blocks.append(
            by_chunk(chunk, [turn(part(lanes, 8 * i, 8), n - first) for n, i in enumerate(rows)])
        )
    return jnp.concatenate(blocks, axis=0)


def turn(block, chunks):
    return pltpu.roll(block, (32 * chunks) % 128, 1) if chunks % 4 else block


def windows(part, packed, last, sent, outs):
    left = index((8, 128), 1) < 64
    for t in range(TILES):
        for pair in range(FIELDS // 8):
            blocks = []
            for group in (2 * pair, 2 * pair + 1):
                lo, hi = (part(t // 2, 8 * i, 8) for i in (2 * group, 2 * group + 1))
                lo, hi = turn(lo, 2 * (t % 2)), turn(hi, 2 - 2 * (t % 2))
                blocks.append(jnp.where(left, lo, hi))
            sent[t, 16 * pair : 16 * pair + 16, :] = packed(jnp.concatenate(blocks, axis=0))
        for pair in range(FIELDS // 16):
            row = PIECE + 16 * pair
            if t == TILES - 1 and last is not None:
                sent[t, row : row + 16, :] = last(pair)
            else:
                sent[t, row : row + 16, :] = packed(tails(part, t, pair))
    tile = lax.axis_index("tile")
    for n, out in enumerate(outs):
        out[...] = sent[(tile + n) % TILES]


def relay_kernel(ref, *refs):
    outs, sent = refs[:-1], refs[-1]

    def part(lanes, row, count):
        base = MAIN * lanes + row // 16 * 16
        skip = row % 16
        return wide(ref[base : base + 16, :])[skip : skip + count]

    def last(pair):
        row = 2 * MAIN + 16 * pair
        return ref[row : row + 16, :]

    windows(part, narrow, last, sent, outs)


def piece(ref, pair, core):
    main = wide(ref[16 * pair : 16 * pair + 16, :])
    row = PIECE + 16 * (pair % (FIELDS // 16))
    tail = wide(ref[row : row + 16, :])
    odd = index((16, 128), 1) // 32 % 2 == 1
    if pair < FIELDS // 16:
        second = jnp.where(odd, tail, turn(main, 3))
    else:
        second = jnp.where(odd, turn(tail, 1), turn(main, 3))
    return narrow(jnp.where(core == 0, main, second))


def core_kernel(*refs):
    sources, out = refs[:-1], refs[-1]
    core = lax.axis_index("depth") % CORES
    for i, ref in enumerate(sources):
        for pair in range(FIELDS // 8):
            row = PIECE * i + 16 * pair
            out[row : row + 16, :] = piece(ref, pair, 1 - core)


def by_chunk(chunk, values):
    return jnp.where(
        chunk == 0,
        values[0],
        jnp.where(chunk == 1, values[1], jnp.where(chunk == 2, values[2], values[3])),
    )


def wide(values):
    return values.astype(jnp.int32).astype(F32)


def narrow(values):
    return values.astype(jnp.int32).astype(I16)


def steps_kernel(*refs):
    arrived, (ops, out0, out1, out2, out3, recv), scratch = refs[:9], refs[9:15], refs[15:]
    cells, firsts, moved, flow, coef, plane, light, ends = scratch
    own = lax.axis_index("depth")
    tile = lax.axis_index("tile")
    core, half = own % CORES, own // CORES
    for i in range(2 * TILES):
        far, distance = divmod(i, TILES)
        at = 4 * ((tile + TILES - distance) % TILES) + CORES * (half ^ far)
        for pair in range(FIELDS // 8):
            recv[at + core, 16 * pair : 16 * pair + 16, :] = piece(arrived[i], pair, core)
        recv[at + 1 - core] = arrived[2 * TILES][PIECE * i : PIECE * i + PIECE, :]
    sub = index((8, 128), 0)
    lane = index((8, 128), 1)
    left = lane < 64

    def spread(d, pair):
        sent = [
            recv[4 * t + d, 16 * pair : 16 * pair + 16, :].astype(jnp.int32).astype(F32)
            for t in range(4)
        ]
        fields = []
        for part in range(2):
            m = [x[8 * part : 8 * part + 8] for x in sent]
            up, across = {}, {}
            for h in range(2):
                a, b = m[2 * h], m[2 * h + 1]
                up[0, h] = jnp.where(sub < 4, a, pltpu.roll(b, 4, 0))
                up[1, h] = jnp.where(sub < 4, pltpu.roll(a, 4, 0), b)
            for p in range(2):
                a, b = up[p, 0], up[p, 1]
                across[p, 0] = jnp.where(left, a, pltpu.roll(b, 64, 1))
                across[p, 1] = jnp.where(left, pltpu.roll(a, 64, 1), b)
            fields += [across[0, 0], across[1, 0], across[0, 1], across[1, 1]]
        return fields

    def take(d, carry):
        last = spread(d, FIELDS // 8 - 1)
        plane[0] = last[4] * (1.0 / CODE)
        plane[1] = last[5]
        unit = [jnp.exp2(last[6 + t]) * (1.0 / CODE) for t in range(2)]
        for pair in range(FIELDS // 8):
            fields = last if pair == FIELDS // 8 - 1 else spread(d, pair)
            for i, value in enumerate(fields):
                which, k = divmod(8 * pair + i, OWN_LEVELS)
                if which < 2:
                    cells[pl.ds(which * 8 * PITCH + OWN_LEVELS * d + k, 8, stride=PITCH), :] = (
                        value * unit[which]
                    )
                elif which < 4:
                    at = pl.ds((which - 2) * 8 * PITCH + OWN_LEVELS * d + k, 8, stride=PITCH)
                    flow[at, :] = value * (FASTEST / CODE)
        return carry

    lax.fori_loop(0, BLOCKS, take, 0)

    for field in (cells, flow):
        for s in range(16):
            field[s * PITCH + LEVELS : (s + 1) * PITCH, :] = jnp.zeros((PITCH - LEVELS, 128), F32)

    def block(base, g):
        return pl.ds(pl.multiple_of(base * PITCH + 8 * g, 8), 8)

    def faces(w):
        size = jnp.abs(w)
        return (
            (-w - size) * (1.0 / 12.0),
            (7.0 * w + 3.0 * size) * (1.0 / 12.0),
            (7.0 * w - 3.0 * size) * (1.0 / 12.0),
            (size - w) * (1.0 / 12.0),
        )

    def prepare(g, carry):
        level = (sub + 8 * g).astype(F32)
        wet = [jnp.where(plane[1, s : s + 1, :] > level, 1.0, 0.0) for s in range(8)]
        for t in range(2):
            for s in range(8):
                at = block(8 * t + s, g)
                cells[at, :] = wet[s] * cells[at, :]
        beyond = jnp.where(left, pltpu.roll(wet[0], 64, 1), 0.0)
        north_w = [
            flow[block(8 + s, g), :] * wet[s] * (wet[s + 1] if s < 7 else beyond) for s in range(8)
        ]
        first = jnp.where(left, 0.0, pltpu.roll(north_w[7], 64, 1))
        merid = [faces(w) for w in [first] + north_w]
        for s in range(8):
            east_w = flow[block(s, g), :] * wet[s] * pltpu.roll(wet[s], 127, 1)
            a, b, d, e = faces(east_w)
            a1, b1, d1, e1 = faces(pltpu.roll(east_w, 1, 1))
            p1, q1, r1, s1 = merid[s]
            p, q, r, s0 = merid[s + 1]
            south = [wet[s] * p1, wet[s] * (q1 - p)]
            north = [wet[s] * (s1 - r), -wet[s] * s0]
            if s < 2:
                south[0] = jnp.where(left, 0.0, south[0])
            if s < 1:
                south[1] = jnp.where(left, 0.0, south[1])
            if s > 6:
                north[0] = jnp.where(left, north[0], 0.0)
            if s > 5:
                north[1] = jnp.where(left, north[1], 0.0)
            coef[g, s, 0] = wet[s] * (1.0 + (d1 - b) + (r1 - q))
            coef[g, s, 1] = wet[s] * a1
            coef[g, s, 2] = wet[s] * (b1 - a)
            coef[g, s, 3] = wet[s] * (e1 - d)
            coef[g, s, 4] = -wet[s] * e
            coef[g, s, 5], coef[g, s, 6] = south
            coef[g, s, 7], coef[g, s, 8] = north
        return carry

    lax.fori_loop(0, PITCH // 8, prepare, 0, unroll=5)

    deep = index((LEVELS, 128), 0)
    light[...] = jnp.exp(deep.astype(F32) * (-4.0 / LEVELS))

    def combine(c, near, far):
        centre = near[1]
        return (
            (c[0] * centre + c[6] * near[0] + c[7] * near[2])
            + (c[5] * far[0] + c[8] * far[1])
            + (c[2] * pltpu.roll(centre, 1, 1) + c[3] * pltpu.roll(centre, 127, 1))
            + (c[1] * pltpu.roll(centre, 2, 1) + c[4] * pltpu.roll(centre, 126, 1))
        )

    def stage(source, g, emit):
        def at(t, s):
            return source[block(8 * t + s, g), :]

        columns = []
        for t in range(2):
            inner = [at(t, s) for s in range(8)]
            turned = [pltpu.roll(inner[s], 64, 1) for s in (6, 7, 0, 1)]
            columns.append(turned[:2] + inner + turned[2:])
        for s in range(8):
            c = [coef[g, s, i] for i in range(9)]
            for t in range(2):
                k = columns[t]
                emit(t, s, combine(c, k[s + 1 : s + 4], (k[s], k[s + 4])))

    def first_stage(g, carry):
        def emit(t, s, value):
            firsts[block(8 * t + s, g), :] = value

        stage(cells, g, emit)
        return carry

    def second_stage(g, carry):
        def emit(t, s, value):
            at = block(8 * t + s, g)
            moved[at, :] = 0.5 * (cells[at, :] + value)

        stage(firsts, g, emit)
        return carry

    def step(n, carry):
        lax.fori_loop(0, PITCH // 8, first_stage, 0, unroll=True)
        lax.fori_loop(0, PITCH // 8, second_stage, 0, unroll=True)
        for pair in range(4):
            mixed = []
            for t in range(2):
                base = (t * 8 + 2 * pair) * PITCH
                both = jnp.concatenate(
                    [moved[base : base + LEVELS, :], moved[base + PITCH : base + PITCH + LEVELS, :]],
                    axis=1,
                ).astype(jnp.bfloat16)
                mixed.append(jnp.dot(ops[t], both, preferred_element_type=F32))
            for i in range(2):
                s = 2 * pair + i
                wet = deep.astype(F32) < plane[1, s : s + 1, :]
                p = jnp.where(wet, mixed[0][:, 128 * i : 128 * i + 128], 0.0)
                q = jnp.where(wet, mixed[1][:, 128 * i : 128 * i + 128], 0.0)
                square = p * p
                uptake = (plane[0, s : s + 1, :] * light[...]) * (
                    square * p / (square + half_sat_sq)
                )
                gain = uptake - remin_rate * q
                cells[s * PITCH : s * PITCH + LEVELS, :] = p - gain
                cells[(8 + s) * PITCH : (8 + s) * PITCH + LEVELS, :] = q + gain
        return carry

    lax.fori_loop(0, STEPS, step, 0)

    chunk = lane // 32

    def send(n, carry):
        to = own ^ n
        blocks = []
        for t in range(2):
            def level(k):
                return cells[pl.ds(t * 8 * PITCH + OWN_LEVELS * to + k, 8, stride=PITCH), :]

            largest = jnp.abs(level(0))
            for k in range(1, OWN_LEVELS):
                largest = jnp.maximum(largest, jnp.abs(level(k)))
            scale = exponent(largest)
            per_unit = CODE * jnp.exp2(-scale)
            blocks += [level(k) * per_unit for k in range(OWN_LEVELS)] + [scale]
        for pair in range(ENDS // 4):
            halves = []
            for i in (2 * pair, 2 * pair + 1):
                a, b = blocks[2 * i], blocks[2 * i + 1]
                halves.append(
                    jnp.where(
                        chunk == 0,
                        pltpu.roll(a, 112, 1),
                        jnp.where(
                            chunk == 1,
                            pltpu.roll(a, 80, 1),
                            jnp.where(chunk == 2, pltpu.roll(b, 48, 1), pltpu.roll(b, 16, 1)),
                        ),
                    )
                )
            ends[n, 16 * pair : 16 * pair + 16, :] = coded(jnp.concatenate(halves, axis=0))
        return carry

    lax.fori_loop(0, BLOCKS, send, 0)
    for n, out in enumerate((out0, out1, out2, out3)):
        out[...] = ends[n]


def turn_kernel(in0, in1, in2, in3, out0, out1, out2, out3, got, sent):
    block = lax.axis_index("depth")
    tile = lax.axis_index("tile")
    for n, ref in enumerate((in0, in1, in2, in3)):
        got[block ^ n] = ref[...]
    sub = index((8, 128), 0)
    chunk = index((8, 128), 1) // 32
    for pair in range(ENDS // 4):
        whole = [
            got[d, 16 * pair : 16 * pair + 16, :].astype(jnp.int32).astype(F32) for d in range(4)
        ]
        halves = {t: [] for t in range(4)}
        for part in range(2):
            m = [x[8 * part : 8 * part + 8] for x in whole]
            lined = {}
            for par in range(2):
                for h in range(2):
                    z = [pltpu.roll(m[d], (32 * (d - 2 * par - h)) % 128, 1) for d in range(4)]
                    lined[par, h] = jnp.where(
                        chunk == 0,
                        z[0],
                        jnp.where(chunk == 1, z[1], jnp.where(chunk == 2, z[2], z[3])),
                    )
            for h in range(2):
                a, b = lined[0, h], lined[1, h]
                halves[2 * h].append(jnp.where(sub < 4, a, pltpu.roll(b, 4, 0)))
                halves[2 * h + 1].append(jnp.where(sub < 4, pltpu.roll(a, 4, 0), b))
        for t in range(4):
            sent[t, 16 * pair : 16 * pair + 16, :] = (
                jnp.concatenate(halves[t], axis=0).astype(jnp.int32).astype(I16)
            )
    for n, out in enumerate((out0, out1, out2, out3)):
        out[...] = sent[(tile + n) % TILES]


def finish_kernel(in0, in1, in2, in3, state, land_sea, depth_index, out, got):
    block = lax.axis_index("depth")
    tile = lax.axis_index("tile")
    for n, ref in enumerate((in0, in1, in2, in3)):
        got[(tile + TILES - n) % TILES] = ref[...]
    wet_levels = jnp.where(land_sea[...] == 1, depth_index[...], 0)
    first = block * OWN_LEVELS
    left = index((16, 128), 1) < 64
    for q in range(4):
        half, west = divmod(q, 2)
        lanes = slice(128 * q, 128 * q + 128)
        values = []
        for pair in range(ENDS // 4):
            x, y = (wide(got[2 * west + i, 16 * pair : 16 * pair + 16, :]) for i in range(2))
            x = jnp.where(left, turn(x, 2 * half), turn(y, 2 - 2 * half))
            values += [x[0:4], x[4:8], x[8:12], x[12:16]]
        for t in range(2):
            base = t * (OWN_LEVELS + 1)
            unit = jnp.exp2(values[base + OWN_LEVELS]) * (1.0 / CODE)
            for k in range(OWN_LEVELS):
                wet = wet_levels[:, lanes] > first + k
                out[0, t, k, :, lanes] = jnp.where(
                    wet, values[base + k] * unit - state[0, t, k, :, lanes], 0.0
                )


def near(*arrays):
    return [pltpu.with_memory_space_constraint(x, pltpu.VMEM) for x in arrays]


def call(kernel, outs, scratch, *args, reserve=8, place=near):
    return pl.pallas_call(
        kernel,
        out_shape=outs,
        in_specs=[VMEM] * len(args),
        out_specs=jax.tree.map(lambda _: VMEM, outs),
        scratch_shapes=scratch,
        compiler_params=pltpu.CompilerParams(vmem_limit_bytes=reserve << 20),
    )(*place(*args))


def across_depth(messages):
    return [messages[0]] + [
        lax.ppermute(messages[n], "depth", [(i, i ^ n) for i in range(BLOCKS)])
        for n in range(1, BLOCKS)
    ]


def across_tiles(messages):
    return [messages[0]] + [
        lax.ppermute(messages[n], "tile", [(i, (i + n) % TILES) for i in range(TILES)])
        for n in range(1, TILES)
    ]


def window_shards(initial_states, velocity, growth, land_sea, depth_index, column_ops):
    message = pltpu.VMEM((4 * ENDS, 128), I16)
    slots = pltpu.VMEM((4, 4 * ENDS, 128), I16)
    cells = pltpu.VMEM((2 * 8 * PITCH, 128), F32)
    both = pltpu.VMEM((BOTH, 128), I16)
    sent = pltpu.VMEM((TILES, BOTH, 128), I16)
    across, *here = call(
        pack_kernel,
        [pltpu.VMEM((2 * MAIN + FIELDS, 128), I16)] + [both] * TILES,
        [pltpu.VMEM((MAIN, 512), F32), sent],
        initial_states,
        velocity,
        growth,
        land_sea,
        depth_index,
        reserve=60,
        place=lambda *args: args,
    )
    across = lax.ppermute(across, "depth", [(i, i ^ CORES) for i in range(BLOCKS)])
    received = across_tiles(here)
    received += across_tiles(call(relay_kernel, [both] * TILES, [sent], across))
    others = call(core_kernel, pltpu.VMEM((2 * TILES * PIECE, 128), I16), [], *received)
    received.append(lax.ppermute(others, "depth", [(i, i ^ 1) for i in range(BLOCKS)]))
    out = call(
        steps_kernel,
        [message] * 4,
        [
            pltpu.VMEM((TILES * BLOCKS, PIECE, 128), I16),
            cells,
            cells,
            cells,
            cells,
            pltpu.VMEM((PITCH // 8, 8, 9, 8, 128), F32),
            pltpu.VMEM((2, 8, 128), F32),
            pltpu.VMEM((LEVELS, 128), F32),
            slots,
        ],
        *received,
        column_ops,
        reserve=16,
    )
    turned = call(turn_kernel, [message] * 4, [slots] * 2, *across_depth(out))
    segs = lax.axis_size("seg")
    last = [
        lax.ppermute(
            turned[n],
            ("seg", "tile"),
            [
                (s * TILES + t, ((s + 1) % segs) * TILES + (t + n) % TILES)
                for s in range(segs)
                for t in range(TILES)
            ],
        )
        for n in range(4)
    ]
    return call(
        finish_kernel,
        jax.ShapeDtypeStruct(initial_states.shape, F32),
        [slots],
        *last,
        initial_states,
        land_sea,
        depth_index,
    )


def shards(initial_states, velocity, growth, land_sea, depth_index, column_ops):
    fits = (
        lax.axis_size("tile") == TILES
        and lax.axis_size("depth") == BLOCKS
        and initial_states.shape == (1, 2, OWN_LEVELS, 4, TILES * BLOCKS * OWN)
    )
    plan = window_shards if fits else stepwise_shards
    return plan(initial_states, velocity, growth, land_sea, depth_index, column_ops)


def solution(mesh):
    return jax.shard_map(
        shards,
        mesh=mesh,
        in_specs=(
            P("seg", None, "depth", "tile", None),
            P("seg", None, "depth", "tile", None),
            P("seg", "tile", None),
            P("tile", None),
            P("tile", None),
            P(),
        ),
        out_specs=P("seg", None, "depth", "tile", None),
        check_vma=False,
    )
```

```python
import jax
import jax.numpy as jnp
from jax import lax
from jax.experimental import pallas as pl
from jax.experimental.pallas import tpu as pltpu
from jax.sharding import PartitionSpec as P

STEPS = 4


half_sat_sq = 0.25
remin_rate = 0.2


def with_halo(cells, sides, width):
    for axis, dim in sides:
        count = lax.axis_size(axis)
        ends = count - 1
        head = lax.slice_in_dim(cells, 0, width, axis=dim)
        tail = lax.slice_in_dim(cells, cells.shape[dim] - width, cells.shape[dim], axis=dim)
        cells = jnp.concatenate(
            [
                lax.ppermute(tail, axis, [(i, (i + 1) % count) for i in range(ends)]),
                cells,
                lax.ppermute(head, axis, [((i + 1) % count, i) for i in range(ends)]),
            ],
            axis=dim,
        )
    return cells


def passed_along(block, axis, distance):
    devices = range(lax.axis_size(axis))
    route = [((i - distance) % len(devices), i) for i in devices]
    return lax.ppermute(block, axis, route)


def face_flux(behind, near_side, far_side, beyond, courant):
    return (
        courant * (7.0 * (near_side + far_side) - (behind + beyond)) / 12.0
        - jnp.abs(courant) * (3.0 * (far_side - near_side) - (beyond - behind)) / 12.0
    )


def tendency(padded, north_faces, east_faces):
    merid = face_flux(
        padded[..., :-3, :],
        padded[..., 1:-2, :],
        padded[..., 2:-1, :],
        padded[..., 3:, :],
        north_faces,
    )
    centre = padded[..., 2:-2, :]
    zonal_flux = face_flux(
        jnp.roll(centre, 1, axis=-1),
        centre,
        jnp.roll(centre, -1, axis=-1),
        jnp.roll(centre, -2, axis=-1),
        east_faces,
    )
    return merid[..., :-1, :] - merid[..., 1:, :] + (jnp.roll(zonal_flux, 1, axis=-1) - zonal_flux)


def biology(mixed, rate, light_level, wet_cells):
    phosphate = mixed[..., 0, :, :, :]
    particles = mixed[..., 1, :, :, :]
    uptake = (
        rate
        * light_level
        * phosphate
        * phosphate
        * phosphate
        / (phosphate * phosphate + half_sat_sq)
    )
    return jnp.stack(
        [
            wet_cells * (phosphate - uptake + remin_rate * particles),
            wet_cells * (particles + uptake - remin_rate * particles),
        ],
        axis=-4,
    )


def stepwise_shards(initial_states, velocity, growth, land_sea, depth_index, column_ops):
    seg_dev = initial_states.shape[0]
    lev_dev = initial_states.shape[2]
    first_level = lax.axis_index("depth") * lev_dev
    levels = first_level + lax.iota(jnp.int32, lev_dev)
    wet_cells = jnp.where(
        (land_sea[None] == 1) & (levels[:, None, None] < depth_index[None]), 1.0, 0.0
    ).astype(jnp.float32)
    light_level = jnp.exp(-4.0 * levels.astype(jnp.float32) / column_ops.shape[1])[:, None, None]
    own_rows = lax.dynamic_slice_in_dim(column_ops, first_level, lev_dev, 1)
    uptake_rate = growth[:, None]
    tracer_state = wet_cells * initial_states
    flow_stack = jnp.concatenate([velocity[:, 0], velocity[:, 1], wet_cells[None]], axis=0)
    flow_edges = with_halo(flow_stack, (("tile", 2),), 3)
    wet_edges = flow_edges[2 * seg_dev]
    north_wide = (flow_edges[seg_dev : 2 * seg_dev, :, :-1] * wet_edges[:, :-1] * wet_edges[:, 1:])[
        :, None
    ]
    wet_wide = wet_edges[:, 1:-1]
    east_wide = (flow_edges[:seg_dev, :, 1:-1] * wet_wide * jnp.roll(wet_wide, -1, axis=-1))[
        :, None
    ]
    north_faces = north_wide[:, :, :, 2:-2]
    east_faces = east_wide[:, :, :, 2:-2]
    for step_index in range(STEPS):
        padded = with_halo(tracer_state, (("tile", 3),), 4)
        first_section = wet_wide * (padded[:, :, :, 2:-2] + tendency(padded, north_wide, east_wide))
        advected = wet_cells * (
            0.5 * tracer_state
            + 0.5
            * (first_section[:, :, :, 2:-2] + tendency(first_section, north_faces, east_faces))
        )
        rounded = advected.astype(jnp.bfloat16)
        mixed = jnp.einsum(
            "tkm,stmrl->stkrl",
            own_rows,
            lax.all_gather(rounded, "depth", axis=2, tiled=True),
            preferred_element_type=jnp.float32,
        )
        tracer_state = biology(wet_cells * mixed, uptake_rate, light_level, wet_cells)
    previous = passed_along(tracer_state, "seg", 1)
    before = jnp.concatenate([previous, tracer_state[: seg_dev - 1]], axis=0)
    return wet_cells * (before - initial_states)


TILES = 4
BLOCKS = 4
LEVELS = 76
OWN_LEVELS = LEVELS // BLOCKS
PITCH = 80
HALF = PITCH // 2
OWN = 32
REACH = 4 * STEPS
WINDOW = OWN + 2 * REACH
CODE = 32000.0
FASTEST = 0.35
FIELDS = 4 * OWN_LEVELS + 4
ENDS = 2 * OWN_LEVELS + 2
PIECE = 2 * FIELDS
MAIN = 4 * FIELDS
BOTH = PIECE + FIELDS
CORES = 2

F32 = jnp.float32
I16 = jnp.int16
VMEM = pl.BlockSpec(memory_space=pltpu.VMEM)


def coded(values):
    return jnp.floor(values + 0.5).astype(jnp.int32).astype(I16)


def exponent(largest):
    return jnp.clip(jnp.ceil(jnp.log2(jnp.maximum(largest, 1e-36))), -119.0, 125.0)


def index(shape, dim):
    return lax.broadcasted_iota(jnp.int32, shape, dim)


def pack_kernel(state, velocity, growth, land_sea, depth_index, *refs):
    (out, *outs), (turned, sent) = refs[:-2], refs[-2:]
    scales = []
    for t in range(2):
        largest = jnp.abs(state[0, t, 0])
        for k in range(1, OWN_LEVELS):
            largest = jnp.maximum(largest, jnp.abs(state[0, t, k]))
        scales.append(exponent(largest))
    per_unit = [CODE * jnp.exp2(-e) for e in scales]
    wet_levels = jnp.where(land_sea[...] == 1, depth_index[...], 0).astype(F32)

    def field(n):
        which, k = divmod(n, OWN_LEVELS)
        if which < 2:
            return state[0, which, k] * per_unit[which]
        if which < 4:
            return velocity[0, which - 2, k] * (CODE / FASTEST)
        return [growth[0] * CODE, wet_levels, scales[0], scales[1]][k]

    for pair in range(FIELDS // 2):
        rows = jnp.concatenate([field(2 * pair), field(2 * pair + 1)], axis=0)
        turned[8 * pair : 8 * pair + 8, :] = pltpu.roll(rows, REACH, 1)
    half = lax.axis_index("depth") // CORES

    def part_of(side):
        def part(lanes, row, count):
            at = pl.ds(pl.multiple_of(128 * ((2 * side + lanes) % 4), 128), 128)
            return turned[row : row + count, at]

        return part

    other = part_of(1 - half)
    for lanes in range(2):
        for row in range(0, MAIN, 16):
            out[MAIN * lanes + row : MAIN * lanes + row + 16, :] = coded(other(lanes, row, 16))
    for pair in range(FIELDS // 16):
        row = 2 * MAIN + 16 * pair
        out[row : row + 16, :] = coded(tails(other, TILES - 1, pair))
    windows(part_of(half), coded, None, sent, outs)


def tails(part, t, pair):
    chunk = index((8, 128), 1) // 32
    lanes, first = (t + 1) // 2, 2 * ((t + 1) % 2)
    blocks = []
    for group in (2 * pair, 2 * pair + 1):
        late = group + FIELDS // 8
        rows = (2 * late, 2 * group, 2 * late + 1, 2 * group + 1)
        blocks.append(
            by_chunk(chunk, [turn(part(lanes, 8 * i, 8), n - first) for n, i in enumerate(rows)])
        )
    return jnp.concatenate(blocks, axis=0)


def turn(block, chunks):
    return pltpu.roll(block, (32 * chunks) % 128, 1) if chunks % 4 else block


def windows(part, packed, last, sent, outs):
    left = index((8, 128), 1) < 64
    for t in range(TILES):
        for pair in range(FIELDS // 8):
            blocks = []
            for group in (2 * pair, 2 * pair + 1):
                lo, hi = (part(t // 2, 8 * i, 8) for i in (2 * group, 2 * group + 1))
                lo, hi = turn(lo, 2 * (t % 2)), turn(hi, 2 - 2 * (t % 2))
                blocks.append(jnp.where(left, lo, hi))
            sent[t, 16 * pair : 16 * pair + 16, :] = packed(jnp.concatenate(blocks, axis=0))
        for pair in range(FIELDS // 16):
            row = PIECE + 16 * pair
            if t == TILES - 1 and last is not None:
                sent[t, row : row + 16, :] = last(pair)
            else:
                sent[t, row : row + 16, :] = packed(tails(part, t, pair))
    tile = lax.axis_index("tile")
    for n, out in enumerate(outs):
        out[...] = sent[(tile + n) % TILES]


def relay_kernel(ref, *refs):
    outs, sent = refs[:-1], refs[-1]

    def part(lanes, row, count):
        base = MAIN * lanes + row // 16 * 16
        skip = row % 16
        return wide(ref[base : base + 16, :])[skip : skip + count]

    def last(pair):
        row = 2 * MAIN + 16 * pair
        return ref[row : row + 16, :]

    windows(part, narrow, last, sent, outs)


def piece(ref, pair, core):
    main = wide(ref[16 * pair : 16 * pair + 16, :])
    row = PIECE + 16 * (pair % (FIELDS // 16))
    tail = wide(ref[row : row + 16, :])
    odd = index((16, 128), 1) // 32 % 2 == 1
    if pair < FIELDS // 16:
        second = jnp.where(odd, tail, turn(main, 3))
    else:
        second = jnp.where(odd, turn(tail, 1), turn(main, 3))
    return narrow(jnp.where(core == 0, main, second))


def core_kernel(*refs):
    sources, out = refs[:-1], refs[-1]
    core = lax.axis_index("depth") % CORES
    for i, ref in enumerate(sources):
        for pair in range(FIELDS // 8):
            row = PIECE * i + 16 * pair
            out[row : row + 16, :] = piece(ref, pair, 1 - core)


def by_chunk(chunk, values):
    return jnp.where(
        chunk == 0,
        values[0],
        jnp.where(chunk == 1, values[1], jnp.where(chunk == 2, values[2], values[3])),
    )


def wide(values):
    return values.astype(jnp.int32).astype(F32)


def narrow(values):
    return values.astype(jnp.int32).astype(I16)


def levels_of(row, core):
    level = row + OWN_LEVELS * core + jnp.where(row >= OWN_LEVELS, OWN_LEVELS, 0)
    return jnp.where(row < 2 * OWN_LEVELS, level, 4 * LEVELS)


def level_rows(shape, core):
    row = index(shape, 0)
    return jnp.where(
        row < HALF, levels_of(row, core), levels_of(row - HALF, 1 - core)
    )


def load_half(recv, side, cells, pitch, base, flow, coef, plane, fresh):
    sub = index((8, 128), 0)
    left = index((8, 128), 1) < 64
    cells_at, flow_at = (pitch, base), (HALF, 0)

    def spread(x, pair):
        sent = [wide(recv[2 * t + x, 16 * pair : 16 * pair + 16, :]) for t in range(TILES)]
        fields = []
        for part in range(2):
            m = [y[8 * part : 8 * part + 8] for y in sent]
            up, across = {}, {}
            for h in range(2):
                a, b = m[2 * h], m[2 * h + 1]
                up[0, h] = jnp.where(sub < 4, a, pltpu.roll(b, 4, 0))
                up[1, h] = jnp.where(sub < 4, pltpu.roll(a, 4, 0), b)
            for p in range(2):
                a, b = up[p, 0], up[p, 1]
                across[p, 0] = jnp.where(left, a, pltpu.roll(b, 64, 1))
                across[p, 1] = jnp.where(left, pltpu.roll(a, 64, 1), b)
            fields += [across[0, 0], across[1, 0], across[0, 1], across[1, 1]]
        return fields

    def take(x, carry):
        last = spread(x, FIELDS // 8 - 1)
        if fresh:
            plane[0] = last[4] * (1.0 / CODE)
            plane[1] = last[5]
        unit = [jnp.exp2(last[6 + t]) * (1.0 / CODE) for t in range(2)]
        for pair in range(FIELDS // 8):
            fields = last if pair == FIELDS // 8 - 1 else spread(x, pair)
            for i, value in enumerate(fields):
                which, k = divmod(8 * pair + i, OWN_LEVELS)
                row = OWN_LEVELS * x + k
                if which < 2:
                    to = pl.ds(which * 8 * pitch + base + row, 8, stride=pitch)
                    cells[to, :] = value * unit[which]
                elif which < 4:
                    to = pl.ds((which - 2) * 8 * HALF + row, 8, stride=HALF)
                    flow[to, :] = value * (FASTEST / CODE)
        return carry

    lax.fori_loop(0, BLOCKS // CORES, take, 0)

    def at(where, row, g):
        return pl.ds(pl.multiple_of(row * where[0] + where[1] + 8 * g, 8), 8)

    spare = jnp.zeros((HALF - 2 * OWN_LEVELS, 128), F32)
    for s in range(16):
        for field, where in ((cells, cells_at), (flow, flow_at)):
            end = s * where[0] + where[1] + HALF
            field[end - spare.shape[0] : end, :] = spare

    def faces(w):
        size = jnp.abs(w)
        return (
            (-w - size) * (1.0 / 12.0),
            (7.0 * w + 3.0 * size) * (1.0 / 12.0),
            (7.0 * w - 3.0 * size) * (1.0 / 12.0),
            (size - w) * (1.0 / 12.0),
        )

    def prepare(g, carry):
        level = levels_of(sub + 8 * g, side).astype(F32)
        wet = [jnp.where(plane[1, s : s + 1, :] > level, 1.0, 0.0) for s in range(8)]
        for t in range(2):
            for s in range(8):
                here = at(cells_at, 8 * t + s, g)
                cells[here, :] = wet[s] * cells[here, :]
        beyond = jnp.where(left, pltpu.roll(wet[0], 64, 1), 0.0)
        north_w = [
            flow[at(flow_at, 8 + s, g), :] * wet[s] * (wet[s + 1] if s < 7 else beyond) for s in range(8)
        ]
        first = jnp.where(left, 0.0, pltpu.roll(north_w[7], 64, 1))
        merid = [faces(w) for w in [first] + north_w]
        for s in range(8):
            east_w = flow[at(flow_at, s, g), :] * wet[s] * pltpu.roll(wet[s], 127, 1)
            a, b, d, e = faces(east_w)
            a1, b1, d1, e1 = faces(pltpu.roll(east_w, 1, 1))
            p1, q1, r1, s1 = merid[s]
            p, q, r, s0 = merid[s + 1]
            south = [wet[s] * p1, wet[s] * (q1 - p)]
            north = [wet[s] * (s1 - r), -wet[s] * s0]
            if s < 2:
                south[0] = jnp.where(left, 0.0, south[0])
            if s < 1:
                south[1] = jnp.where(left, 0.0, south[1])
            if s > 6:
                north[0] = jnp.where(left, north[0], 0.0)
            if s > 5:
                north[1] = jnp.where(left, north[1], 0.0)
            coef[g, s, 0] = wet[s] * (1.0 + (d1 - b) + (r1 - q))
            coef[g, s, 1] = wet[s] * a1
            coef[g, s, 2] = wet[s] * (b1 - a)
            coef[g, s, 3] = wet[s] * (e1 - d)
            coef[g, s, 4] = -wet[s] * e
            coef[g, s, 5], coef[g, s, 6] = south
            coef[g, s, 7], coef[g, s, 8] = north
        return carry

    lax.fori_loop(0, HALF // 8, prepare, 0, unroll=True)


def own_kernel(*refs):
    arrived, (ops, cells, coef, plane, ordered, recv, flow) = refs[: 2 * TILES], refs[2 * TILES :]
    own = lax.axis_index("depth")
    tile = lax.axis_index("tile")
    core, half = own % CORES, own // CORES
    for i, ref in enumerate(arrived):
        far, distance = divmod(i, TILES)
        to = 2 * ((tile + TILES - distance) % TILES) + (half ^ far)
        for pair in range(FIELDS // 8):
            recv[to, 16 * pair : 16 * pair + 16, :] = piece(ref, pair, core)
    load_half(recv, core, cells, HALF, 0, flow, coef, plane, True)
    shape = (PITCH, LEVELS)
    pick = jnp.where(level_rows(shape, core) == index(shape, 1), 1.0, 0.0).astype(jnp.bfloat16)
    for t in range(2):
        rows = jnp.dot(pick, ops[t], preferred_element_type=F32).astype(jnp.bfloat16)
        both = lax.dot_general(rows, pick, (((1,), (1,)), ((), ())), preferred_element_type=F32)
        ordered[t] = both.astype(jnp.bfloat16)


def steps_kernel(
    others, own_cells, own_coef, plane, ops, out0, out1, out2, out3,
    recv, cells, firsts, moved, flow, coef, light, ends,
):
    own = lax.axis_index("depth")
    tile = lax.axis_index("tile")
    core, half = own % CORES, own // CORES
    for i in range(2 * TILES):
        far, distance = divmod(i, TILES)
        to = 2 * ((tile + TILES - distance) % TILES) + (half ^ far)
        recv[to] = others[PIECE * i : PIECE * i + PIECE, :]
    load_half(recv, 1 - core, cells, PITCH, HALF, flow, coef, plane, False)
    for s in range(16):
        cells[PITCH * s : PITCH * s + HALF, :] = own_cells[HALF * s : HALF * s + HALF, :]
    lane = index((8, 128), 1)

    def block(base, g):
        return slice(base * PITCH + 8 * g, base * PITCH + 8 * g + 8)

    deep = level_rows((PITCH, 128), core).astype(F32)
    light[...] = jnp.exp(deep * (-4.0 / LEVELS))

    def combine(c, near, far):
        centre = near[1]
        return (
            (c[0] * centre + c[6] * near[0] + c[7] * near[2])
            + (c[5] * far[0] + c[8] * far[1])
            + (c[2] * pltpu.roll(centre, 1, 1) + c[3] * pltpu.roll(centre, 127, 1))
            + (c[1] * pltpu.roll(centre, 2, 1) + c[4] * pltpu.roll(centre, 126, 1))
        )

    def stage(source, g, emit):
        def at(t, s):
            return source[block(8 * t + s, g), :]

        columns = []
        for t in range(2):
            inner = [at(t, s) for s in range(8)]
            turned = [pltpu.roll(inner[s], 64, 1) for s in (6, 7, 0, 1)]
            columns.append(turned[:2] + inner + turned[2:])
        for s in range(8):
            stencil = own_coef.at[g, s] if g < HALF // 8 else coef.at[g - HALF // 8, s]
            c = [stencil[i] for i in range(9)]
            for t in range(2):
                k = columns[t]
                emit(t, s, combine(c, k[s + 1 : s + 4], (k[s], k[s + 4])))

    def first_stage(g):
        def emit(t, s, value):
            firsts[block(8 * t + s, g), :] = value

        stage(cells, g, emit)

    def second_stage(g):
        def emit(t, s, value):
            at = block(8 * t + s, g)
            moved[at, :] = 0.5 * (cells[at, :] + value)

        stage(firsts, g, emit)

    def step(n, carry):
        for part in (first_stage, second_stage):
            for g in range(PITCH // 8):
                part(g)
        for pair in range(4):
            mixed = []
            for t in range(2):
                base = (t * 8 + 2 * pair) * PITCH
                both = jnp.concatenate(
                    [moved[base : base + PITCH, :], moved[base + PITCH : base + 2 * PITCH, :]], axis=1
                ).astype(jnp.bfloat16)
                mixed.append(jnp.dot(ops[t], both, preferred_element_type=F32))
            for i in range(2):
                s = 2 * pair + i
                wet = deep < plane[1, s : s + 1, :]
                p = jnp.where(wet, mixed[0][:, 128 * i : 128 * i + 128], 0.0)
                q = jnp.where(wet, mixed[1][:, 128 * i : 128 * i + 128], 0.0)
                square = p * p
                uptake = (plane[0, s : s + 1, :] * light[...]) * (
                    square * p / (square + half_sat_sq)
                )
                gain = uptake - remin_rate * q
                cells[s * PITCH : s * PITCH + PITCH, :] = p - gain
                cells[(8 + s) * PITCH : (8 + s) * PITCH + PITCH, :] = q + gain
        return carry

    lax.fori_loop(0, STEPS, step, 0)

    chunk = lane // 32

    def send(n, carry):
        first = HALF * (n % CORES) + OWN_LEVELS * (half ^ (n // CORES))
        blocks = []
        for t in range(2):
            def level(k):
                return cells[pl.ds(t * 8 * PITCH + first + k, 8, stride=PITCH), :]

            largest = jnp.abs(level(0))
            for k in range(1, OWN_LEVELS):
                largest = jnp.maximum(largest, jnp.abs(level(k)))
            scale = exponent(largest)
            per_unit = CODE * jnp.exp2(-scale)
            blocks += [level(k) * per_unit for k in range(OWN_LEVELS)] + [scale]
        for pair in range(ENDS // 4):
            halves = []
            for i in (2 * pair, 2 * pair + 1):
                a, b = blocks[2 * i], blocks[2 * i + 1]
                halves.append(
                    jnp.where(
                        chunk == 0,
                        pltpu.roll(a, 112, 1),
                        jnp.where(
                            chunk == 1,
                            pltpu.roll(a, 80, 1),
                            jnp.where(chunk == 2, pltpu.roll(b, 48, 1), pltpu.roll(b, 16, 1)),
                        ),
                    )
                )
            ends[n, 16 * pair : 16 * pair + 16, :] = coded(jnp.concatenate(halves, axis=0))
        return carry

    lax.fori_loop(0, BLOCKS, send, 0)
    for n, out in enumerate((out0, out1, out2, out3)):
        out[...] = ends[n]


def turn_kernel(in0, in1, in2, in3, out0, out1, out2, out3, got, sent):
    block = lax.axis_index("depth")
    tile = lax.axis_index("tile")
    for n, ref in enumerate((in0, in1, in2, in3)):
        got[block ^ n] = ref[...]
    sub = index((8, 128), 0)
    chunk = index((8, 128), 1) // 32
    for pair in range(ENDS // 4):
        whole = [
            got[d, 16 * pair : 16 * pair + 16, :].astype(jnp.int32).astype(F32) for d in range(4)
        ]
        halves = {t: [] for t in range(4)}
        for part in range(2):
            m = [x[8 * part : 8 * part + 8] for x in whole]
            lined = {}
            for par in range(2):
                for h in range(2):
                    z = [pltpu.roll(m[d], (32 * (d - 2 * par - h)) % 128, 1) for d in range(4)]
                    lined[par, h] = jnp.where(
                        chunk == 0,
                        z[0],
                        jnp.where(chunk == 1, z[1], jnp.where(chunk == 2, z[2], z[3])),
                    )
            for h in range(2):
                a, b = lined[0, h], lined[1, h]
                halves[2 * h].append(jnp.where(sub < 4, a, pltpu.roll(b, 4, 0)))
                halves[2 * h + 1].append(jnp.where(sub < 4, pltpu.roll(a, 4, 0), b))
        for t in range(4):
            sent[t, 16 * pair : 16 * pair + 16, :] = (
                jnp.concatenate(halves[t], axis=0).astype(jnp.int32).astype(I16)
            )
    for n, out in enumerate((out0, out1, out2, out3)):
        out[...] = sent[(tile + n) % TILES]


def finish_kernel(in0, in1, in2, in3, state, land_sea, depth_index, out, got):
    block = lax.axis_index("depth")
    tile = lax.axis_index("tile")
    for n, ref in enumerate((in0, in1, in2, in3)):
        got[(tile + TILES - n) % TILES] = ref[...]
    wet_levels = jnp.where(land_sea[...] == 1, depth_index[...], 0)
    first = block * OWN_LEVELS
    left = index((16, 128), 1) < 64
    for q in range(4):
        half, west = divmod(q, 2)
        lanes = slice(128 * q, 128 * q + 128)
        values = []
        for pair in range(ENDS // 4):
            x, y = (wide(got[2 * west + i, 16 * pair : 16 * pair + 16, :]) for i in range(2))
            x = jnp.where(left, turn(x, 2 * half), turn(y, 2 - 2 * half))
            values += [x[0:4], x[4:8], x[8:12], x[12:16]]
        for t in range(2):
            base = t * (OWN_LEVELS + 1)
            unit = jnp.exp2(values[base + OWN_LEVELS]) * (1.0 / CODE)
            for k in range(OWN_LEVELS):
                wet = wet_levels[:, lanes] > first + k
                out[0, t, k, :, lanes] = jnp.where(
                    wet, values[base + k] * unit - state[0, t, k, :, lanes], 0.0
                )


def near(*arrays):
    return [pltpu.with_memory_space_constraint(x, pltpu.VMEM) for x in arrays]


def call(kernel, outs, scratch, *args, reserve=8, place=near):
    return pl.pallas_call(
        kernel,
        out_shape=outs,
        in_specs=[VMEM] * len(args),
        out_specs=jax.tree.map(lambda _: VMEM, outs),
        scratch_shapes=scratch,
        compiler_params=pltpu.CompilerParams(vmem_limit_bytes=reserve << 20),
    )(*place(*args))


def across_depth(messages):
    return [messages[0]] + [
        lax.ppermute(messages[n], "depth", [(i, i ^ n) for i in range(BLOCKS)])
        for n in range(1, BLOCKS)
    ]


def across_tiles(messages):
    return [messages[0]] + [
        lax.ppermute(messages[n], "tile", [(i, (i + n) % TILES) for i in range(TILES)])
        for n in range(1, TILES)
    ]


def window_shards(initial_states, velocity, growth, land_sea, depth_index, column_ops):
    message = pltpu.VMEM((4 * ENDS, 128), I16)
    slots = pltpu.VMEM((4, 4 * ENDS, 128), I16)
    cells = pltpu.VMEM((2 * 8 * PITCH, 128), F32)
    both = pltpu.VMEM((BOTH, 128), I16)
    sent = pltpu.VMEM((TILES, BOTH, 128), I16)
    across, *here = call(
        pack_kernel,
        [pltpu.VMEM((2 * MAIN + FIELDS, 128), I16)] + [both] * TILES,
        [pltpu.VMEM((MAIN, 512), F32), sent],
        initial_states,
        velocity,
        growth,
        land_sea,
        depth_index,
        reserve=60,
        place=lambda *args: args,
    )
    across = lax.ppermute(across, "depth", [(i, i ^ CORES) for i in range(BLOCKS)])
    received = across_tiles(here)
    received += across_tiles(call(relay_kernel, [both] * TILES, [sent], across))
    others = call(core_kernel, pltpu.VMEM((2 * TILES * PIECE, 128), I16), [], *received)
    others = lax.ppermute(others, "depth", [(i, i ^ 1) for i in range(BLOCKS)])
    pieces = pltpu.VMEM((2 * TILES, PIECE, 128), I16)
    flow = pltpu.VMEM((2 * 8 * HALF, 128), F32)
    coef = pltpu.VMEM((HALF // 8, 8, 9, 8, 128), F32)
    loaded = call(
        own_kernel,
        [flow, coef, pltpu.VMEM((2, 8, 128), F32), pltpu.VMEM((2, PITCH, PITCH), jnp.bfloat16)],
        [pieces, flow],
        *received,
        column_ops,
    )
    out = call(
        steps_kernel,
        [message] * 4,
        [pieces, cells, cells, cells, flow, coef, pltpu.VMEM((PITCH, 128), F32), slots],
        others,
        *loaded,
        reserve=16,
    )
    turned = call(turn_kernel, [message] * 4, [slots] * 2, *across_depth(out))
    segs = lax.axis_size("seg")
    last = [
        lax.ppermute(
            turned[n],
            ("seg", "tile"),
            [
                (s * TILES + t, ((s + 1) % segs) * TILES + (t + n) % TILES)
                for s in range(segs)
                for t in range(TILES)
            ],
        )
        for n in range(4)
    ]
    return call(
        finish_kernel,
        jax.ShapeDtypeStruct(initial_states.shape, F32),
        [slots],
        *last,
        initial_states,
        land_sea,
        depth_index,
    )


def shards(initial_states, velocity, growth, land_sea, depth_index, column_ops):
    fits = (
        lax.axis_size("tile") == TILES
        and lax.axis_size("depth") == BLOCKS
        and initial_states.shape == (1, 2, OWN_LEVELS, 4, TILES * BLOCKS * OWN)
    )
    plan = window_shards if fits else stepwise_shards
    return plan(initial_states, velocity, growth, land_sea, depth_index, column_ops)


def solution(mesh):
    return jax.shard_map(
        shards,
        mesh=mesh,
        in_specs=(
            P("seg", None, "depth", "tile", None),
            P("seg", None, "depth", "tile", None),
            P("seg", "tile", None),
            P("tile", None),
            P("tile", None),
            P(),
        ),
        out_specs=P("seg", None, "depth", "tile", None),
        check_vma=False,
    )
```

```python
import jax
import jax.numpy as jnp
from jax import lax
from jax.experimental import pallas as pl
from jax.experimental.pallas import tpu as pltpu
from jax.sharding import PartitionSpec as P

STEPS = 4


half_sat_sq = 0.25
remin_rate = 0.2


def with_halo(cells, sides, width):
    for axis, dim in sides:
        count = lax.axis_size(axis)
        ends = count - 1
        head = lax.slice_in_dim(cells, 0, width, axis=dim)
        tail = lax.slice_in_dim(cells, cells.shape[dim] - width, cells.shape[dim], axis=dim)
        cells = jnp.concatenate(
            [
                lax.ppermute(tail, axis, [(i, (i + 1) % count) for i in range(ends)]),
                cells,
                lax.ppermute(head, axis, [((i + 1) % count, i) for i in range(ends)]),
            ],
            axis=dim,
        )
    return cells


def passed_along(block, axis, distance):
    devices = range(lax.axis_size(axis))
    route = [((i - distance) % len(devices), i) for i in devices]
    return lax.ppermute(block, axis, route)


def face_flux(behind, near_side, far_side, beyond, courant):
    return (
        courant * (7.0 * (near_side + far_side) - (behind + beyond)) / 12.0
        - jnp.abs(courant) * (3.0 * (far_side - near_side) - (beyond - behind)) / 12.0
    )


def tendency(padded, north_faces, east_faces):
    merid = face_flux(
        padded[..., :-3, :],
        padded[..., 1:-2, :],
        padded[..., 2:-1, :],
        padded[..., 3:, :],
        north_faces,
    )
    centre = padded[..., 2:-2, :]
    zonal_flux = face_flux(
        jnp.roll(centre, 1, axis=-1),
        centre,
        jnp.roll(centre, -1, axis=-1),
        jnp.roll(centre, -2, axis=-1),
        east_faces,
    )
    return merid[..., :-1, :] - merid[..., 1:, :] + (jnp.roll(zonal_flux, 1, axis=-1) - zonal_flux)


def biology(mixed, rate, light_level, wet_cells):
    phosphate = mixed[..., 0, :, :, :]
    particles = mixed[..., 1, :, :, :]
    uptake = (
        rate
        * light_level
        * phosphate
        * phosphate
        * phosphate
        / (phosphate * phosphate + half_sat_sq)
    )
    return jnp.stack(
        [
            wet_cells * (phosphate - uptake + remin_rate * particles),
            wet_cells * (particles + uptake - remin_rate * particles),
        ],
        axis=-4,
    )


def stepwise_shards(initial_states, velocity, growth, land_sea, depth_index, column_ops):
    seg_dev = initial_states.shape[0]
    lev_dev = initial_states.shape[2]
    first_level = lax.axis_index("depth") * lev_dev
    levels = first_level + lax.iota(jnp.int32, lev_dev)
    wet_cells = jnp.where(
        (land_sea[None] == 1) & (levels[:, None, None] < depth_index[None]), 1.0, 0.0
    ).astype(jnp.float32)
    light_level = jnp.exp(-4.0 * levels.astype(jnp.float32) / column_ops.shape[1])[:, None, None]
    own_rows = lax.dynamic_slice_in_dim(column_ops, first_level, lev_dev, 1)
    uptake_rate = growth[:, None]
    tracer_state = wet_cells * initial_states
    flow_stack = jnp.concatenate([velocity[:, 0], velocity[:, 1], wet_cells[None]], axis=0)
    flow_edges = with_halo(flow_stack, (("tile", 2),), 3)
    wet_edges = flow_edges[2 * seg_dev]
    north_wide = (flow_edges[seg_dev : 2 * seg_dev, :, :-1] * wet_edges[:, :-1] * wet_edges[:, 1:])[
        :, None
    ]
    wet_wide = wet_edges[:, 1:-1]
    east_wide = (flow_edges[:seg_dev, :, 1:-1] * wet_wide * jnp.roll(wet_wide, -1, axis=-1))[
        :, None
    ]
    north_faces = north_wide[:, :, :, 2:-2]
    east_faces = east_wide[:, :, :, 2:-2]
    for step_index in range(STEPS):
        padded = with_halo(tracer_state, (("tile", 3),), 4)
        first_section = wet_wide * (padded[:, :, :, 2:-2] + tendency(padded, north_wide, east_wide))
        advected = wet_cells * (
            0.5 * tracer_state
            + 0.5
            * (first_section[:, :, :, 2:-2] + tendency(first_section, north_faces, east_faces))
        )
        rounded = advected.astype(jnp.bfloat16)
        mixed = jnp.einsum(
            "tkm,stmrl->stkrl",
            own_rows,
            lax.all_gather(rounded, "depth", axis=2, tiled=True),
            preferred_element_type=jnp.float32,
        )
        tracer_state = biology(wet_cells * mixed, uptake_rate, light_level, wet_cells)
    previous = passed_along(tracer_state, "seg", 1)
    before = jnp.concatenate([previous, tracer_state[: seg_dev - 1]], axis=0)
    return wet_cells * (before - initial_states)


TILES = 4
BLOCKS = 4
LEVELS = 76
OWN_LEVELS = LEVELS // BLOCKS
PITCH = 80
HALF = PITCH // 2
OWN = 32
REACH = 4 * STEPS
WINDOW = OWN + 2 * REACH
CODE = 32000.0
FASTEST = 0.35
FIELDS = 4 * OWN_LEVELS + 4
ENDS = 2 * OWN_LEVELS + 2
PIECE = 2 * FIELDS
MAIN = 4 * FIELDS
BOTH = PIECE + FIELDS
CORES = 2

F32 = jnp.float32
I16 = jnp.int16
VMEM = pl.BlockSpec(memory_space=pltpu.VMEM)


def coded(values):
    return jnp.floor(values + 0.5).astype(jnp.int32).astype(I16)


def exponent(largest):
    return jnp.clip(jnp.ceil(jnp.log2(jnp.maximum(largest, 1e-36))), -119.0, 125.0)


def index(shape, dim):
    return lax.broadcasted_iota(jnp.int32, shape, dim)


def pack_kernel(state, velocity, growth, land_sea, depth_index, *refs):
    (out, *outs), (turned, sent) = refs[:-2], refs[-2:]
    scales = []
    for t in range(2):
        largest = jnp.abs(state[0, t, 0])
        for k in range(1, OWN_LEVELS):
            largest = jnp.maximum(largest, jnp.abs(state[0, t, k]))
        scales.append(exponent(largest))
    per_unit = [CODE * jnp.exp2(-e) for e in scales]
    wet_levels = jnp.where(land_sea[...] == 1, depth_index[...], 0).astype(F32)

    def field(n):
        which, k = divmod(n, OWN_LEVELS)
        if which < 2:
            return state[0, which, k] * per_unit[which]
        if which < 4:
            return velocity[0, which - 2, k] * (CODE / FASTEST)
        return [growth[0] * CODE, wet_levels, scales[0], scales[1]][k]

    for pair in range(FIELDS // 2):
        rows = jnp.concatenate([field(2 * pair), field(2 * pair + 1)], axis=0)
        turned[8 * pair : 8 * pair + 8, :] = pltpu.roll(rows, REACH, 1)
    half = lax.axis_index("depth") // CORES

    def part_of(side):
        def part(lanes, row, count):
            at = pl.ds(pl.multiple_of(128 * ((2 * side + lanes) % 4), 128), 128)
            return turned[row : row + count, at]

        return part

    other = part_of(1 - half)
    for lanes in range(2):
        for row in range(0, MAIN, 16):
            out[MAIN * lanes + row : MAIN * lanes + row + 16, :] = coded(other(lanes, row, 16))
    for pair in range(FIELDS // 16):
        row = 2 * MAIN + 16 * pair
        out[row : row + 16, :] = coded(tails(other, TILES - 1, pair))
    windows(part_of(half), coded, None, sent, outs)


def tails(part, t, pair):
    chunk = index((8, 128), 1) // 32
    lanes, first = (t + 1) // 2, 2 * ((t + 1) % 2)
    blocks = []
    for group in (2 * pair, 2 * pair + 1):
        late = group + FIELDS // 8
        rows = (2 * late, 2 * group, 2 * late + 1, 2 * group + 1)
        blocks.append(
            by_chunk(chunk, [turn(part(lanes, 8 * i, 8), n - first) for n, i in enumerate(rows)])
        )
    return jnp.concatenate(blocks, axis=0)


def turn(block, chunks):
    return pltpu.roll(block, (32 * chunks) % 128, 1) if chunks % 4 else block


def windows(part, packed, last, sent, outs):
    left = index((8, 128), 1) < 64
    for t in range(TILES):
        for pair in range(FIELDS // 8):
            blocks = []
            for group in (2 * pair, 2 * pair + 1):
                lo, hi = (part(t // 2, 8 * i, 8) for i in (2 * group, 2 * group + 1))
                lo, hi = turn(lo, 2 * (t % 2)), turn(hi, 2 - 2 * (t % 2))
                blocks.append(jnp.where(left, lo, hi))
            sent[t, 16 * pair : 16 * pair + 16, :] = packed(jnp.concatenate(blocks, axis=0))
        for pair in range(FIELDS // 16):
            row = PIECE + 16 * pair
            if t == TILES - 1 and last is not None:
                sent[t, row : row + 16, :] = last(pair)
            else:
                sent[t, row : row + 16, :] = packed(tails(part, t, pair))
    tile = lax.axis_index("tile")
    for n, out in enumerate(outs):
        out[...] = sent[(tile + n) % TILES]


def relay_kernel(ref, *refs):
    outs, sent = refs[:-1], refs[-1]

    def part(lanes, row, count):
        base = MAIN * lanes + row // 16 * 16
        skip = row % 16
        return wide(ref[base : base + 16, :])[skip : skip + count]

    def last(pair):
        row = 2 * MAIN + 16 * pair
        return ref[row : row + 16, :]

    windows(part, narrow, last, sent, outs)


def piece(ref, pair, core):
    main = wide(ref[16 * pair : 16 * pair + 16, :])
    row = PIECE + 16 * (pair % (FIELDS // 16))
    tail = wide(ref[row : row + 16, :])
    odd = index((16, 128), 1) // 32 % 2 == 1
    if pair < FIELDS // 16:
        second = jnp.where(odd, tail, turn(main, 3))
    else:
        second = jnp.where(odd, turn(tail, 1), turn(main, 3))
    return narrow(jnp.where(core == 0, main, second))


def core_kernel(*refs):
    sources, out = refs[:-1], refs[-1]
    core = lax.axis_index("depth") % CORES
    for i, ref in enumerate(sources):
        for pair in range(FIELDS // 8):
            row = PIECE * i + 16 * pair
            out[row : row + 16, :] = piece(ref, pair, 1 - core)


def by_chunk(chunk, values):
    return jnp.where(
        chunk == 0,
        values[0],
        jnp.where(chunk == 1, values[1], jnp.where(chunk == 2, values[2], values[3])),
    )


def wide(values):
    return values.astype(jnp.int32).astype(F32)


def narrow(values):
    return values.astype(jnp.int32).astype(I16)


def levels_of(row, core):
    level = row + OWN_LEVELS * core + jnp.where(row >= OWN_LEVELS, OWN_LEVELS, 0)
    return jnp.where(row < 2 * OWN_LEVELS, level, 4 * LEVELS)


def level_rows(shape, core):
    row = index(shape, 0)
    return jnp.where(
        row < HALF, levels_of(row, core), levels_of(row - HALF, 1 - core)
    )


def load_half(recv, side, cells, pitch, base, flow, coef, plane, fresh):
    sub = index((8, 128), 0)
    left = index((8, 128), 1) < 64
    cells_at, flow_at = (pitch, base), (HALF, 0)

    def spread(x, pair):
        sent = [wide(recv[2 * t + x, 16 * pair : 16 * pair + 16, :]) for t in range(TILES)]
        fields = []
        for part in range(2):
            m = [y[8 * part : 8 * part + 8] for y in sent]
            up, across = {}, {}
            for h in range(2):
                a, b = m[2 * h], m[2 * h + 1]
                up[0, h] = jnp.where(sub < 4, a, pltpu.roll(b, 4, 0))
                up[1, h] = jnp.where(sub < 4, pltpu.roll(a, 4, 0), b)
            for p in range(2):
                a, b = up[p, 0], up[p, 1]
                across[p, 0] = jnp.where(left, a, pltpu.roll(b, 64, 1))
                across[p, 1] = jnp.where(left, pltpu.roll(a, 64, 1), b)
            fields += [across[0, 0], across[1, 0], across[0, 1], across[1, 1]]
        return fields

    def take(x, carry):
        last = spread(x, FIELDS // 8 - 1)
        if fresh:
            plane[0] = last[4] * (1.0 / CODE)
            plane[1] = last[5]
        unit = [jnp.exp2(last[6 + t]) * (1.0 / CODE) for t in range(2)]
        for pair in range(FIELDS // 8):
            fields = last if pair == FIELDS // 8 - 1 else spread(x, pair)
            for i, value in enumerate(fields):
                which, k = divmod(8 * pair + i, OWN_LEVELS)
                row = OWN_LEVELS * x + k
                if which < 2:
                    to = pl.ds(which * 8 * pitch + base + row, 8, stride=pitch)
                    cells[to, :] = value * unit[which]
                elif which < 4:
                    to = pl.ds((which - 2) * 8 * HALF + row, 8, stride=HALF)
                    flow[to, :] = value * (FASTEST / CODE)
        return carry

    lax.fori_loop(0, BLOCKS // CORES, take, 0)

    def at(where, row, g):
        return pl.ds(pl.multiple_of(row * where[0] + where[1] + 8 * g, 8), 8)

    spare = jnp.zeros((HALF - 2 * OWN_LEVELS, 128), F32)
    for s in range(16):
        for field, where in ((cells, cells_at), (flow, flow_at)):
            end = s * where[0] + where[1] + HALF
            field[end - spare.shape[0] : end, :] = spare

    def faces(w):
        size = jnp.abs(w)
        return (
            (-w - size) * (1.0 / 12.0),
            (7.0 * w + 3.0 * size) * (1.0 / 12.0),
            (7.0 * w - 3.0 * size) * (1.0 / 12.0),
            (size - w) * (1.0 / 12.0),
        )

    def prepare(g, carry):
        level = levels_of(sub + 8 * g, side).astype(F32)
        wet = [jnp.where(plane[1, s : s + 1, :] > level, 1.0, 0.0) for s in range(8)]
        for t in range(2):
            for s in range(8):
                here = at(cells_at, 8 * t + s, g)
                cells[here, :] = wet[s] * cells[here, :]
        beyond = jnp.where(left, pltpu.roll(wet[0], 64, 1), 0.0)
        north_w = [
            flow[at(flow_at, 8 + s, g), :] * wet[s] * (wet[s + 1] if s < 7 else beyond) for s in range(8)
        ]
        first = jnp.where(left, 0.0, pltpu.roll(north_w[7], 64, 1))
        merid = [faces(w) for w in [first] + north_w]
        for s in range(8):
            east_w = flow[at(flow_at, s, g), :] * wet[s] * pltpu.roll(wet[s], 127, 1)
            a, b, d, e = faces(east_w)
            a1, b1, d1, e1 = faces(pltpu.roll(east_w, 1, 1))
            p1, q1, r1, s1 = merid[s]
            p, q, r, s0 = merid[s + 1]
            south = [wet[s] * p1, wet[s] * (q1 - p)]
            north = [wet[s] * (s1 - r), -wet[s] * s0]
            if s < 2:
                south[0] = jnp.where(left, 0.0, south[0])
            if s < 1:
                south[1] = jnp.where(left, 0.0, south[1])
            if s > 6:
                north[0] = jnp.where(left, north[0], 0.0)
            if s > 5:
                north[1] = jnp.where(left, north[1], 0.0)
            coef[g, s, 0] = wet[s] * (1.0 + (d1 - b) + (r1 - q))
            coef[g, s, 1] = wet[s] * a1
            coef[g, s, 2] = wet[s] * (b1 - a)
            coef[g, s, 3] = wet[s] * (e1 - d)
            coef[g, s, 4] = -wet[s] * e
            coef[g, s, 5], coef[g, s, 6] = south
            coef[g, s, 7], coef[g, s, 8] = north
        return carry

    lax.fori_loop(0, HALF // 8, prepare, 0, unroll=True)


def own_kernel(*refs):
    arrived, (ops, cells, coef, plane, ordered, recv, flow) = refs[: 2 * TILES], refs[2 * TILES :]
    own = lax.axis_index("depth")
    tile = lax.axis_index("tile")
    core, half = own % CORES, own // CORES
    for i, ref in enumerate(arrived):
        far, distance = divmod(i, TILES)
        to = 2 * ((tile + TILES - distance) % TILES) + (half ^ far)
        for pair in range(FIELDS // 8):
            recv[to, 16 * pair : 16 * pair + 16, :] = piece(ref, pair, core)
    load_half(recv, core, cells, HALF, 0, flow, coef, plane, True)
    shape = (PITCH, LEVELS)
    pick = jnp.where(level_rows(shape, core) == index(shape, 1), 1.0, 0.0).astype(jnp.bfloat16)
    for t in range(2):
        rows = jnp.dot(pick, ops[t], preferred_element_type=F32).astype(jnp.bfloat16)
        both = lax.dot_general(rows, pick, (((1,), (1,)), ((), ())), preferred_element_type=F32)
        ordered[t] = both.astype(jnp.bfloat16)


def steps_kernel(
    others, own_cells, own_coef, plane, ops, out0, out1, out2, out3,
    recv, cells, firsts, moved, flow, coef, light, ends,
):
    own = lax.axis_index("depth")
    tile = lax.axis_index("tile")
    core, half = own % CORES, own // CORES
    for i in range(2 * TILES):
        far, distance = divmod(i, TILES)
        to = 2 * ((tile + TILES - distance) % TILES) + (half ^ far)
        recv[to] = others[PIECE * i : PIECE * i + PIECE, :]
    load_half(recv, 1 - core, cells, PITCH, HALF, flow, coef, plane, False)
    for s in range(16):
        cells[PITCH * s : PITCH * s + HALF, :] = own_cells[HALF * s : HALF * s + HALF, :]
    lane = index((8, 128), 1)

    def block(base, g):
        return slice(base * PITCH + 8 * g, base * PITCH + 8 * g + 8)

    deep = level_rows((PITCH, 128), core).astype(F32)
    light[...] = jnp.exp(deep * (-4.0 / LEVELS))

    source_lane, lanes = index((256, 256), 0) % 128, index((256, 256), 1)
    shifts = jnp.where(
        lanes % 128 == (source_lane + jnp.where(lanes < 128, 2, 126)) % 128, 1.0, 0.0
    ).astype(jnp.bfloat16)

    def combine(c, near, far, two):
        centre = near[1]
        return (
            (c[0] * centre + c[6] * near[0] + c[7] * near[2])
            + (c[5] * far[0] + c[8] * far[1])
            + (c[2] * pltpu.roll(centre, 1, 1) + c[3] * pltpu.roll(centre, 127, 1))
            + (c[1] * two[0] + c[4] * two[1])
        )

    def stage(source, g, emit):
        def at(t, s):
            return source[block(8 * t + s, g), :]

        rows = jnp.concatenate([at(t, s) for t in range(2) for s in range(8)], axis=0)
        high = rows.astype(jnp.bfloat16)
        low = (rows - high.astype(F32)).astype(jnp.bfloat16)
        moves = jnp.dot(jnp.concatenate([high, low], axis=1), shifts, preferred_element_type=F32)

        columns = []
        for t in range(2):
            inner = [at(t, s) for s in range(8)]
            turned = [pltpu.roll(inner[s], 64, 1) for s in (6, 7, 0, 1)]
            columns.append(turned[:2] + inner + turned[2:])
        for s in range(8):
            stencil = own_coef.at[g, s] if g < HALF // 8 else coef.at[g - HALF // 8, s]
            c = [stencil[i] for i in range(9)]
            for t in range(2):
                k = columns[t]
                row = slice(8 * (8 * t + s), 8 * (8 * t + s) + 8)
                two = moves[row, :128], moves[row, 128:]
                emit(t, s, combine(c, k[s + 1 : s + 4], (k[s], k[s + 4]), two))

    def first_stage(g):
        def emit(t, s, value):
            firsts[block(8 * t + s, g), :] = value

        stage(cells, g, emit)

    def second_stage(g):
        def emit(t, s, value):
            at = block(8 * t + s, g)
            moved[at, :] = 0.5 * (cells[at, :] + value)

        stage(firsts, g, emit)

    def step(n, carry):
        for g in range(PITCH // 8 + 1):
            if g < PITCH // 8:
                first_stage(g)
            if g > 0:
                second_stage(g - 1)
        for pair in range(4):
            mixed = []
            for t in range(2):
                base = (t * 8 + 2 * pair) * PITCH
                both = jnp.concatenate(
                    [moved[base : base + PITCH, :], moved[base + PITCH : base + 2 * PITCH, :]], axis=1
                ).astype(jnp.bfloat16)
                mixed.append(jnp.dot(ops[t], both, preferred_element_type=F32))
            for i in range(2):
                s = 2 * pair + i
                wet = deep < plane[1, s : s + 1, :]
                p = jnp.where(wet, mixed[0][:, 128 * i : 128 * i + 128], 0.0)
                q = jnp.where(wet, mixed[1][:, 128 * i : 128 * i + 128], 0.0)
                square = p * p
                uptake = (plane[0, s : s + 1, :] * light[...]) * (
                    square * p / (square + half_sat_sq)
                )
                gain = uptake - remin_rate * q
                cells[s * PITCH : s * PITCH + PITCH, :] = p - gain
                cells[(8 + s) * PITCH : (8 + s) * PITCH + PITCH, :] = q + gain
        return carry

    lax.fori_loop(0, STEPS, step, 0)

    chunk = lane // 32

    def send(n, carry):
        first = HALF * (n % CORES) + OWN_LEVELS * (half ^ (n // CORES))
        blocks = []
        for t in range(2):
            def level(k):
                return cells[pl.ds(t * 8 * PITCH + first + k, 8, stride=PITCH), :]

            largest = jnp.abs(level(0))
            for k in range(1, OWN_LEVELS):
                largest = jnp.maximum(largest, jnp.abs(level(k)))
            scale = exponent(largest)
            per_unit = CODE * jnp.exp2(-scale)
            blocks += [level(k) * per_unit for k in range(OWN_LEVELS)] + [scale]
        for pair in range(ENDS // 4):
            halves = []
            for i in (2 * pair, 2 * pair + 1):
                a, b = blocks[2 * i], blocks[2 * i + 1]
                halves.append(
                    jnp.where(
                        chunk == 0,
                        pltpu.roll(a, 112, 1),
                        jnp.where(
                            chunk == 1,
                            pltpu.roll(a, 80, 1),
                            jnp.where(chunk == 2, pltpu.roll(b, 48, 1), pltpu.roll(b, 16, 1)),
                        ),
                    )
                )
            ends[n, 16 * pair : 16 * pair + 16, :] = coded(jnp.concatenate(halves, axis=0))
        return carry

    lax.fori_loop(0, BLOCKS, send, 0, unroll=True)
    for n, out in enumerate((out0, out1, out2, out3)):
        out[...] = ends[n]


def turn_kernel(in0, in1, in2, in3, out0, out1, out2, out3, got, sent):
    block = lax.axis_index("depth")
    tile = lax.axis_index("tile")
    for n, ref in enumerate((in0, in1, in2, in3)):
        got[block ^ n] = ref[...]
    sub = index((8, 128), 0)
    chunk = index((8, 128), 1) // 32
    for pair in range(ENDS // 4):
        whole = [
            got[d, 16 * pair : 16 * pair + 16, :].astype(jnp.int32).astype(F32) for d in range(4)
        ]
        halves = {t: [] for t in range(4)}
        for part in range(2):
            m = [x[8 * part : 8 * part + 8] for x in whole]
            lined = {}
            for par in range(2):
                for h in range(2):
                    z = [pltpu.roll(m[d], (32 * (d - 2 * par - h)) % 128, 1) for d in range(4)]
                    lined[par, h] = jnp.where(
                        chunk == 0,
                        z[0],
                        jnp.where(chunk == 1, z[1], jnp.where(chunk == 2, z[2], z[3])),
                    )
            for h in range(2):
                a, b = lined[0, h], lined[1, h]
                halves[2 * h].append(jnp.where(sub < 4, a, pltpu.roll(b, 4, 0)))
                halves[2 * h + 1].append(jnp.where(sub < 4, pltpu.roll(a, 4, 0), b))
        for t in range(4):
            sent[t, 16 * pair : 16 * pair + 16, :] = (
                jnp.concatenate(halves[t], axis=0).astype(jnp.int32).astype(I16)
            )
    for n, out in enumerate((out0, out1, out2, out3)):
        out[...] = sent[(tile + n) % TILES]


def finish_kernel(in0, in1, in2, in3, state, land_sea, depth_index, out, got):
    block = lax.axis_index("depth")
    tile = lax.axis_index("tile")
    for n, ref in enumerate((in0, in1, in2, in3)):
        got[(tile + TILES - n) % TILES] = ref[...]
    wet_levels = jnp.where(land_sea[...] == 1, depth_index[...], 0)
    first = block * OWN_LEVELS
    left = index((16, 128), 1) < 64
    for q in range(4):
        half, west = divmod(q, 2)
        lanes = slice(128 * q, 128 * q + 128)
        values = []
        for pair in range(ENDS // 4):
            x, y = (wide(got[2 * west + i, 16 * pair : 16 * pair + 16, :]) for i in range(2))
            x = jnp.where(left, turn(x, 2 * half), turn(y, 2 - 2 * half))
            values += [x[0:4], x[4:8], x[8:12], x[12:16]]
        for t in range(2):
            base = t * (OWN_LEVELS + 1)
            unit = jnp.exp2(values[base + OWN_LEVELS]) * (1.0 / CODE)
            for k in range(OWN_LEVELS):
                wet = wet_levels[:, lanes] > first + k
                out[0, t, k, :, lanes] = jnp.where(
                    wet, values[base + k] * unit - state[0, t, k, :, lanes], 0.0
                )


def near(*arrays):
    return [pltpu.with_memory_space_constraint(x, pltpu.VMEM) for x in arrays]


def call(kernel, outs, scratch, *args, reserve=8, place=near):
    return pl.pallas_call(
        kernel,
        out_shape=outs,
        in_specs=[VMEM] * len(args),
        out_specs=jax.tree.map(lambda _: VMEM, outs),
        scratch_shapes=scratch,
        compiler_params=pltpu.CompilerParams(vmem_limit_bytes=reserve << 20),
    )(*place(*args))


def across_depth(messages):
    return [messages[0]] + [
        lax.ppermute(messages[n], "depth", [(i, i ^ n) for i in range(BLOCKS)])
        for n in range(1, BLOCKS)
    ]


def across_tiles(messages):
    return [messages[0]] + [
        lax.ppermute(messages[n], "tile", [(i, (i + n) % TILES) for i in range(TILES)])
        for n in range(1, TILES)
    ]


def window_shards(initial_states, velocity, growth, land_sea, depth_index, column_ops):
    message = pltpu.VMEM((4 * ENDS, 128), I16)
    slots = pltpu.VMEM((4, 4 * ENDS, 128), I16)
    cells = pltpu.VMEM((2 * 8 * PITCH, 128), F32)
    both = pltpu.VMEM((BOTH, 128), I16)
    sent = pltpu.VMEM((TILES, BOTH, 128), I16)
    across, *here = call(
        pack_kernel,
        [pltpu.VMEM((2 * MAIN + FIELDS, 128), I16)] + [both] * TILES,
        [pltpu.VMEM((MAIN, 512), F32), sent],
        initial_states,
        velocity,
        growth,
        land_sea,
        depth_index,
        reserve=60,
        place=lambda *args: args,
    )
    across = lax.ppermute(across, "depth", [(i, i ^ CORES) for i in range(BLOCKS)])
    received = across_tiles(here)
    received += across_tiles(call(relay_kernel, [both] * TILES, [sent], across))
    others = call(core_kernel, pltpu.VMEM((2 * TILES * PIECE, 128), I16), [], *received)
    others = lax.ppermute(others, "depth", [(i, i ^ 1) for i in range(BLOCKS)])
    pieces = pltpu.VMEM((2 * TILES, PIECE, 128), I16)
    flow = pltpu.VMEM((2 * 8 * HALF, 128), F32)
    coef = pltpu.VMEM((HALF // 8, 8, 9, 8, 128), F32)
    loaded = call(
        own_kernel,
        [flow, coef, pltpu.VMEM((2, 8, 128), F32), pltpu.VMEM((2, PITCH, PITCH), jnp.bfloat16)],
        [pieces, flow],
        *received,
        column_ops,
    )
    out = call(
        steps_kernel,
        [message] * 4,
        [pieces, cells, cells, cells, flow, coef, pltpu.VMEM((PITCH, 128), F32), slots],
        others,
        *loaded,
        reserve=16,
    )
    turned = call(turn_kernel, [message] * 4, [slots] * 2, *across_depth(out))
    segs = lax.axis_size("seg")
    last = [
        lax.ppermute(
            turned[n],
            ("seg", "tile"),
            [
                (s * TILES + t, ((s + 1) % segs) * TILES + (t + n) % TILES)
                for s in range(segs)
                for t in range(TILES)
            ],
        )
        for n in range(4)
    ]
    return call(
        finish_kernel,
        jax.ShapeDtypeStruct(initial_states.shape, F32),
        [slots],
        *last,
        initial_states,
        land_sea,
        depth_index,
    )


def shards(initial_states, velocity, growth, land_sea, depth_index, column_ops):
    fits = (
        lax.axis_size("tile") == TILES
        and lax.axis_size("depth") == BLOCKS
        and initial_states.shape == (1, 2, OWN_LEVELS, 4, TILES * BLOCKS * OWN)
    )
    plan = window_shards if fits else stepwise_shards
    return plan(initial_states, velocity, growth, land_sea, depth_index, column_ops)


def solution(mesh):
    return jax.shard_map(
        shards,
        mesh=mesh,
        in_specs=(
            P("seg", None, "depth", "tile", None),
            P("seg", None, "depth", "tile", None),
            P("seg", "tile", None),
            P("tile", None),
            P("tile", None),
            P(),
        ),
        out_specs=P("seg", None, "depth", "tile", None),
        check_vma=False,
    )
```

```python
import jax
import jax.numpy as jnp
from jax import lax
from jax.experimental import pallas as pl
from jax.experimental.pallas import tpu as pltpu
from jax.sharding import PartitionSpec as P

STEPS = 4


half_sat_sq = 0.25
remin_rate = 0.2


def with_halo(cells, sides, width):
    for axis, dim in sides:
        count = lax.axis_size(axis)
        ends = count - 1
        head = lax.slice_in_dim(cells, 0, width, axis=dim)
        tail = lax.slice_in_dim(cells, cells.shape[dim] - width, cells.shape[dim], axis=dim)
        cells = jnp.concatenate(
            [
                lax.ppermute(tail, axis, [(i, (i + 1) % count) for i in range(ends)]),
                cells,
                lax.ppermute(head, axis, [((i + 1) % count, i) for i in range(ends)]),
            ],
            axis=dim,
        )
    return cells


def passed_along(block, axis, distance):
    devices = range(lax.axis_size(axis))
    route = [((i - distance) % len(devices), i) for i in devices]
    return lax.ppermute(block, axis, route)


def face_flux(behind, near_side, far_side, beyond, courant):
    return (
        courant * (7.0 * (near_side + far_side) - (behind + beyond)) / 12.0
        - jnp.abs(courant) * (3.0 * (far_side - near_side) - (beyond - behind)) / 12.0
    )


def tendency(padded, north_faces, east_faces):
    merid = face_flux(
        padded[..., :-3, :],
        padded[..., 1:-2, :],
        padded[..., 2:-1, :],
        padded[..., 3:, :],
        north_faces,
    )
    centre = padded[..., 2:-2, :]
    zonal_flux = face_flux(
        jnp.roll(centre, 1, axis=-1),
        centre,
        jnp.roll(centre, -1, axis=-1),
        jnp.roll(centre, -2, axis=-1),
        east_faces,
    )
    return merid[..., :-1, :] - merid[..., 1:, :] + (jnp.roll(zonal_flux, 1, axis=-1) - zonal_flux)


def biology(mixed, rate, light_level, wet_cells):
    phosphate = mixed[..., 0, :, :, :]
    particles = mixed[..., 1, :, :, :]
    uptake = (
        rate
        * light_level
        * phosphate
        * phosphate
        * phosphate
        / (phosphate * phosphate + half_sat_sq)
    )
    return jnp.stack(
        [
            wet_cells * (phosphate - uptake + remin_rate * particles),
            wet_cells * (particles + uptake - remin_rate * particles),
        ],
        axis=-4,
    )


def stepwise_shards(initial_states, velocity, growth, land_sea, depth_index, column_ops):
    seg_dev = initial_states.shape[0]
    lev_dev = initial_states.shape[2]
    first_level = lax.axis_index("depth") * lev_dev
    levels = first_level + lax.iota(jnp.int32, lev_dev)
    wet_cells = jnp.where(
        (land_sea[None] == 1) & (levels[:, None, None] < depth_index[None]), 1.0, 0.0
    ).astype(jnp.float32)
    light_level = jnp.exp(-4.0 * levels.astype(jnp.float32) / column_ops.shape[1])[:, None, None]
    own_rows = lax.dynamic_slice_in_dim(column_ops, first_level, lev_dev, 1)
    uptake_rate = growth[:, None]
    tracer_state = wet_cells * initial_states
    flow_stack = jnp.concatenate([velocity[:, 0], velocity[:, 1], wet_cells[None]], axis=0)
    flow_edges = with_halo(flow_stack, (("tile", 2),), 3)
    wet_edges = flow_edges[2 * seg_dev]
    north_wide = (flow_edges[seg_dev : 2 * seg_dev, :, :-1] * wet_edges[:, :-1] * wet_edges[:, 1:])[
        :, None
    ]
    wet_wide = wet_edges[:, 1:-1]
    east_wide = (flow_edges[:seg_dev, :, 1:-1] * wet_wide * jnp.roll(wet_wide, -1, axis=-1))[
        :, None
    ]
    north_faces = north_wide[:, :, :, 2:-2]
    east_faces = east_wide[:, :, :, 2:-2]
    for step_index in range(STEPS):
        padded = with_halo(tracer_state, (("tile", 3),), 4)
        first_section = wet_wide * (padded[:, :, :, 2:-2] + tendency(padded, north_wide, east_wide))
        advected = wet_cells * (
            0.5 * tracer_state
            + 0.5
            * (first_section[:, :, :, 2:-2] + tendency(first_section, north_faces, east_faces))
        )
        rounded = advected.astype(jnp.bfloat16)
        mixed = jnp.einsum(
            "tkm,stmrl->stkrl",
            own_rows,
            lax.all_gather(rounded, "depth", axis=2, tiled=True),
            preferred_element_type=jnp.float32,
        )
        tracer_state = biology(wet_cells * mixed, uptake_rate, light_level, wet_cells)
    previous = passed_along(tracer_state, "seg", 1)
    before = jnp.concatenate([previous, tracer_state[: seg_dev - 1]], axis=0)
    return wet_cells * (before - initial_states)


TILES = 4
BLOCKS = 4
LEVELS = 76
OWN_LEVELS = LEVELS // BLOCKS
PITCH = 80
HALF = PITCH // 2
OWN = 32
REACH = 4 * STEPS
WINDOW = OWN + 2 * REACH
CODE = 32000.0
FASTEST = 0.35
FIELDS = 4 * OWN_LEVELS + 4
ENDS = 2 * OWN_LEVELS + 2
PIECE = 2 * FIELDS
MAIN = 4 * FIELDS
BOTH = PIECE + FIELDS
CORES = 2

F32 = jnp.float32
I16 = jnp.int16
VMEM = pl.BlockSpec(memory_space=pltpu.VMEM)


def coded(values):
    return jnp.floor(values + 0.5).astype(jnp.int32).astype(I16)


def exponent(largest):
    return jnp.clip(jnp.ceil(jnp.log2(jnp.maximum(largest, 1e-36))), -119.0, 125.0)


def index(shape, dim):
    return lax.broadcasted_iota(jnp.int32, shape, dim)


def pack_kernel(state, velocity, growth, land_sea, depth_index, *refs):
    (out, *outs), (turned, sent) = refs[:-2], refs[-2:]
    scales = []
    for t in range(2):
        largest = jnp.abs(state[0, t, 0])
        for k in range(1, OWN_LEVELS):
            largest = jnp.maximum(largest, jnp.abs(state[0, t, k]))
        scales.append(exponent(largest))
    per_unit = [CODE * jnp.exp2(-e) for e in scales]
    wet_levels = jnp.where(land_sea[...] == 1, depth_index[...], 0).astype(F32)

    def field(n):
        which, k = divmod(n, OWN_LEVELS)
        if which < 2:
            return state[0, which, k] * per_unit[which]
        if which < 4:
            return velocity[0, which - 2, k] * (CODE / FASTEST)
        return [growth[0] * CODE, wet_levels, scales[0], scales[1]][k]

    for pair in range(FIELDS // 2):
        rows = jnp.concatenate([field(2 * pair), field(2 * pair + 1)], axis=0)
        turned[8 * pair : 8 * pair + 8, :] = pltpu.roll(rows, REACH, 1)
    half = lax.axis_index("depth") // CORES

    def part_of(side):
        def part(lanes, row, count):
            at = pl.ds(pl.multiple_of(128 * ((2 * side + lanes) % 4), 128), 128)
            return turned[row : row + count, at]

        return part

    other = part_of(1 - half)
    for lanes in range(2):
        for row in range(0, MAIN, 16):
            out[MAIN * lanes + row : MAIN * lanes + row + 16, :] = coded(other(lanes, row, 16))
    for pair in range(FIELDS // 16):
        row = 2 * MAIN + 16 * pair
        out[row : row + 16, :] = coded(tails(other, TILES - 1, pair))
    windows(part_of(half), coded, None, sent, outs)


def tails(part, t, pair):
    chunk = index((8, 128), 1) // 32
    lanes, first = (t + 1) // 2, 2 * ((t + 1) % 2)
    blocks = []
    for group in (2 * pair, 2 * pair + 1):
        late = group + FIELDS // 8
        rows = (2 * late, 2 * group, 2 * late + 1, 2 * group + 1)
        blocks.append(
            by_chunk(chunk, [turn(part(lanes, 8 * i, 8), n - first) for n, i in enumerate(rows)])
        )
    return jnp.concatenate(blocks, axis=0)


def turn(block, chunks):
    return pltpu.roll(block, (32 * chunks) % 128, 1) if chunks % 4 else block


def windows(part, packed, last, sent, outs):
    left = index((8, 128), 1) < 64
    for t in range(TILES):
        for pair in range(FIELDS // 8):
            blocks = []
            for group in (2 * pair, 2 * pair + 1):
                lo, hi = (part(t // 2, 8 * i, 8) for i in (2 * group, 2 * group + 1))
                lo, hi = turn(lo, 2 * (t % 2)), turn(hi, 2 - 2 * (t % 2))
                blocks.append(jnp.where(left, lo, hi))
            sent[t, 16 * pair : 16 * pair + 16, :] = packed(jnp.concatenate(blocks, axis=0))
        for pair in range(FIELDS // 16):
            row = PIECE + 16 * pair
            if t == TILES - 1 and last is not None:
                sent[t, row : row + 16, :] = last(pair)
            else:
                sent[t, row : row + 16, :] = packed(tails(part, t, pair))
    tile = lax.axis_index("tile")
    for n, out in enumerate(outs):
        out[...] = sent[(tile + n) % TILES]


def relay_kernel(ref, *refs):
    outs, sent = refs[:-1], refs[-1]

    def part(lanes, row, count):
        base = MAIN * lanes + row // 16 * 16
        skip = row % 16
        return wide(ref[base : base + 16, :])[skip : skip + count]

    def last(pair):
        row = 2 * MAIN + 16 * pair
        return ref[row : row + 16, :]

    windows(part, narrow, last, sent, outs)


def piece(ref, pair, core):
    main = wide(ref[16 * pair : 16 * pair + 16, :])
    row = PIECE + 16 * (pair % (FIELDS // 16))
    tail = wide(ref[row : row + 16, :])
    odd = index((16, 128), 1) // 32 % 2 == 1
    if pair < FIELDS // 16:
        second = jnp.where(odd, tail, turn(main, 3))
    else:
        second = jnp.where(odd, turn(tail, 1), turn(main, 3))
    return narrow(jnp.where(core == 0, main, second))


def core_kernel(*refs):
    sources, out = refs[:-1], refs[-1]
    core = lax.axis_index("depth") % CORES
    for i, ref in enumerate(sources):
        for pair in range(FIELDS // 8):
            row = PIECE * i + 16 * pair
            out[row : row + 16, :] = piece(ref, pair, 1 - core)


def by_chunk(chunk, values):
    return jnp.where(
        chunk == 0,
        values[0],
        jnp.where(chunk == 1, values[1], jnp.where(chunk == 2, values[2], values[3])),
    )


def wide(values):
    return values.astype(jnp.int32).astype(F32)


def narrow(values):
    return values.astype(jnp.int32).astype(I16)


def levels_of(row, half):
    return jnp.where(row < 2 * OWN_LEVELS, row + 2 * OWN_LEVELS * half, 4 * LEVELS)


def level_rows(shape, half):
    row = index(shape, 0)
    return jnp.where(row < HALF, levels_of(row, half), levels_of(row - HALF, 1 - half))


def gather(recv, tiles, others):
    tile = lax.axis_index("tile")
    core = lax.axis_index("depth") % CORES
    for distance, ref in enumerate(tiles):
        to = CORES * ((tile + TILES - distance) % TILES)
        for pair in range(FIELDS // 8):
            recv[to + core, 16 * pair : 16 * pair + 16, :] = piece(ref, pair, core)
        recv[to + 1 - core] = others[PIECE * distance : PIECE * distance + PIECE, :]


def load_half(recv, side, cells, pitch, base, flow, coef, plane, fresh):
    sub = index((8, 128), 0)
    left = index((8, 128), 1) < 64
    cells_at, flow_at = (pitch, base), (HALF, 0)

    def spread(x, pair):
        sent = [wide(recv[2 * t + x, 16 * pair : 16 * pair + 16, :]) for t in range(TILES)]
        fields = []
        for part in range(2):
            m = [y[8 * part : 8 * part + 8] for y in sent]
            up, across = {}, {}
            for h in range(2):
                a, b = m[2 * h], m[2 * h + 1]
                up[0, h] = jnp.where(sub < 4, a, pltpu.roll(b, 4, 0))
                up[1, h] = jnp.where(sub < 4, pltpu.roll(a, 4, 0), b)
            for p in range(2):
                a, b = up[p, 0], up[p, 1]
                across[p, 0] = jnp.where(left, a, pltpu.roll(b, 64, 1))
                across[p, 1] = jnp.where(left, pltpu.roll(a, 64, 1), b)
            fields += [across[0, 0], across[1, 0], across[0, 1], across[1, 1]]
        return fields

    def take(x, carry):
        last = spread(x, FIELDS // 8 - 1)
        if fresh:
            plane[0] = last[4] * (1.0 / CODE)
            plane[1] = last[5]
        unit = [jnp.exp2(last[6 + t]) * (1.0 / CODE) for t in range(2)]
        for pair in range(FIELDS // 8):
            fields = last if pair == FIELDS // 8 - 1 else spread(x, pair)
            for i, value in enumerate(fields):
                which, k = divmod(8 * pair + i, OWN_LEVELS)
                row = OWN_LEVELS * x + k
                if which < 2:
                    to = pl.ds(which * 8 * pitch + base + row, 8, stride=pitch)
                    cells[to, :] = value * unit[which]
                elif which < 4:
                    to = pl.ds((which - 2) * 8 * HALF + row, 8, stride=HALF)
                    flow[to, :] = value * (FASTEST / CODE)
        return carry

    lax.fori_loop(0, BLOCKS // CORES, take, 0)

    def at(where, row, g):
        return pl.ds(pl.multiple_of(row * where[0] + where[1] + 8 * g, 8), 8)

    spare = jnp.zeros((HALF - 2 * OWN_LEVELS, 128), F32)
    for s in range(16):
        for field, where in ((cells, cells_at), (flow, flow_at)):
            end = s * where[0] + where[1] + HALF
            field[end - spare.shape[0] : end, :] = spare

    def faces(w):
        size = jnp.abs(w)
        return (
            (-w - size) * (1.0 / 12.0),
            (7.0 * w + 3.0 * size) * (1.0 / 12.0),
            (7.0 * w - 3.0 * size) * (1.0 / 12.0),
            (size - w) * (1.0 / 12.0),
        )

    def prepare(g, carry):
        level = levels_of(sub + 8 * g, side).astype(F32)
        wet = [jnp.where(plane[1, s : s + 1, :] > level, 1.0, 0.0) for s in range(8)]
        for t in range(2):
            for s in range(8):
                here = at(cells_at, 8 * t + s, g)
                cells[here, :] = wet[s] * cells[here, :]
        beyond = jnp.where(left, pltpu.roll(wet[0], 64, 1), 0.0)
        north_w = [
            flow[at(flow_at, 8 + s, g), :] * wet[s] * (wet[s + 1] if s < 7 else beyond) for s in range(8)
        ]
        first = jnp.where(left, 0.0, pltpu.roll(north_w[7], 64, 1))
        merid = [faces(w) for w in [first] + north_w]
        for s in range(8):
            east_w = flow[at(flow_at, s, g), :] * wet[s] * pltpu.roll(wet[s], 127, 1)
            a, b, d, e = faces(east_w)
            a1, b1, d1, e1 = faces(pltpu.roll(east_w, 1, 1))
            p1, q1, r1, s1 = merid[s]
            p, q, r, s0 = merid[s + 1]
            south = [wet[s] * p1, wet[s] * (q1 - p)]
            north = [wet[s] * (s1 - r), -wet[s] * s0]
            if s < 2:
                south[0] = jnp.where(left, 0.0, south[0])
            if s < 1:
                south[1] = jnp.where(left, 0.0, south[1])
            if s > 6:
                north[0] = jnp.where(left, north[0], 0.0)
            if s > 5:
                north[1] = jnp.where(left, north[1], 0.0)
            coef[g, s, 0] = wet[s] * (1.0 + (d1 - b) + (r1 - q))
            coef[g, s, 1] = wet[s] * a1
            coef[g, s, 2] = wet[s] * (b1 - a)
            coef[g, s, 3] = wet[s] * (e1 - d)
            coef[g, s, 4] = -wet[s] * e
            coef[g, s, 5], coef[g, s, 6] = south
            coef[g, s, 7], coef[g, s, 8] = north
        return carry

    lax.fori_loop(0, HALF // 8, prepare, 0, unroll=True)


def own_kernel(*refs):
    tiles, (others, ops, cells, coef, plane, ordered, recv, flow) = refs[:TILES], refs[TILES:]
    half = lax.axis_index("depth") // CORES
    gather(recv, tiles, others)
    load_half(recv, half, cells, HALF, 0, flow, coef, plane, True)
    shape = (PITCH, LEVELS)
    pick = jnp.where(level_rows(shape, half) == index(shape, 1), 1.0, 0.0).astype(jnp.bfloat16)
    for t in range(2):
        rows = jnp.dot(pick, ops[t], preferred_element_type=F32).astype(jnp.bfloat16)
        both = lax.dot_general(rows, pick, (((1,), (1,)), ((), ())), preferred_element_type=F32)
        ordered[t] = both.astype(jnp.bfloat16)


def steps_kernel(*refs):
    tiles, refs = refs[:TILES], refs[TILES:]
    (others, own_cells, own_coef, plane, ops, out0, out1, out2, out3), scratch = refs[:9], refs[9:]
    recv, cells, firsts, moved, flow, coef, light, ends = scratch
    own = lax.axis_index("depth")
    core, half = own % CORES, own // CORES
    gather(recv, tiles, others)
    load_half(recv, 1 - half, cells, PITCH, HALF, flow, coef, plane, False)
    for s in range(16):
        cells[PITCH * s : PITCH * s + HALF, :] = own_cells[HALF * s : HALF * s + HALF, :]
    lane = index((8, 128), 1)

    def block(base, g):
        return slice(base * PITCH + 8 * g, base * PITCH + 8 * g + 8)

    deep = level_rows((PITCH, 128), half).astype(F32)
    light[...] = jnp.exp(deep * (-4.0 / LEVELS))

    source_lane, lanes = index((256, 256), 0) % 128, index((256, 256), 1)
    shifts = jnp.where(
        lanes % 128 == (source_lane + jnp.where(lanes < 128, 2, 126)) % 128, 1.0, 0.0
    ).astype(jnp.bfloat16)

    def combine(c, near, far, two):
        centre = near[1]
        return (
            (c[0] * centre + c[6] * near[0] + c[7] * near[2])
            + (c[5] * far[0] + c[8] * far[1])
            + (c[2] * pltpu.roll(centre, 1, 1) + c[3] * pltpu.roll(centre, 127, 1))
            + (c[1] * two[0] + c[4] * two[1])
        )

    def stage(source, g, emit):
        def at(t, s):
            return source[block(8 * t + s, g), :]

        rows = jnp.concatenate([at(t, s) for t in range(2) for s in range(8)], axis=0)
        high = rows.astype(jnp.bfloat16)
        low = (rows - high.astype(F32)).astype(jnp.bfloat16)
        moves = jnp.dot(jnp.concatenate([high, low], axis=1), shifts, preferred_element_type=F32)

        columns = []
        for t in range(2):
            inner = [at(t, s) for s in range(8)]
            turned = [pltpu.roll(inner[s], 64, 1) for s in (6, 7, 0, 1)]
            columns.append(turned[:2] + inner + turned[2:])
        for s in range(8):
            stencil = own_coef.at[g, s] if g < HALF // 8 else coef.at[g - HALF // 8, s]
            c = [stencil[i] for i in range(9)]
            for t in range(2):
                k = columns[t]
                row = slice(8 * (8 * t + s), 8 * (8 * t + s) + 8)
                two = moves[row, :128], moves[row, 128:]
                emit(t, s, combine(c, k[s + 1 : s + 4], (k[s], k[s + 4]), two))

    def first_stage(g):
        def emit(t, s, value):
            firsts[block(8 * t + s, g), :] = value

        stage(cells, g, emit)

    def second_stage(g):
        def emit(t, s, value):
            at = block(8 * t + s, g)
            moved[at, :] = 0.5 * (cells[at, :] + value)

        stage(firsts, g, emit)

    def step(n, carry):
        for g in range(PITCH // 8 + 1):
            if g < PITCH // 8:
                first_stage(g)
            if g > 0:
                second_stage(g - 1)
        for pair in range(4):
            mixed = []
            for t in range(2):
                base = (t * 8 + 2 * pair) * PITCH
                both = jnp.concatenate(
                    [moved[base : base + PITCH, :], moved[base + PITCH : base + 2 * PITCH, :]], axis=1
                ).astype(jnp.bfloat16)
                mixed.append(jnp.dot(ops[t], both, preferred_element_type=F32))
            for i in range(2):
                s = 2 * pair + i
                wet = deep < plane[1, s : s + 1, :]
                p = jnp.where(wet, mixed[0][:, 128 * i : 128 * i + 128], 0.0)
                q = jnp.where(wet, mixed[1][:, 128 * i : 128 * i + 128], 0.0)
                square = p * p
                uptake = (plane[0, s : s + 1, :] * light[...]) * (
                    square * p / (square + half_sat_sq)
                )
                gain = uptake - remin_rate * q
                cells[s * PITCH : s * PITCH + PITCH, :] = p - gain
                cells[(8 + s) * PITCH : (8 + s) * PITCH + PITCH, :] = q + gain
        return carry

    lax.fori_loop(0, STEPS, step, 0)

    chunk = lane // 32

    def send(n, carry):
        first = HALF * (n // CORES) + OWN_LEVELS * (core ^ (n % CORES))
        blocks = []
        for t in range(2):
            def level(k):
                return cells[pl.ds(t * 8 * PITCH + first + k, 8, stride=PITCH), :]

            largest = jnp.abs(level(0))
            for k in range(1, OWN_LEVELS):
                largest = jnp.maximum(largest, jnp.abs(level(k)))
            scale = exponent(largest)
            per_unit = CODE * jnp.exp2(-scale)
            blocks += [level(k) * per_unit for k in range(OWN_LEVELS)] + [scale]
        for pair in range(ENDS // 4):
            halves = []
            for i in (2 * pair, 2 * pair + 1):
                a, b = blocks[2 * i], blocks[2 * i + 1]
                halves.append(
                    jnp.where(
                        chunk == 0,
                        pltpu.roll(a, 112, 1),
                        jnp.where(
                            chunk == 1,
                            pltpu.roll(a, 80, 1),
                            jnp.where(chunk == 2, pltpu.roll(b, 48, 1), pltpu.roll(b, 16, 1)),
                        ),
                    )
                )
            ends[n, 16 * pair : 16 * pair + 16, :] = coded(jnp.concatenate(halves, axis=0))
        return carry

    lax.fori_loop(0, BLOCKS, send, 0, unroll=True)
    for n, out in enumerate((out0, out1, out2, out3)):
        out[...] = ends[n]


def turn_kernel(in0, in1, in2, in3, out0, out1, out2, out3, got, sent):
    block = lax.axis_index("depth")
    tile = lax.axis_index("tile")
    for n, ref in enumerate((in0, in1, in2, in3)):
        got[block ^ n] = ref[...]
    sub = index((8, 128), 0)
    chunk = index((8, 128), 1) // 32
    for pair in range(ENDS // 4):
        whole = [
            got[d, 16 * pair : 16 * pair + 16, :].astype(jnp.int32).astype(F32) for d in range(4)
        ]
        halves = {t: [] for t in range(4)}
        for part in range(2):
            m = [x[8 * part : 8 * part + 8] for x in whole]
            lined = {}
            for par in range(2):
                for h in range(2):
                    z = [pltpu.roll(m[d], (32 * (d - 2 * par - h)) % 128, 1) for d in range(4)]
                    lined[par, h] = jnp.where(
                        chunk == 0,
                        z[0],
                        jnp.where(chunk == 1, z[1], jnp.where(chunk == 2, z[2], z[3])),
                    )
            for h in range(2):
                a, b = lined[0, h], lined[1, h]
                halves[2 * h].append(jnp.where(sub < 4, a, pltpu.roll(b, 4, 0)))
                halves[2 * h + 1].append(jnp.where(sub < 4, pltpu.roll(a, 4, 0), b))
        for t in range(4):
            sent[t, 16 * pair : 16 * pair + 16, :] = (
                jnp.concatenate(halves[t], axis=0).astype(jnp.int32).astype(I16)
            )
    for n, out in enumerate((out0, out1, out2, out3)):
        out[...] = sent[(tile + n) % TILES]


def finish_kernel(in0, in1, in2, in3, state, land_sea, depth_index, out, got):
    block = lax.axis_index("depth")
    tile = lax.axis_index("tile")
    for n, ref in enumerate((in0, in1, in2, in3)):
        got[(tile + TILES - n) % TILES] = ref[...]
    wet_levels = jnp.where(land_sea[...] == 1, depth_index[...], 0)
    first = block * OWN_LEVELS
    left = index((16, 128), 1) < 64
    for q in range(4):
        half, west = divmod(q, 2)
        lanes = slice(128 * q, 128 * q + 128)
        values = []
        for pair in range(ENDS // 4):
            x, y = (wide(got[2 * west + i, 16 * pair : 16 * pair + 16, :]) for i in range(2))
            x = jnp.where(left, turn(x, 2 * half), turn(y, 2 - 2 * half))
            values += [x[0:4], x[4:8], x[8:12], x[12:16]]
        for t in range(2):
            base = t * (OWN_LEVELS + 1)
            unit = jnp.exp2(values[base + OWN_LEVELS]) * (1.0 / CODE)
            for k in range(OWN_LEVELS):
                wet = wet_levels[:, lanes] > first + k
                out[0, t, k, :, lanes] = jnp.where(
                    wet, values[base + k] * unit - state[0, t, k, :, lanes], 0.0
                )


def near(*arrays):
    return [pltpu.with_memory_space_constraint(x, pltpu.VMEM) for x in arrays]


def call(kernel, outs, scratch, *args, reserve=8, place=near):
    return pl.pallas_call(
        kernel,
        out_shape=outs,
        in_specs=[VMEM] * len(args),
        out_specs=jax.tree.map(lambda _: VMEM, outs),
        scratch_shapes=scratch,
        compiler_params=pltpu.CompilerParams(vmem_limit_bytes=reserve << 20),
    )(*place(*args))


def across_depth(messages):
    return [messages[0]] + [
        lax.ppermute(messages[n], "depth", [(i, i ^ n) for i in range(BLOCKS)])
        for n in range(1, BLOCKS)
    ]


def across_tiles(messages):
    return [messages[0]] + [
        lax.ppermute(messages[n], "tile", [(i, (i + n) % TILES) for i in range(TILES)])
        for n in range(1, TILES)
    ]


def window_shards(initial_states, velocity, growth, land_sea, depth_index, column_ops):
    message = pltpu.VMEM((4 * ENDS, 128), I16)
    slots = pltpu.VMEM((4, 4 * ENDS, 128), I16)
    cells = pltpu.VMEM((2 * 8 * PITCH, 128), F32)
    both = pltpu.VMEM((BOTH, 128), I16)
    sent = pltpu.VMEM((TILES, BOTH, 128), I16)
    across, *here = call(
        pack_kernel,
        [pltpu.VMEM((2 * MAIN + FIELDS, 128), I16)] + [both] * TILES,
        [pltpu.VMEM((MAIN, 512), F32), sent],
        initial_states,
        velocity,
        growth,
        land_sea,
        depth_index,
        reserve=60,
        place=lambda *args: args,
    )
    across = lax.ppermute(across, "depth", [(i, i ^ CORES) for i in range(BLOCKS)])
    loaded = []
    for messages in (here, call(relay_kernel, [both] * TILES, [sent], across)):
        tiles = across_tiles(messages)
        others = call(core_kernel, pltpu.VMEM((TILES * PIECE, 128), I16), [], *tiles)
        others = lax.ppermute(others, "depth", [(i, i ^ 1) for i in range(BLOCKS)])
        loaded.append((*tiles, others))
    pieces = pltpu.VMEM((TILES * CORES, PIECE, 128), I16)
    flow = pltpu.VMEM((2 * 8 * HALF, 128), F32)
    coef = pltpu.VMEM((HALF // 8, 8, 9, 8, 128), F32)
    near_levels = call(
        own_kernel,
        [flow, coef, pltpu.VMEM((2, 8, 128), F32), pltpu.VMEM((2, PITCH, PITCH), jnp.bfloat16)],
        [pieces, flow],
        *loaded[0],
        column_ops,
    )
    out = call(
        steps_kernel,
        [message] * 4,
        [pieces, cells, cells, cells, flow, coef, pltpu.VMEM((PITCH, 128), F32), slots],
        *loaded[1],
        *near_levels,
        reserve=16,
    )
    turned = call(turn_kernel, [message] * 4, [slots] * 2, *across_depth(out))
    segs = lax.axis_size("seg")
    last = [
        lax.ppermute(
            turned[n],
            ("seg", "tile"),
            [
                (s * TILES + t, ((s + 1) % segs) * TILES + (t + n) % TILES)
                for s in range(segs)
                for t in range(TILES)
            ],
        )
        for n in range(4)
    ]
    return call(
        finish_kernel,
        jax.ShapeDtypeStruct(initial_states.shape, F32),
        [slots],
        *last,
        initial_states,
        land_sea,
        depth_index,
    )


def shards(initial_states, velocity, growth, land_sea, depth_index, column_ops):
    fits = (
        lax.axis_size("tile") == TILES
        and lax.axis_size("depth") == BLOCKS
        and initial_states.shape == (1, 2, OWN_LEVELS, 4, TILES * BLOCKS * OWN)
    )
    plan = window_shards if fits else stepwise_shards
    return plan(initial_states, velocity, growth, land_sea, depth_index, column_ops)


def solution(mesh):
    return jax.shard_map(
        shards,
        mesh=mesh,
        in_specs=(
            P("seg", None, "depth", "tile", None),
            P("seg", None, "depth", "tile", None),
            P("seg", "tile", None),
            P("tile", None),
            P("tile", None),
            P(),
        ),
        out_specs=P("seg", None, "depth", "tile", None),
        check_vma=False,
    )
```

```python
import jax
import jax.numpy as jnp
from jax import lax
from jax.experimental import pallas as pl
from jax.experimental.pallas import tpu as pltpu
from jax.sharding import PartitionSpec as P

STEPS = 4


half_sat_sq = 0.25
remin_rate = 0.2


def with_halo(cells, sides, width):
    for axis, dim in sides:
        count = lax.axis_size(axis)
        ends = count - 1
        head = lax.slice_in_dim(cells, 0, width, axis=dim)
        tail = lax.slice_in_dim(cells, cells.shape[dim] - width, cells.shape[dim], axis=dim)
        cells = jnp.concatenate(
            [
                lax.ppermute(tail, axis, [(i, (i + 1) % count) for i in range(ends)]),
                cells,
                lax.ppermute(head, axis, [((i + 1) % count, i) for i in range(ends)]),
            ],
            axis=dim,
        )
    return cells


def passed_along(block, axis, distance):
    devices = range(lax.axis_size(axis))
    route = [((i - distance) % len(devices), i) for i in devices]
    return lax.ppermute(block, axis, route)


def face_flux(behind, near_side, far_side, beyond, courant):
    return (
        courant * (7.0 * (near_side + far_side) - (behind + beyond)) / 12.0
        - jnp.abs(courant) * (3.0 * (far_side - near_side) - (beyond - behind)) / 12.0
    )


def tendency(padded, north_faces, east_faces):
    merid = face_flux(
        padded[..., :-3, :],
        padded[..., 1:-2, :],
        padded[..., 2:-1, :],
        padded[..., 3:, :],
        north_faces,
    )
    centre = padded[..., 2:-2, :]
    zonal_flux = face_flux(
        jnp.roll(centre, 1, axis=-1),
        centre,
        jnp.roll(centre, -1, axis=-1),
        jnp.roll(centre, -2, axis=-1),
        east_faces,
    )
    return merid[..., :-1, :] - merid[..., 1:, :] + (jnp.roll(zonal_flux, 1, axis=-1) - zonal_flux)


def biology(mixed, rate, light_level, wet_cells):
    phosphate = mixed[..., 0, :, :, :]
    particles = mixed[..., 1, :, :, :]
    uptake = (
        rate
        * light_level
        * phosphate
        * phosphate
        * phosphate
        / (phosphate * phosphate + half_sat_sq)
    )
    return jnp.stack(
        [
            wet_cells * (phosphate - uptake + remin_rate * particles),
            wet_cells * (particles + uptake - remin_rate * particles),
        ],
        axis=-4,
    )


def stepwise_shards(initial_states, velocity, growth, land_sea, depth_index, column_ops):
    seg_dev = initial_states.shape[0]
    lev_dev = initial_states.shape[2]
    first_level = lax.axis_index("depth") * lev_dev
    levels = first_level + lax.iota(jnp.int32, lev_dev)
    wet_cells = jnp.where(
        (land_sea[None] == 1) & (levels[:, None, None] < depth_index[None]), 1.0, 0.0
    ).astype(jnp.float32)
    light_level = jnp.exp(-4.0 * levels.astype(jnp.float32) / column_ops.shape[1])[:, None, None]
    own_rows = lax.dynamic_slice_in_dim(column_ops, first_level, lev_dev, 1)
    uptake_rate = growth[:, None]
    tracer_state = wet_cells * initial_states
    flow_stack = jnp.concatenate([velocity[:, 0], velocity[:, 1], wet_cells[None]], axis=0)
    flow_edges = with_halo(flow_stack, (("tile", 2),), 3)
    wet_edges = flow_edges[2 * seg_dev]
    north_wide = (flow_edges[seg_dev : 2 * seg_dev, :, :-1] * wet_edges[:, :-1] * wet_edges[:, 1:])[
        :, None
    ]
    wet_wide = wet_edges[:, 1:-1]
    east_wide = (flow_edges[:seg_dev, :, 1:-1] * wet_wide * jnp.roll(wet_wide, -1, axis=-1))[
        :, None
    ]
    north_faces = north_wide[:, :, :, 2:-2]
    east_faces = east_wide[:, :, :, 2:-2]
    for step_index in range(STEPS):
        padded = with_halo(tracer_state, (("tile", 3),), 4)
        first_section = wet_wide * (padded[:, :, :, 2:-2] + tendency(padded, north_wide, east_wide))
        advected = wet_cells * (
            0.5 * tracer_state
            + 0.5
            * (first_section[:, :, :, 2:-2] + tendency(first_section, north_faces, east_faces))
        )
        rounded = advected.astype(jnp.bfloat16)
        mixed = jnp.einsum(
            "tkm,stmrl->stkrl",
            own_rows,
            lax.all_gather(rounded, "depth", axis=2, tiled=True),
            preferred_element_type=jnp.float32,
        )
        tracer_state = biology(wet_cells * mixed, uptake_rate, light_level, wet_cells)
    previous = passed_along(tracer_state, "seg", 1)
    before = jnp.concatenate([previous, tracer_state[: seg_dev - 1]], axis=0)
    return wet_cells * (before - initial_states)


TILES = 4
BLOCKS = 4
LEVELS = 76
OWN_LEVELS = LEVELS // BLOCKS
PITCH = 80
HALF = PITCH // 2
OWN = 32
REACH = 4 * STEPS
WINDOW = OWN + 2 * REACH
CODE = 32000.0
FASTEST = 0.35
FIELDS = 4 * OWN_LEVELS + 4
ENDS = 2 * OWN_LEVELS + 2
PIECE = 2 * FIELDS
MAIN = 4 * FIELDS
BOTH = PIECE + FIELDS
CORES = 2

F32 = jnp.float32
I16 = jnp.int16
VMEM = pl.BlockSpec(memory_space=pltpu.VMEM)


def coded(values):
    return jnp.floor(values + 0.5).astype(jnp.int32).astype(I16)


def exponent(largest):
    return jnp.clip(jnp.ceil(jnp.log2(jnp.maximum(largest, 1e-30))), -99.0, 125.0)


def index(shape, dim):
    return lax.broadcasted_iota(jnp.int32, shape, dim)


def pack_kernel(state, velocity, growth, land_sea, depth_index, *refs):
    (out, *outs), (turned, sent) = refs[:-2], refs[-2:]
    scales = []
    for t in range(2):
        largest = jnp.abs(state[0, t, 0])
        for k in range(1, OWN_LEVELS):
            largest = jnp.maximum(largest, jnp.abs(state[0, t, k]))
        scales.append(exponent(largest))
    per_unit = [CODE * jnp.exp2(-e) for e in scales]
    wet_levels = jnp.where(land_sea[...] == 1, depth_index[...], 0).astype(F32)

    def field(n):
        which, k = divmod(n, OWN_LEVELS)
        if which < 2:
            return state[0, which, k] * per_unit[which]
        if which < 4:
            return velocity[0, which - 2, k] * (CODE / FASTEST)
        return [growth[0] * CODE, wet_levels, scales[0], scales[1]][k]

    for pair in range(FIELDS // 2):
        rows = jnp.concatenate([field(2 * pair), field(2 * pair + 1)], axis=0)
        turned[8 * pair : 8 * pair + 8, :] = pltpu.roll(rows, REACH, 1)
    half = lax.axis_index("depth") // CORES

    def part_of(side):
        def part(lanes, row, count):
            at = pl.ds(pl.multiple_of(128 * ((2 * side + lanes) % 4), 128), 128)
            return turned[row : row + count, at]

        return part

    other = part_of(1 - half)
    for lanes in range(2):
        for row in range(0, MAIN, 16):
            out[MAIN * lanes + row : MAIN * lanes + row + 16, :] = coded(other(lanes, row, 16))
    for pair in range(FIELDS // 16):
        row = 2 * MAIN + 16 * pair
        out[row : row + 16, :] = coded(tails(other, TILES - 1, pair))
    windows(part_of(half), coded, None, sent, outs)


def tails(part, t, pair):
    chunk = index((8, 128), 1) // 32
    lanes, first = (t + 1) // 2, 2 * ((t + 1) % 2)
    blocks = []
    for group in (2 * pair, 2 * pair + 1):
        late = group + FIELDS // 8
        rows = (2 * late, 2 * group, 2 * late + 1, 2 * group + 1)
        blocks.append(
            by_chunk(chunk, [turn(part(lanes, 8 * i, 8), n - first) for n, i in enumerate(rows)])
        )
    return jnp.concatenate(blocks, axis=0)


def turn(block, chunks):
    return pltpu.roll(block, (32 * chunks) % 128, 1) if chunks % 4 else block


def windows(part, packed, last, sent, outs):
    left = index((8, 128), 1) < 64
    for t in range(TILES):
        for pair in range(FIELDS // 8):
            blocks = []
            for group in (2 * pair, 2 * pair + 1):
                lo, hi = (part(t // 2, 8 * i, 8) for i in (2 * group, 2 * group + 1))
                lo, hi = turn(lo, 2 * (t % 2)), turn(hi, 2 - 2 * (t % 2))
                blocks.append(jnp.where(left, lo, hi))
            sent[t, 16 * pair : 16 * pair + 16, :] = packed(jnp.concatenate(blocks, axis=0))
        for pair in range(FIELDS // 16):
            row = PIECE + 16 * pair
            if t == TILES - 1 and last is not None:
                sent[t, row : row + 16, :] = last(pair)
            else:
                sent[t, row : row + 16, :] = packed(tails(part, t, pair))
    tile = lax.axis_index("tile")
    for n, out in enumerate(outs):
        out[...] = sent[(tile + n) % TILES]


def relay_kernel(ref, *refs):
    outs, sent = refs[:-1], refs[-1]

    def part(lanes, row, count):
        base = MAIN * lanes + row // 16 * 16
        skip = row % 16
        return wide(ref[base : base + 16, :])[skip : skip + count]

    def last(pair):
        row = 2 * MAIN + 16 * pair
        return ref[row : row + 16, :]

    windows(part, narrow, last, sent, outs)


def piece(ref, pair, core):
    main = wide(ref[16 * pair : 16 * pair + 16, :])
    row = PIECE + 16 * (pair % (FIELDS // 16))
    tail = wide(ref[row : row + 16, :])
    odd = index((16, 128), 1) // 32 % 2 == 1
    if pair < FIELDS // 16:
        second = jnp.where(odd, tail, turn(main, 3))
    else:
        second = jnp.where(odd, turn(tail, 1), turn(main, 3))
    return narrow(jnp.where(core == 0, main, second))


def core_kernel(*refs):
    sources, out = refs[:-1], refs[-1]
    core = lax.axis_index("depth") % CORES
    for i, ref in enumerate(sources):
        for pair in range(FIELDS // 8):
            row = PIECE * i + 16 * pair
            out[row : row + 16, :] = piece(ref, pair, 1 - core)


def by_chunk(chunk, values):
    return jnp.where(
        chunk == 0,
        values[0],
        jnp.where(chunk == 1, values[1], jnp.where(chunk == 2, values[2], values[3])),
    )


def wide(values):
    return values.astype(jnp.int32).astype(F32)


def narrow(values):
    return values.astype(jnp.int32).astype(I16)


def levels_of(row, half):
    return jnp.where(row < 2 * OWN_LEVELS, row + 2 * OWN_LEVELS * half, 4 * LEVELS)


def level_rows(shape, half):
    row = index(shape, 0)
    return jnp.where(row < HALF, levels_of(row, half), levels_of(row - HALF, 1 - half))


def gather(recv, tiles, others):
    tile = lax.axis_index("tile")
    core = lax.axis_index("depth") % CORES
    for distance, ref in enumerate(tiles):
        to = CORES * ((tile + TILES - distance) % TILES)
        for pair in range(FIELDS // 8):
            recv[to + core, 16 * pair : 16 * pair + 16, :] = piece(ref, pair, core)
        recv[to + 1 - core] = others[PIECE * distance : PIECE * distance + PIECE, :]


def load_half(recv, side, cells, pitch, base, flow, coef, plane, fresh):
    sub = index((8, 128), 0)
    left = index((8, 128), 1) < 64
    cells_at, flow_at = (pitch, base), (HALF, 0)

    def spread(x, pair):
        sent = [wide(recv[2 * t + x, 16 * pair : 16 * pair + 16, :]) for t in range(TILES)]
        fields = []
        for part in range(2):
            m = [y[8 * part : 8 * part + 8] for y in sent]
            up, across = {}, {}
            for h in range(2):
                a, b = m[2 * h], m[2 * h + 1]
                up[0, h] = jnp.where(sub < 4, a, pltpu.roll(b, 4, 0))
                up[1, h] = jnp.where(sub < 4, pltpu.roll(a, 4, 0), b)
            for p in range(2):
                a, b = up[p, 0], up[p, 1]
                across[p, 0] = jnp.where(left, a, pltpu.roll(b, 64, 1))
                across[p, 1] = jnp.where(left, pltpu.roll(a, 64, 1), b)
            fields += [across[0, 0], across[1, 0], across[0, 1], across[1, 1]]
        return fields

    def take(x, carry):
        last = spread(x, FIELDS // 8 - 1)
        if fresh:
            plane[0] = last[4] * (1.0 / CODE)
            plane[1] = last[5]
        unit = [jnp.exp2(last[6 + t]) * (1.0 / CODE) for t in range(2)]
        for pair in range(FIELDS // 8):
            fields = last if pair == FIELDS // 8 - 1 else spread(x, pair)
            for i, value in enumerate(fields):
                which, k = divmod(8 * pair + i, OWN_LEVELS)
                row = OWN_LEVELS * x + k
                if which < 2:
                    to = pl.ds(which * 8 * pitch + base + row, 8, stride=pitch)
                    cells[to, :] = value * unit[which]
                elif which < 4:
                    to = pl.ds((which - 2) * 8 * HALF + row, 8, stride=HALF)
                    flow[to, :] = value * (FASTEST / CODE)
        return carry

    lax.fori_loop(0, BLOCKS // CORES, take, 0)

    def at(where, row, g):
        return pl.ds(pl.multiple_of(row * where[0] + where[1] + 8 * g, 8), 8)

    spare = jnp.zeros((HALF - 2 * OWN_LEVELS, 128), F32)
    for s in range(16):
        for field, where in ((cells, cells_at), (flow, flow_at)):
            end = s * where[0] + where[1] + HALF
            field[end - spare.shape[0] : end, :] = spare

    def faces(w):
        size = jnp.abs(w)
        return (
            (-w - size) * (1.0 / 12.0),
            (7.0 * w + 3.0 * size) * (1.0 / 12.0),
            (7.0 * w - 3.0 * size) * (1.0 / 12.0),
            (size - w) * (1.0 / 12.0),
        )

    def prepare(g, carry):
        level = levels_of(sub + 8 * g, side).astype(F32)
        wet = [jnp.where(plane[1, s : s + 1, :] > level, 1.0, 0.0) for s in range(8)]
        for t in range(2):
            for s in range(8):
                here = at(cells_at, 8 * t + s, g)
                cells[here, :] = wet[s] * cells[here, :]
        beyond = jnp.where(left, pltpu.roll(wet[0], 64, 1), 0.0)
        north_w = [
            flow[at(flow_at, 8 + s, g), :] * wet[s] * (wet[s + 1] if s < 7 else beyond) for s in range(8)
        ]
        first = jnp.where(left, 0.0, pltpu.roll(north_w[7], 64, 1))
        merid = [faces(w) for w in [first] + north_w]
        for s in range(8):
            east_w = flow[at(flow_at, s, g), :] * wet[s] * pltpu.roll(wet[s], 127, 1)
            a, b, d, e = faces(east_w)
            a1, b1, d1, e1 = faces(pltpu.roll(east_w, 1, 1))
            p1, q1, r1, s1 = merid[s]
            p, q, r, s0 = merid[s + 1]
            south = [wet[s] * p1, wet[s] * (q1 - p)]
            north = [wet[s] * (s1 - r), -wet[s] * s0]
            if s < 2:
                south[0] = jnp.where(left, 0.0, south[0])
            if s < 1:
                south[1] = jnp.where(left, 0.0, south[1])
            if s > 6:
                north[0] = jnp.where(left, north[0], 0.0)
            if s > 5:
                north[1] = jnp.where(left, north[1], 0.0)
            coef[g, s, 0] = wet[s] * (1.0 + (d1 - b) + (r1 - q))
            coef[g, s, 1] = wet[s] * a1
            coef[g, s, 2] = wet[s] * (b1 - a)
            coef[g, s, 3] = wet[s] * (e1 - d)
            coef[g, s, 4] = -wet[s] * e
            coef[g, s, 5], coef[g, s, 6] = south
            coef[g, s, 7], coef[g, s, 8] = north
        return carry

    lax.fori_loop(0, HALF // 8, prepare, 0, unroll=True)


def own_kernel(*refs):
    tiles, (others, ops, cells, coef, plane, ordered, recv, flow) = refs[:TILES], refs[TILES:]
    half = lax.axis_index("depth") // CORES
    gather(recv, tiles, others)
    load_half(recv, half, cells, HALF, 0, flow, coef, plane, True)
    shape = (PITCH, LEVELS)
    pick = jnp.where(level_rows(shape, half) == index(shape, 1), 1.0, 0.0).astype(jnp.bfloat16)
    for t in range(2):
        rows = jnp.dot(pick, ops[t], preferred_element_type=F32).astype(jnp.bfloat16)
        both = lax.dot_general(rows, pick, (((1,), (1,)), ((), ())), preferred_element_type=F32)
        ordered[t] = both.astype(jnp.bfloat16)


def steps_kernel(*refs):
    tiles, refs = refs[:TILES], refs[TILES:]
    (others, own_cells, own_coef, plane, ops, out0, out1, out2, out3), scratch = refs[:9], refs[9:]
    recv, cells, firsts, moved, flow, coef, light, ends = scratch
    own = lax.axis_index("depth")
    core, half = own % CORES, own // CORES
    gather(recv, tiles, others)
    load_half(recv, 1 - half, cells, PITCH, HALF, flow, coef, plane, False)
    for s in range(16):
        cells[PITCH * s : PITCH * s + HALF, :] = own_cells[HALF * s : HALF * s + HALF, :]
    lane = index((8, 128), 1)

    def block(base, g):
        return slice(base * PITCH + 8 * g, base * PITCH + 8 * g + 8)

    deep = level_rows((PITCH, 128), half).astype(F32)
    light[...] = jnp.exp(deep * (-4.0 / LEVELS))

    source_lane, lanes = index((256, 256), 0) % 128, index((256, 256), 1)
    shifts = jnp.where(
        lanes % 128 == (source_lane + jnp.where(lanes < 128, 2, 126)) % 128, 1.0, 0.0
    ).astype(jnp.bfloat16)

    def combine(c, near, far, two):
        centre = near[1]
        return (
            (c[0] * centre + c[6] * near[0] + c[7] * near[2])
            + (c[5] * far[0] + c[8] * far[1])
            + (c[2] * pltpu.roll(centre, 1, 1) + c[3] * pltpu.roll(centre, 127, 1))
            + (c[1] * two[0] + c[4] * two[1])
        )

    def stage(source, gs, emit):
        def at(t, s, g):
            return source[block(8 * t + s, g), :]

        rows = jnp.concatenate(
            [at(t, s, g) for g in gs for t in range(2) for s in range(8)], axis=0
        )
        high = rows.astype(jnp.bfloat16)
        low = (rows - high.astype(F32)).astype(jnp.bfloat16)
        moves = jnp.dot(jnp.concatenate([high, low], axis=1), shifts, preferred_element_type=F32)
        for i, g in enumerate(gs):
            columns = []
            for t in range(2):
                inner = [at(t, s, g) for s in range(8)]
                turned = [pltpu.roll(inner[s], 64, 1) for s in (6, 7, 0, 1)]
                columns.append(turned[:2] + inner + turned[2:])
            for s in range(8):
                stencil = own_coef.at[g, s] if g < HALF // 8 else coef.at[g - HALF // 8, s]
                c = [stencil[i] for i in range(9)]
                for t in range(2):
                    k = columns[t]
                    first = 128 * i + 8 * (8 * t + s)
                    row = slice(first, first + 8)
                    two = moves[row, :128], moves[row, 128:]
                    emit(t, s, g, combine(c, k[s + 1 : s + 4], (k[s], k[s + 4]), two))

    def first_stage(gs):
        def emit(t, s, g, value):
            firsts[block(8 * t + s, g), :] = value

        stage(cells, gs, emit)

    def second_stage(gs):
        def emit(t, s, g, value):
            at = block(8 * t + s, g)
            moved[at, :] = 0.5 * (cells[at, :] + value)

        stage(firsts, gs, emit)

    def step(n, carry):
        sets = [tuple(range(g, g + 2)) for g in range(0, PITCH // 8, 2)]
        for i in range(len(sets) + 1):
            if i < len(sets):
                first_stage(sets[i])
            if i > 0:
                second_stage(sets[i - 1])
        for pair in range(4):
            mixed = []
            for t in range(2):
                base = (t * 8 + 2 * pair) * PITCH
                both = jnp.concatenate(
                    [moved[base : base + PITCH, :], moved[base + PITCH : base + 2 * PITCH, :]], axis=1
                ).astype(jnp.bfloat16)
                mixed.append(jnp.dot(ops[t], both, preferred_element_type=F32))
            for i in range(2):
                s = 2 * pair + i
                wet = deep < plane[1, s : s + 1, :]
                p = jnp.where(wet, mixed[0][:, 128 * i : 128 * i + 128], 0.0)
                q = jnp.where(wet, mixed[1][:, 128 * i : 128 * i + 128], 0.0)
                square = p * p
                uptake = (plane[0, s : s + 1, :] * light[...]) * (
                    square * p / (square + half_sat_sq)
                )
                gain = uptake - remin_rate * q
                cells[s * PITCH : s * PITCH + PITCH, :] = p - gain
                cells[(8 + s) * PITCH : (8 + s) * PITCH + PITCH, :] = q + gain
        return carry

    lax.fori_loop(0, STEPS, step, 0)

    chunk = lane // 32

    def send(n, carry):
        first = HALF * (n // CORES) + OWN_LEVELS * (core ^ (n % CORES))
        blocks = []
        for t in range(2):
            def level(k):
                return cells[pl.ds(t * 8 * PITCH + first + k, 8, stride=PITCH), :]

            largest = jnp.abs(level(0))
            for k in range(1, OWN_LEVELS):
                largest = jnp.maximum(largest, jnp.abs(level(k)))
            scale = exponent(largest)
            per_unit = CODE * jnp.exp2(-scale)
            blocks += [level(k) * per_unit for k in range(OWN_LEVELS)] + [scale]
        for pair in range(ENDS // 4):
            halves = []
            for i in (2 * pair, 2 * pair + 1):
                a, b = blocks[2 * i], blocks[2 * i + 1]
                halves.append(
                    jnp.where(
                        chunk == 0,
                        pltpu.roll(a, 112, 1),
                        jnp.where(
                            chunk == 1,
                            pltpu.roll(a, 80, 1),
                            jnp.where(chunk == 2, pltpu.roll(b, 48, 1), pltpu.roll(b, 16, 1)),
                        ),
                    )
                )
            ends[n, 16 * pair : 16 * pair + 16, :] = coded(jnp.concatenate(halves, axis=0))
        return carry

    lax.fori_loop(0, BLOCKS, send, 0, unroll=True)
    for n, out in enumerate((out0, out1, out2, out3)):
        out[...] = ends[n]


def turn_kernel(in0, in1, in2, in3, out0, out1, out2, out3, got, sent):
    block = lax.axis_index("depth")
    tile = lax.axis_index("tile")
    for n, ref in enumerate((in0, in1, in2, in3)):
        got[block ^ n] = ref[...]
    sub = index((8, 128), 0)
    chunk = index((8, 128), 1) // 32
    for pair in range(ENDS // 4):
        whole = [
            got[d, 16 * pair : 16 * pair + 16, :].astype(jnp.int32).astype(F32) for d in range(4)
        ]
        halves = {t: [] for t in range(4)}
        for part in range(2):
            m = [x[8 * part : 8 * part + 8] for x in whole]
            lined = {}
            for par in range(2):
                for h in range(2):
                    z = [pltpu.roll(m[d], (32 * (d - 2 * par - h)) % 128, 1) for d in range(4)]
                    lined[par, h] = jnp.where(
                        chunk == 0,
                        z[0],
                        jnp.where(chunk == 1, z[1], jnp.where(chunk == 2, z[2], z[3])),
                    )
            for h in range(2):
                a, b = lined[0, h], lined[1, h]
                halves[2 * h].append(jnp.where(sub < 4, a, pltpu.roll(b, 4, 0)))
                halves[2 * h + 1].append(jnp.where(sub < 4, pltpu.roll(a, 4, 0), b))
        for t in range(4):
            sent[t, 16 * pair : 16 * pair + 16, :] = (
                jnp.concatenate(halves[t], axis=0).astype(jnp.int32).astype(I16)
            )
    for n, out in enumerate((out0, out1, out2, out3)):
        out[...] = sent[(tile + n) % TILES]


def finish_kernel(in0, in1, in2, in3, state, land_sea, depth_index, out, got):
    block = lax.axis_index("depth")
    tile = lax.axis_index("tile")
    for n, ref in enumerate((in0, in1, in2, in3)):
        got[(tile + TILES - n) % TILES] = ref[...]
    wet_levels = jnp.where(land_sea[...] == 1, depth_index[...], 0)
    first = block * OWN_LEVELS
    left = index((16, 128), 1) < 64
    for q in range(4):
        half, west = divmod(q, 2)
        lanes = slice(128 * q, 128 * q + 128)
        values = []
        for pair in range(ENDS // 4):
            x, y = (wide(got[2 * west + i, 16 * pair : 16 * pair + 16, :]) for i in range(2))
            x = jnp.where(left, turn(x, 2 * half), turn(y, 2 - 2 * half))
            values += [x[0:4], x[4:8], x[8:12], x[12:16]]
        for t in range(2):
            base = t * (OWN_LEVELS + 1)
            unit = jnp.exp2(values[base + OWN_LEVELS]) * (1.0 / CODE)
            for k in range(OWN_LEVELS):
                wet = wet_levels[:, lanes] > first + k
                out[0, t, k, :, lanes] = jnp.where(
                    wet, values[base + k] * unit - state[0, t, k, :, lanes], 0.0
                )


def near(*arrays):
    return [pltpu.with_memory_space_constraint(x, pltpu.VMEM) for x in arrays]


def call(kernel, outs, scratch, *args, reserve=8, place=near):
    return pl.pallas_call(
        kernel,
        out_shape=outs,
        in_specs=[VMEM] * len(args),
        out_specs=jax.tree.map(lambda _: VMEM, outs),
        scratch_shapes=scratch,
        compiler_params=pltpu.CompilerParams(vmem_limit_bytes=reserve << 20),
    )(*place(*args))


def across_depth(messages):
    return [messages[0]] + [
        lax.ppermute(messages[n], "depth", [(i, i ^ n) for i in range(BLOCKS)])
        for n in range(1, BLOCKS)
    ]


def across_tiles(messages):
    return [messages[0]] + [
        lax.ppermute(messages[n], "tile", [(i, (i + n) % TILES) for i in range(TILES)])
        for n in range(1, TILES)
    ]


def window_shards(initial_states, velocity, growth, land_sea, depth_index, column_ops):
    message = pltpu.VMEM((4 * ENDS, 128), I16)
    slots = pltpu.VMEM((4, 4 * ENDS, 128), I16)
    cells = pltpu.VMEM((2 * 8 * PITCH, 128), F32)
    both = pltpu.VMEM((BOTH, 128), I16)
    sent = pltpu.VMEM((TILES, BOTH, 128), I16)
    across, *here = call(
        pack_kernel,
        [pltpu.VMEM((2 * MAIN + FIELDS, 128), I16)] + [both] * TILES,
        [pltpu.VMEM((MAIN, 512), F32), sent],
        initial_states,
        velocity,
        growth,
        land_sea,
        depth_index,
        reserve=60,
        place=lambda *args: args,
    )
    across = lax.ppermute(across, "depth", [(i, i ^ CORES) for i in range(BLOCKS)])
    loaded = []
    for messages in (here, call(relay_kernel, [both] * TILES, [sent], across)):
        tiles = across_tiles(messages)
        others = call(core_kernel, pltpu.VMEM((TILES * PIECE, 128), I16), [], *tiles)
        others = lax.ppermute(others, "depth", [(i, i ^ 1) for i in range(BLOCKS)])
        loaded.append((*tiles, others))
    pieces = pltpu.VMEM((TILES * CORES, PIECE, 128), I16)
    flow = pltpu.VMEM((2 * 8 * HALF, 128), F32)
    coef = pltpu.VMEM((HALF // 8, 8, 9, 8, 128), F32)
    near_levels = call(
        own_kernel,
        [flow, coef, pltpu.VMEM((2, 8, 128), F32), pltpu.VMEM((2, PITCH, PITCH), jnp.bfloat16)],
        [pieces, flow],
        *loaded[0],
        column_ops,
    )
    out = call(
        steps_kernel,
        [message] * 4,
        [pieces, cells, cells, cells, flow, coef, pltpu.VMEM((PITCH, 128), F32), slots],
        *loaded[1],
        *near_levels,
        reserve=16,
    )
    turned = call(turn_kernel, [message] * 4, [slots] * 2, *across_depth(out))
    segs = lax.axis_size("seg")
    last = [
        lax.ppermute(
            turned[n],
            ("seg", "tile"),
            [
                (s * TILES + t, ((s + 1) % segs) * TILES + (t + n) % TILES)
                for s in range(segs)
                for t in range(TILES)
            ],
        )
        for n in range(4)
    ]
    return call(
        finish_kernel,
        jax.ShapeDtypeStruct(initial_states.shape, F32),
        [slots],
        *last,
        initial_states,
        land_sea,
        depth_index,
    )


def shards(initial_states, velocity, growth, land_sea, depth_index, column_ops):
    fits = (
        lax.axis_size("tile") == TILES
        and lax.axis_size("depth") == BLOCKS
        and initial_states.shape == (1, 2, OWN_LEVELS, 4, TILES * BLOCKS * OWN)
    )
    plan = window_shards if fits else stepwise_shards
    return plan(initial_states, velocity, growth, land_sea, depth_index, column_ops)


def solution(mesh):
    return jax.shard_map(
        shards,
        mesh=mesh,
        in_specs=(
            P("seg", None, "depth", "tile", None),
            P("seg", None, "depth", "tile", None),
            P("seg", "tile", None),
            P("tile", None),
            P("tile", None),
            P(),
        ),
        out_specs=P("seg", None, "depth", "tile", None),
        check_vma=False,
    )
```

```python
import jax
import jax.numpy as jnp
from jax import lax
from jax.experimental import pallas as pl
from jax.experimental.pallas import tpu as pltpu
from jax.sharding import PartitionSpec as P

STEPS = 4


half_sat_sq = 0.25
remin_rate = 0.2


def with_halo(cells, sides, width):
    for axis, dim in sides:
        count = lax.axis_size(axis)
        ends = count - 1
        head = lax.slice_in_dim(cells, 0, width, axis=dim)
        tail = lax.slice_in_dim(cells, cells.shape[dim] - width, cells.shape[dim], axis=dim)
        cells = jnp.concatenate(
            [
                lax.ppermute(tail, axis, [(i, (i + 1) % count) for i in range(ends)]),
                cells,
                lax.ppermute(head, axis, [((i + 1) % count, i) for i in range(ends)]),
            ],
            axis=dim,
        )
    return cells


def passed_along(block, axis, distance):
    devices = range(lax.axis_size(axis))
    route = [((i - distance) % len(devices), i) for i in devices]
    return lax.ppermute(block, axis, route)


def face_flux(behind, near_side, far_side, beyond, courant):
    return (
        courant * (7.0 * (near_side + far_side) - (behind + beyond)) / 12.0
        - jnp.abs(courant) * (3.0 * (far_side - near_side) - (beyond - behind)) / 12.0
    )


def tendency(padded, north_faces, east_faces):
    merid = face_flux(
        padded[..., :-3, :],
        padded[..., 1:-2, :],
        padded[..., 2:-1, :],
        padded[..., 3:, :],
        north_faces,
    )
    centre = padded[..., 2:-2, :]
    zonal_flux = face_flux(
        jnp.roll(centre, 1, axis=-1),
        centre,
        jnp.roll(centre, -1, axis=-1),
        jnp.roll(centre, -2, axis=-1),
        east_faces,
    )
    return merid[..., :-1, :] - merid[..., 1:, :] + (jnp.roll(zonal_flux, 1, axis=-1) - zonal_flux)


def biology(mixed, rate, light_level, wet_cells):
    phosphate = mixed[..., 0, :, :, :]
    particles = mixed[..., 1, :, :, :]
    uptake = (
        rate
        * light_level
        * phosphate
        * phosphate
        * phosphate
        / (phosphate * phosphate + half_sat_sq)
    )
    return jnp.stack(
        [
            wet_cells * (phosphate - uptake + remin_rate * particles),
            wet_cells * (particles + uptake - remin_rate * particles),
        ],
        axis=-4,
    )


def stepwise_shards(initial_states, velocity, growth, land_sea, depth_index, column_ops):
    seg_dev = initial_states.shape[0]
    lev_dev = initial_states.shape[2]
    first_level = lax.axis_index("depth") * lev_dev
    levels = first_level + lax.iota(jnp.int32, lev_dev)
    wet_cells = jnp.where(
        (land_sea[None] == 1) & (levels[:, None, None] < depth_index[None]), 1.0, 0.0
    ).astype(jnp.float32)
    light_level = jnp.exp(-4.0 * levels.astype(jnp.float32) / column_ops.shape[1])[:, None, None]
    own_rows = lax.dynamic_slice_in_dim(column_ops, first_level, lev_dev, 1)
    uptake_rate = growth[:, None]
    tracer_state = wet_cells * initial_states
    flow_stack = jnp.concatenate([velocity[:, 0], velocity[:, 1], wet_cells[None]], axis=0)
    flow_edges = with_halo(flow_stack, (("tile", 2),), 3)
    wet_edges = flow_edges[2 * seg_dev]
    north_wide = (flow_edges[seg_dev : 2 * seg_dev, :, :-1] * wet_edges[:, :-1] * wet_edges[:, 1:])[
        :, None
    ]
    wet_wide = wet_edges[:, 1:-1]
    east_wide = (flow_edges[:seg_dev, :, 1:-1] * wet_wide * jnp.roll(wet_wide, -1, axis=-1))[
        :, None
    ]
    north_faces = north_wide[:, :, :, 2:-2]
    east_faces = east_wide[:, :, :, 2:-2]
    for step_index in range(STEPS):
        padded = with_halo(tracer_state, (("tile", 3),), 4)
        first_section = wet_wide * (padded[:, :, :, 2:-2] + tendency(padded, north_wide, east_wide))
        advected = wet_cells * (
            0.5 * tracer_state
            + 0.5
            * (first_section[:, :, :, 2:-2] + tendency(first_section, north_faces, east_faces))
        )
        rounded = advected.astype(jnp.bfloat16)
        mixed = jnp.einsum(
            "tkm,stmrl->stkrl",
            own_rows,
            lax.all_gather(rounded, "depth", axis=2, tiled=True),
            preferred_element_type=jnp.float32,
        )
        tracer_state = biology(wet_cells * mixed, uptake_rate, light_level, wet_cells)
    previous = passed_along(tracer_state, "seg", 1)
    before = jnp.concatenate([previous, tracer_state[: seg_dev - 1]], axis=0)
    return wet_cells * (before - initial_states)


TILES = 4
BLOCKS = 4
LEVELS = 76
OWN_LEVELS = LEVELS // BLOCKS
PITCH = 80
HALF = PITCH // 2
OWN = 32
REACH = 4 * STEPS
WINDOW = OWN + 2 * REACH
CODE = 32000.0
FASTEST = 0.35
FIELDS = 4 * OWN_LEVELS + 4
ENDS = 2 * OWN_LEVELS + 2
PIECE = 2 * FIELDS
MAIN = 4 * FIELDS
BOTH = PIECE + FIELDS
CORES = 2

F32 = jnp.float32
I16 = jnp.int16
VMEM = pl.BlockSpec(memory_space=pltpu.VMEM)


def coded(values):
    return jnp.floor(values + 0.5).astype(jnp.int32).astype(I16)


def exponent(largest):
    return jnp.clip(jnp.ceil(jnp.log2(jnp.maximum(largest, 1e-30))), -99.0, 125.0)


def index(shape, dim):
    return lax.broadcasted_iota(jnp.int32, shape, dim)


def pack_kernel(state, velocity, growth, land_sea, depth_index, *refs):
    (out, *outs), (turned, sent) = refs[:-2], refs[-2:]
    scales = []
    for t in range(2):
        largest = jnp.abs(state[0, t, 0])
        for k in range(1, OWN_LEVELS):
            largest = jnp.maximum(largest, jnp.abs(state[0, t, k]))
        scales.append(exponent(largest))
    per_unit = [CODE * jnp.exp2(-e) for e in scales]
    wet_levels = jnp.where(land_sea[...] == 1, depth_index[...], 0).astype(F32)

    def field(n):
        which, k = divmod(n, OWN_LEVELS)
        if which < 2:
            return state[0, which, k] * per_unit[which]
        if which < 4:
            return velocity[0, which - 2, k] * (CODE / FASTEST)
        return [growth[0] * CODE, wet_levels, scales[0], scales[1]][k]

    for pair in range(FIELDS // 2):
        rows = jnp.concatenate([field(2 * pair), field(2 * pair + 1)], axis=0)
        turned[8 * pair : 8 * pair + 8, :] = pltpu.roll(rows, REACH, 1)
    half = lax.axis_index("depth") // CORES

    def part_of(side):
        def part(lanes, row, count):
            at = pl.ds(pl.multiple_of(128 * ((2 * side + lanes) % 4), 128), 128)
            return turned[row : row + count, at]

        return part

    other = part_of(1 - half)
    for lanes in range(2):
        for row in range(0, MAIN, 16):
            out[MAIN * lanes + row : MAIN * lanes + row + 16, :] = coded(other(lanes, row, 16))
    for pair in range(FIELDS // 16):
        row = 2 * MAIN + 16 * pair
        out[row : row + 16, :] = coded(tails(other, TILES - 1, pair))
    windows(part_of(half), coded, None, sent, outs)


def tails(part, t, pair):
    chunk = index((8, 128), 1) // 32
    lanes, first = (t + 1) // 2, 2 * ((t + 1) % 2)
    blocks = []
    for group in (2 * pair, 2 * pair + 1):
        late = group + FIELDS // 8
        rows = (2 * late, 2 * group, 2 * late + 1, 2 * group + 1)
        blocks.append(
            by_chunk(chunk, [turn(part(lanes, 8 * i, 8), n - first) for n, i in enumerate(rows)])
        )
    return jnp.concatenate(blocks, axis=0)


def turn(block, chunks):
    return pltpu.roll(block, (32 * chunks) % 128, 1) if chunks % 4 else block


def windows(part, packed, last, sent, outs):
    left = index((8, 128), 1) < 64
    for t in range(TILES):
        for pair in range(FIELDS // 8):
            blocks = []
            for group in (2 * pair, 2 * pair + 1):
                lo, hi = (part(t // 2, 8 * i, 8) for i in (2 * group, 2 * group + 1))
                lo, hi = turn(lo, 2 * (t % 2)), turn(hi, 2 - 2 * (t % 2))
                blocks.append(jnp.where(left, lo, hi))
            sent[t, 16 * pair : 16 * pair + 16, :] = packed(jnp.concatenate(blocks, axis=0))
        for pair in range(FIELDS // 16):
            row = PIECE + 16 * pair
            if t == TILES - 1 and last is not None:
                sent[t, row : row + 16, :] = last(pair)
            else:
                sent[t, row : row + 16, :] = packed(tails(part, t, pair))
    tile = lax.axis_index("tile")
    for n, out in enumerate(outs):
        out[...] = sent[(tile + n) % TILES]


def relay_kernel(ref, *refs):
    outs, sent = refs[:-1], refs[-1]

    def part(lanes, row, count):
        base = MAIN * lanes + row // 16 * 16
        skip = row % 16
        return wide(ref[base : base + 16, :])[skip : skip + count]

    def last(pair):
        row = 2 * MAIN + 16 * pair
        return ref[row : row + 16, :]

    windows(part, narrow, last, sent, outs)


def piece(ref, pair, core):
    main = wide(ref[16 * pair : 16 * pair + 16, :])
    row = PIECE + 16 * (pair % (FIELDS // 16))
    tail = wide(ref[row : row + 16, :])
    odd = index((16, 128), 1) // 32 % 2 == 1
    if pair < FIELDS // 16:
        second = jnp.where(odd, tail, turn(main, 3))
    else:
        second = jnp.where(odd, turn(tail, 1), turn(main, 3))
    return narrow(jnp.where(core == 0, main, second))


def core_kernel(*refs):
    sources, out = refs[:-1], refs[-1]
    core = lax.axis_index("depth") % CORES
    for i, ref in enumerate(sources):
        for pair in range(FIELDS // 8):
            row = PIECE * i + 16 * pair
            out[row : row + 16, :] = piece(ref, pair, 1 - core)


def by_chunk(chunk, values):
    return jnp.where(
        chunk == 0,
        values[0],
        jnp.where(chunk == 1, values[1], jnp.where(chunk == 2, values[2], values[3])),
    )


def wide(values):
    return values.astype(jnp.int32).astype(F32)


def narrow(values):
    return values.astype(jnp.int32).astype(I16)


def levels_of(row, half):
    return jnp.where(row < 2 * OWN_LEVELS, row + 2 * OWN_LEVELS * half, 4 * LEVELS)


def level_rows(shape, half):
    row = index(shape, 0)
    return jnp.where(row < HALF, levels_of(row, half), levels_of(row - HALF, 1 - half))


def gather(recv, tiles, others):
    tile = lax.axis_index("tile")
    core = lax.axis_index("depth") % CORES
    for distance, ref in enumerate(tiles):
        to = CORES * ((tile + TILES - distance) % TILES)
        for pair in range(FIELDS // 8):
            recv[to + core, 16 * pair : 16 * pair + 16, :] = piece(ref, pair, core)
        recv[to + 1 - core] = others[PIECE * distance : PIECE * distance + PIECE, :]


def load_half(recv, side, cells, pitch, base, flow, coef, plane, fresh):
    sub = index((8, 128), 0)
    left = index((8, 128), 1) < 64
    cells_at, flow_at = (pitch, base), (HALF, 0)

    def spread(x, pair):
        sent = [wide(recv[2 * t + x, 16 * pair : 16 * pair + 16, :]) for t in range(TILES)]
        fields = []
        for part in range(2):
            m = [y[8 * part : 8 * part + 8] for y in sent]
            up, across = {}, {}
            for h in range(2):
                a, b = m[2 * h], m[2 * h + 1]
                up[0, h] = jnp.where(sub < 4, a, pltpu.roll(b, 4, 0))
                up[1, h] = jnp.where(sub < 4, pltpu.roll(a, 4, 0), b)
            for p in range(2):
                a, b = up[p, 0], up[p, 1]
                across[p, 0] = jnp.where(left, a, pltpu.roll(b, 64, 1))
                across[p, 1] = jnp.where(left, pltpu.roll(a, 64, 1), b)
            fields += [across[0, 0], across[1, 0], across[0, 1], across[1, 1]]
        return fields

    def take(x, carry):
        last = spread(x, FIELDS // 8 - 1)
        if fresh:
            plane[0] = last[4] * (1.0 / CODE)
            plane[1] = last[5]
        unit = [jnp.exp2(last[6 + t]) * (1.0 / CODE) for t in range(2)]
        for pair in range(FIELDS // 8):
            fields = last if pair == FIELDS // 8 - 1 else spread(x, pair)
            for i, value in enumerate(fields):
                which, k = divmod(8 * pair + i, OWN_LEVELS)
                row = OWN_LEVELS * x + k
                if which < 2:
                    to = pl.ds(which * 8 * pitch + base + row, 8, stride=pitch)
                    cells[to, :] = value * unit[which]
                elif which < 4:
                    to = pl.ds((which - 2) * 8 * HALF + row, 8, stride=HALF)
                    flow[to, :] = value * (FASTEST / CODE)
        return carry

    lax.fori_loop(0, BLOCKS // CORES, take, 0)

    def at(where, row, g):
        return pl.ds(pl.multiple_of(row * where[0] + where[1] + 8 * g, 8), 8)

    spare = jnp.zeros((HALF - 2 * OWN_LEVELS, 128), F32)
    for s in range(16):
        for field, where in ((cells, cells_at), (flow, flow_at)):
            end = s * where[0] + where[1] + HALF
            field[end - spare.shape[0] : end, :] = spare

    def faces(w):
        size = jnp.abs(w)
        return (
            (-w - size) * (1.0 / 12.0),
            (7.0 * w + 3.0 * size) * (1.0 / 12.0),
            (7.0 * w - 3.0 * size) * (1.0 / 12.0),
            (size - w) * (1.0 / 12.0),
        )

    def prepare(g, carry):
        level = levels_of(sub + 8 * g, side).astype(F32)
        wet = [jnp.where(plane[1, s : s + 1, :] > level, 1.0, 0.0) for s in range(8)]
        for t in range(2):
            for s in range(8):
                here = at(cells_at, 8 * t + s, g)
                cells[here, :] = wet[s] * cells[here, :]
        beyond = jnp.where(left, pltpu.roll(wet[0], 64, 1), 0.0)
        north_w = [
            flow[at(flow_at, 8 + s, g), :] * wet[s] * (wet[s + 1] if s < 7 else beyond) for s in range(8)
        ]
        first = jnp.where(left, 0.0, pltpu.roll(north_w[7], 64, 1))
        merid = [faces(w) for w in [first] + north_w]
        for s in range(8):
            east_w = flow[at(flow_at, s, g), :] * wet[s] * pltpu.roll(wet[s], 127, 1)
            a, b, d, e = faces(east_w)
            a1, b1, d1, e1 = faces(pltpu.roll(east_w, 1, 1))
            p1, q1, r1, s1 = merid[s]
            p, q, r, s0 = merid[s + 1]
            south = [wet[s] * p1, wet[s] * (q1 - p)]
            north = [wet[s] * (s1 - r), -wet[s] * s0]
            if s < 2:
                south[0] = jnp.where(left, 0.0, south[0])
            if s < 1:
                south[1] = jnp.where(left, 0.0, south[1])
            if s > 6:
                north[0] = jnp.where(left, north[0], 0.0)
            if s > 5:
                north[1] = jnp.where(left, north[1], 0.0)
            coef[g, s, 0] = wet[s] * (1.0 + (d1 - b) + (r1 - q))
            coef[g, s, 1] = wet[s] * a1
            coef[g, s, 2] = wet[s] * (b1 - a)
            coef[g, s, 3] = wet[s] * (e1 - d)
            coef[g, s, 4] = -wet[s] * e
            coef[g, s, 5], coef[g, s, 6] = south
            coef[g, s, 7], coef[g, s, 8] = north
        return carry

    lax.fori_loop(0, HALF // 8, prepare, 0, unroll=True)


def own_kernel(*refs):
    tiles, (others, ops, cells, coef, plane, ordered, recv, flow) = refs[:TILES], refs[TILES:]
    half = lax.axis_index("depth") // CORES
    gather(recv, tiles, others)
    load_half(recv, half, cells, HALF, 0, flow, coef, plane, True)
    shape = (PITCH, LEVELS)
    pick = jnp.where(level_rows(shape, half) == index(shape, 1), 1.0, 0.0).astype(jnp.bfloat16)
    for t in range(2):
        rows = jnp.dot(pick, ops[t], preferred_element_type=F32).astype(jnp.bfloat16)
        both = lax.dot_general(rows, pick, (((1,), (1,)), ((), ())), preferred_element_type=F32)
        ordered[t] = both.astype(jnp.bfloat16)


def steps_kernel(*refs):
    tiles, refs = refs[:TILES], refs[TILES:]
    (others, own_cells, own_coef, plane, ops, out0, out1, out2, out3), scratch = refs[:9], refs[9:]
    recv, cells, firsts, moved, flow, coef, light, ends = scratch
    own = lax.axis_index("depth")
    core, half = own % CORES, own // CORES
    gather(recv, tiles, others)
    load_half(recv, 1 - half, cells, PITCH, HALF, flow, coef, plane, False)
    for s in range(16):
        cells[PITCH * s : PITCH * s + HALF, :] = own_cells[HALF * s : HALF * s + HALF, :]
    lane = index((8, 128), 1)

    def block(base, g):
        return slice(base * PITCH + 8 * g, base * PITCH + 8 * g + 8)

    deep = level_rows((PITCH, 128), half).astype(F32)
    light[...] = jnp.exp(deep * (-4.0 / LEVELS))

    source_lane, lanes = index((256, 256), 0) % 128, index((256, 256), 1)
    shifts = jnp.where(
        lanes % 128 == (source_lane + jnp.where(lanes < 128, 2, 126)) % 128, 1.0, 0.0
    ).astype(jnp.bfloat16)

    def combine(c, near, far, two):
        centre = near[1]
        return (
            (c[0] * centre + c[6] * near[0] + c[7] * near[2])
            + (c[5] * far[0] + c[8] * far[1])
            + (c[2] * pltpu.roll(centre, 1, 1) + c[3] * pltpu.roll(centre, 127, 1))
            + (c[1] * two[0] + c[4] * two[1])
        )

    def stage(source, gs, emit):
        def at(t, s, g):
            return source[block(8 * t + s, g), :]

        rows = jnp.concatenate(
            [at(t, s, g) for g in gs for t in range(2) for s in range(8)], axis=0
        )
        high = rows.astype(jnp.bfloat16)
        low = (rows - high.astype(F32)).astype(jnp.bfloat16)
        moves = jnp.dot(jnp.concatenate([high, low], axis=1), shifts, preferred_element_type=F32)
        for i, g in enumerate(gs):
            columns = []
            for t in range(2):
                inner = [at(t, s, g) for s in range(8)]
                turned = [pltpu.roll(inner[s], 64, 1) for s in (6, 7, 0, 1)]
                columns.append(turned[:2] + inner + turned[2:])
            for s in range(8):
                stencil = own_coef.at[g, s] if g < HALF // 8 else coef.at[g - HALF // 8, s]
                c = [stencil[i] for i in range(9)]
                for t in range(2):
                    k = columns[t]
                    first = 128 * i + 8 * (8 * t + s)
                    row = slice(first, first + 8)
                    two = moves[row, :128], moves[row, 128:]
                    emit(t, s, g, combine(c, k[s + 1 : s + 4], (k[s], k[s + 4]), two))

    def first_stage(gs):
        def emit(t, s, g, value):
            firsts[block(8 * t + s, g), :] = value

        stage(cells, gs, emit)

    def second_stage(gs):
        def emit(t, s, g, value):
            at = block(8 * t + s, g)
            moved[at, :] = 0.5 * (cells[at, :] + value)

        stage(firsts, gs, emit)

    def step(n, carry):
        sets = [tuple(range(g, g + 2)) for g in range(0, PITCH // 8, 2)]
        for i in range(len(sets) + 1):
            if i < len(sets):
                first_stage(sets[i])
            if i > 0:
                second_stage(sets[i - 1])
        for pair in range(4):
            mixed = []
            for t in range(2):
                base = (t * 8 + 2 * pair) * PITCH
                both = jnp.concatenate(
                    [moved[base : base + PITCH, :], moved[base + PITCH : base + 2 * PITCH, :]], axis=1
                ).astype(jnp.bfloat16)
                mixed.append(jnp.dot(ops[t], both, preferred_element_type=F32))
            for i in range(2):
                s = 2 * pair + i
                wet = deep < plane[1, s : s + 1, :]
                p = jnp.where(wet, mixed[0][:, 128 * i : 128 * i + 128], 0.0)
                q = jnp.where(wet, mixed[1][:, 128 * i : 128 * i + 128], 0.0)
                square = p * p
                uptake = (plane[0, s : s + 1, :] * light[...]) * (
                    square * p / (square + half_sat_sq)
                )
                gain = uptake - remin_rate * q
                cells[s * PITCH : s * PITCH + PITCH, :] = p - gain
                cells[(8 + s) * PITCH : (8 + s) * PITCH + PITCH, :] = q + gain
        return carry

    lax.fori_loop(0, STEPS, step, 0)

    chunk = lane // 32

    def send(n, carry):
        first = HALF * (n // CORES) + OWN_LEVELS * (core ^ (n % CORES))
        blocks = []
        for t in range(2):
            def level(k):
                return cells[pl.ds(t * 8 * PITCH + first + k, 8, stride=PITCH), :]

            largest = jnp.abs(level(0))
            for k in range(1, OWN_LEVELS):
                largest = jnp.maximum(largest, jnp.abs(level(k)))
            scale = exponent(largest)
            per_unit = CODE * jnp.exp2(-scale)
            blocks += [level(k) * per_unit for k in range(OWN_LEVELS)] + [scale]
        for pair in range(ENDS // 4):
            halves = []
            for i in (2 * pair, 2 * pair + 1):
                a, b = blocks[2 * i], blocks[2 * i + 1]
                halves.append(
                    jnp.where(
                        chunk == 0,
                        pltpu.roll(a, 112, 1),
                        jnp.where(
                            chunk == 1,
                            pltpu.roll(a, 80, 1),
                            jnp.where(chunk == 2, pltpu.roll(b, 48, 1), pltpu.roll(b, 16, 1)),
                        ),
                    )
                )
            ends[n, 16 * pair : 16 * pair + 16, :] = coded(jnp.concatenate(halves, axis=0))
        return carry

    lax.fori_loop(0, BLOCKS, send, 0, unroll=True)
    for n, out in enumerate((out0, out1, out2, out3)):
        out[...] = ends[n]


def turn_kernel(in0, in1, in2, in3, out0, out1, out2, out3, got, sent):
    block = lax.axis_index("depth")
    tile = lax.axis_index("tile")
    for n, ref in enumerate((in0, in1, in2, in3)):
        got[block ^ n] = ref[...]
    sub = index((8, 128), 0)
    chunk = index((8, 128), 1) // 32
    for pair in range(ENDS // 4):
        whole = [
            got[d, 16 * pair : 16 * pair + 16, :].astype(jnp.int32).astype(F32) for d in range(4)
        ]
        halves = {t: [] for t in range(4)}
        for part in range(2):
            m = [x[8 * part : 8 * part + 8] for x in whole]
            lined = {}
            for par in range(2):
                for h in range(2):
                    z = [pltpu.roll(m[d], (32 * (d - 2 * par - h)) % 128, 1) for d in range(4)]
                    lined[par, h] = jnp.where(
                        chunk == 0,
                        z[0],
                        jnp.where(chunk == 1, z[1], jnp.where(chunk == 2, z[2], z[3])),
                    )
            for h in range(2):
                a, b = lined[0, h], lined[1, h]
                halves[2 * h].append(jnp.where(sub < 4, a, pltpu.roll(b, 4, 0)))
                halves[2 * h + 1].append(jnp.where(sub < 4, pltpu.roll(a, 4, 0), b))
        for t in range(4):
            sent[t, 16 * pair : 16 * pair + 16, :] = (
                jnp.concatenate(halves[t], axis=0).astype(jnp.int32).astype(I16)
            )
    for n, out in enumerate((out0, out1, out2, out3)):
        out[...] = sent[(tile + n) % TILES]


def finish_kernel(in0, in1, in2, in3, state, land_sea, depth_index, far, got, out, sent):
    block = lax.axis_index("depth")
    tile = lax.axis_index("tile")
    for n, ref in enumerate((in0, in1, in2, in3)):
        got[(tile + TILES - n) % TILES] = ref[...]
    wet_levels = jnp.where(land_sea[...] == 1, depth_index[...], 0)
    first = block * OWN_LEVELS
    left = index((16, 128), 1) < 64
    windows_of = []
    for q in range(4):
        half, west = divmod(q, 2)
        lanes = slice(128 * q, 128 * q + 128)
        values = []
        for pair in range(ENDS // 4):
            x, y = (wide(got[2 * west + i, 16 * pair : 16 * pair + 16, :]) for i in range(2))
            x = jnp.where(left, turn(x, 2 * half), turn(y, 2 - 2 * half))
            values += [x[0:4], x[4:8], x[8:12], x[12:16]]
        windows_of.append(values)
    copies = [
        pltpu.make_async_copy(out.at[0, t], far.at[0, t], sent.at[t]) for t in range(2)
    ]
    for t in range(2):
        base = t * (OWN_LEVELS + 1)
        for q, values in enumerate(windows_of):
            lanes = slice(128 * q, 128 * q + 128)
            unit = jnp.exp2(values[base + OWN_LEVELS]) * (1.0 / CODE)
            for k in range(OWN_LEVELS):
                wet = wet_levels[:, lanes] > first + k
                out[0, t, k, :, lanes] = jnp.where(
                    wet, values[base + k] * unit - state[0, t, k, :, lanes], 0.0
                )
        copies[t].start()
    for copy in copies:
        copy.wait()


def near(*arrays):
    return [pltpu.with_memory_space_constraint(x, pltpu.VMEM) for x in arrays]


def call(kernel, outs, scratch, *args, reserve=8, place=near):
    return pl.pallas_call(
        kernel,
        out_shape=outs,
        in_specs=[VMEM] * len(args),
        out_specs=jax.tree.map(lambda _: VMEM, outs),
        scratch_shapes=scratch,
        compiler_params=pltpu.CompilerParams(vmem_limit_bytes=reserve << 20),
    )(*place(*args))


def across_depth(messages):
    return [messages[0]] + [
        lax.ppermute(messages[n], "depth", [(i, i ^ n) for i in range(BLOCKS)])
        for n in range(1, BLOCKS)
    ]


def across_tiles(messages):
    return [messages[0]] + [
        lax.ppermute(messages[n], "tile", [(i, (i + n) % TILES) for i in range(TILES)])
        for n in range(1, TILES)
    ]


def window_shards(initial_states, velocity, growth, land_sea, depth_index, column_ops):
    message = pltpu.VMEM((4 * ENDS, 128), I16)
    slots = pltpu.VMEM((4, 4 * ENDS, 128), I16)
    cells = pltpu.VMEM((2 * 8 * PITCH, 128), F32)
    both = pltpu.VMEM((BOTH, 128), I16)
    sent = pltpu.VMEM((TILES, BOTH, 128), I16)
    across, *here = call(
        pack_kernel,
        [pltpu.VMEM((2 * MAIN + FIELDS, 128), I16)] + [both] * TILES,
        [pltpu.VMEM((MAIN, 512), F32), sent],
        initial_states,
        velocity,
        growth,
        land_sea,
        depth_index,
        reserve=60,
        place=lambda *args: args,
    )
    across = lax.ppermute(across, "depth", [(i, i ^ CORES) for i in range(BLOCKS)])
    loaded = []
    for messages in (here, call(relay_kernel, [both] * TILES, [sent], across)):
        tiles = across_tiles(messages)
        others = call(core_kernel, pltpu.VMEM((TILES * PIECE, 128), I16), [], *tiles)
        others = lax.ppermute(others, "depth", [(i, i ^ 1) for i in range(BLOCKS)])
        loaded.append((*tiles, others))
    pieces = pltpu.VMEM((TILES * CORES, PIECE, 128), I16)
    flow = pltpu.VMEM((2 * 8 * HALF, 128), F32)
    coef = pltpu.VMEM((HALF // 8, 8, 9, 8, 128), F32)
    near_levels = call(
        own_kernel,
        [flow, coef, pltpu.VMEM((2, 8, 128), F32), pltpu.VMEM((2, PITCH, PITCH), jnp.bfloat16)],
        [pieces, flow],
        *loaded[0],
        column_ops,
    )
    out = call(
        steps_kernel,
        [message] * 4,
        [pieces, cells, cells, cells, flow, coef, pltpu.VMEM((PITCH, 128), F32), slots],
        *loaded[1],
        *near_levels,
        reserve=16,
    )
    turned = call(turn_kernel, [message] * 4, [slots] * 2, *across_depth(out))
    segs = lax.axis_size("seg")
    last = [
        lax.ppermute(
            turned[n],
            ("seg", "tile"),
            [
                (s * TILES + t, ((s + 1) % segs) * TILES + (t + n) % TILES)
                for s in range(segs)
                for t in range(TILES)
            ],
        )
        for n in range(4)
    ]
    arguments = near(*last, initial_states, land_sea, depth_index)
    return pl.pallas_call(
        finish_kernel,
        out_shape=jax.ShapeDtypeStruct(initial_states.shape, F32),
        in_specs=[VMEM] * len(arguments),
        out_specs=pl.BlockSpec(memory_space=pl.ANY),
        scratch_shapes=[
            slots,
            pltpu.VMEM(initial_states.shape, F32),
            pltpu.SemaphoreType.DMA((2,)),
        ],
        compiler_params=pltpu.CompilerParams(vmem_limit_bytes=8 << 20),
    )(*arguments)


def shards(initial_states, velocity, growth, land_sea, depth_index, column_ops):
    fits = (
        lax.axis_size("tile") == TILES
        and lax.axis_size("depth") == BLOCKS
        and initial_states.shape == (1, 2, OWN_LEVELS, 4, TILES * BLOCKS * OWN)
    )
    plan = window_shards if fits else stepwise_shards
    return plan(initial_states, velocity, growth, land_sea, depth_index, column_ops)


def solution(mesh):
    return jax.shard_map(
        shards,
        mesh=mesh,
        in_specs=(
            P("seg", None, "depth", "tile", None),
            P("seg", None, "depth", "tile", None),
            P("seg", "tile", None),
            P("tile", None),
            P("tile", None),
            P(),
        ),
        out_specs=P("seg", None, "depth", "tile", None),
        check_vma=False,
    )
```
